256 devices in a mesh: alpha: 8 (over x, z_lo), beta: 32 (over y, z_hi, core).
Axes of the slice: x: 4, y: 4, z: 8 (z_hi: 4, z_lo: 2; z = z_hi * 2 + z_lo), core: 2. Of those that a mesh axis runs over, the one named last changes fastest.
Arguments:
- coef: bfloat16 [8192, 4096], P('alpha', 'beta'), may hold values from -6 to 6
- beta_ops: bfloat16 [4096, 512], P('beta'), may hold values from -0.25 to 0.25
- beta_cols: int32 [32, 4], P('beta'), may hold values from 0 to 31, as said below
- alpha_ops: bfloat16 [8192, 4096], P('alpha'), may hold values from -0.09375 to 0.09375
- alpha_cols: int32 [8, 4], P('alpha'), may hold values from 0 to 7, as said below
- pair_alpha: bfloat16 [8192, 576], P('alpha'), may hold values from -12 to 12
- pair_beta: bfloat16 [4096, 576], P('beta'), may hold values from -0.09375 to 0.09375
- pair_coupling: bfloat16 [576, 576], replicated, may hold values from -0.25 to 0.25
- denominators: float32 [8192, 4096], P('alpha', 'beta'), may hold values from 0.5 to 4
Outputs:
- sigma_scaled: float32 [8192, 4096], P('alpha', 'beta')
The draws below stay inside these ranges and needn't reach their ends.
Inputs may be any that keep to these rules, and one draw needn't show every extreme that they name: `beta_cols`: the 4 entries of row j are different and each lies within two blocks of j, counted around the beta blocks cyclically. `alpha_cols`: each entry of row i is i or one of its two neighbours, counted around the alpha blocks cyclically; entries may repeat.
All inputs are finite; a program needn't handle non-finite values.
Results may differ from the reference program's by a relative error of at most 0.013.
Values may be sent and summed in bfloat16 or wider, within the bound.
No kernel may reach another device: no remote copies, remote signals or barrier semaphores. Data moves between devices by JAX's collectives and lax.ppermute only.
A program may use at most 128 MiB of HBM per device.

```python
import math
import jax
import jax.numpy as jnp
from jax import lax

RA = 1024
RB = 128
KB = 4
KA = 4
P_SIZE = 576
NA = 8192
NB = 4096
N_ALPHA = 8
N_BETA = 32


def draw_beta_cols(key, part):
    keys = jax.random.split(jax.random.fold_in(key, 11), N_BETA)
    offsets = jax.vmap(lambda single: jax.random.permutation(single, 5)[:KB])(keys) - 2
    rows = jnp.arange(N_BETA, dtype=jnp.int32)[:, None]
    return ((rows + offsets + N_BETA) % N_BETA).astype(jnp.int32)


def draw_alpha_cols(key, part):
    base = jax.random.fold_in(key, 23)
    free_offsets = jax.random.randint(jax.random.fold_in(base, 1), (N_ALPHA, KA - 2), -1, 2)
    fixed_offsets = jnp.broadcast_to(jnp.array([-1, 1], dtype=jnp.int32)[None, :], (N_ALPHA, 2))
    offsets = jnp.concatenate([fixed_offsets, free_offsets.astype(jnp.int32)], axis=1)
    keys = jax.random.split(jax.random.fold_in(base, 2), N_ALPHA)
    orders = jax.vmap(lambda single: jax.random.permutation(single, KA))(keys)
    offsets = jnp.take_along_axis(offsets, orders.astype(jnp.int32), axis=1)
    rows = jnp.arange(N_ALPHA, dtype=jnp.int32)[:, None]
    return ((rows + offsets + N_ALPHA) % N_ALPHA).astype(jnp.int32)


def block_scale(stream_key, extent, shards, least, top_value):
    loudness, own = 1.0, jax.random.fold_in(stream_key, 6)
    for position, shards_of in shards:
        steps = jnp.exp(jax.random.uniform(jax.random.fold_in(own, position), (shards_of,), jnp.float32, least / len(shards), top_value / len(shards)))
        loudness = loudness * jnp.repeat(steps, extent[position] // shards_of).reshape([-1 if axis == position else 1 for axis in range(len(extent))])
    return loudness


def scatter_about(stream_key, dims, width, limit, shards=(), kind=jnp.bfloat16):
    values = jax.random.normal(stream_key, dims, jnp.float32) * width
    if len(shards) > 0:
        values = block_scale(stream_key, dims, shards, -0.22, 0.18) * values
    return jnp.clip(values, min=-limit, max=limit).astype(kind)


def setup_inputs(seed: int = 0) -> dict:
    key_list = jax.random.split(jax.random.key(seed), 10)
    coef = scatter_about(key_list[0], (NA, NB), 1.0, 6.0, ((0, 8), (1, 32)))
    beta_ops = scatter_about(key_list[1], (NB, KB * RB), (KB * RB) ** -0.5, 0.25, ((0, 32),))
    beta_cols = draw_beta_cols(jax.random.fold_in(key_list[9], 71), 0)
    alpha_ops = scatter_about(key_list[3], (NA, KA * RA), (KA * RA) ** -0.5, 0.09375, ((0, 8),))
    alpha_cols = draw_alpha_cols(jax.random.fold_in(key_list[9], 71), 0)
    pair_alpha = scatter_about(key_list[5], (NA, P_SIZE), 2.0, 12.0, ((0, 8),))
    pair_beta = scatter_about(key_list[6], (NB, P_SIZE), NB ** -0.5, 0.09375, ((0, 32),))
    pair_coupling = scatter_about(key_list[7], (P_SIZE, P_SIZE), P_SIZE ** -0.5, 0.25)
    denominators = jnp.clip(jnp.exp(math.log(4.0) - 2.0794415 * jax.random.uniform(key_list[8], (NA, NB), jnp.float32) ** block_scale(key_list[8], (NA, NB), ((0, 8), (1, 32)), -0.2, 0.2)), 0.5, 4.0)
    return {"coef": coef, "beta_ops": beta_ops, "beta_cols": beta_cols, "alpha_ops": alpha_ops, "alpha_cols": alpha_cols, "pair_alpha": pair_alpha, "pair_beta": pair_beta, "pair_coupling": pair_coupling, "denominators": denominators}


def reference(coef, beta_ops, beta_cols, alpha_ops, alpha_cols, pair_alpha, pair_beta, pair_coupling, denominators):
    def beta_block(index):
        blocks = lax.dynamic_slice_in_dim(beta_ops, index * RB, RB, 0)
        total = jnp.zeros((coef.shape[0], RB), jnp.float32)
        for listed in range(KB):
            source = lax.dynamic_slice_in_dim(coef, (beta_cols[index, listed] * RB).astype(jnp.int32), RB, 1)
            tile_part = blocks[:, listed * RB:(listed + 1) * RB]
            total = total + lax.dot_general(source, tile_part, (((1,), (1,)), ((), ())), preferred_element_type=jnp.float32)
        return total

    same_beta = lax.map(beta_block, jnp.arange(N_BETA, dtype=jnp.int32))
    same_beta = jnp.transpose(same_beta, (1, 0, 2)).reshape(coef.shape[0], coef.shape[1])

    def alpha_block(index):
        blocks = lax.dynamic_slice_in_dim(alpha_ops, index * RA, RA, 0)
        total = jnp.zeros((RA, coef.shape[1]), jnp.float32)
        for listed in range(KA):
            source = lax.dynamic_slice_in_dim(coef, (alpha_cols[index, listed] * RA).astype(jnp.int32), RA, 0)
            tile_part = blocks[:, listed * RA:(listed + 1) * RA]
            total = total + jnp.dot(tile_part, source, preferred_element_type=jnp.float32)
        return total

    same_alpha = lax.map(alpha_block, jnp.arange(N_ALPHA, dtype=jnp.int32))
    same_alpha = same_alpha.reshape(coef.shape[0], coef.shape[1])

    density = jnp.dot(coef, pair_beta, preferred_element_type=jnp.float32).astype(jnp.bfloat16)
    excited = (jnp.dot(density, pair_coupling, preferred_element_type=jnp.float32) * pair_alpha.astype(jnp.float32)).astype(jnp.bfloat16)
    mixed = lax.dot_general(excited, pair_beta, (((1,), (1,)), ((), ())), preferred_element_type=jnp.float32)
    return (same_beta + same_alpha + mixed) / denominators
```

```python
import jax
import jax.numpy as jnp
from jax import lax
from jax.experimental import pallas as pl
from jax.experimental.pallas import tpu as pltpu
from jax.sharding import Mesh
from jax.sharding import PartitionSpec as P

ALPHA = ("x", "zl")
BETA = ("y", "zh", "c")
F32 = jnp.float32
BF16 = jnp.bfloat16
SMEM = pl.BlockSpec(memory_space=pltpu.SMEM)
VMEM = pl.BlockSpec(memory_space=pltpu.VMEM)
MIB = 1 << 20


def dot(a, b, dims=((1,), (0,))):
    return lax.dot_general(a, b, (dims, ((), ())), preferred_element_type=F32)


def estimate(flops, moved):
    return pl.CostEstimate(flops=flops, bytes_accessed=moved, transcendentals=0)


def swapped(block, axis, mask):
    count = lax.axis_size(axis)
    return lax.ppermute(block, axis, [(i, i ^ mask) for i in range(count)])


def rotated(block, axis, distance):
    count = lax.axis_size(axis)
    return lax.ppermute(block, axis, [(i, (i + distance) % count) for i in range(count)])


def density_parts(where, own, mate, pair_own, pair_mate):
    pairs = pair_own.shape[0]
    width = own.shape[1]

    def kernel(where_ref, own_ref, mate_ref, po_ref, pm_ref, *outs):
        left = jnp.concatenate([po_ref[...], pm_ref[...]], axis=1)
        for k, out in enumerate(outs):
            rows = pl.ds(pl.multiple_of(where_ref[k] * width, width), width)
            right = jnp.concatenate([own_ref[rows, :], mate_ref[rows, :]], axis=1)
            out[...] = dot(left, right, ((1,), (1,))).astype(BF16)

    return pl.pallas_call(
        kernel,
        out_shape=[jax.ShapeDtypeStruct((pairs, width), BF16)] * 4,
        in_specs=[SMEM] + [VMEM] * 4,
        out_specs=[VMEM] * 4,
        compiler_params=pltpu.CompilerParams(vmem_limit_bytes=16 * MIB),
        cost_estimate=estimate(8 * pairs * width * width * 2, 1 * MIB),
        name="density_parts",
    )(where, own, mate, pair_own, pair_mate)


def excited_block(where, near, far, coupling, pair_alpha):
    pairs, width = near.shape

    def kernel(where_ref, near_ref, far_ref, coupling_ref, pa_ref, out_ref):
        total = near_ref[...].astype(F32) + far_ref[...].astype(F32)
        density = total.T.astype(BF16)
        rows = pl.ds(pl.multiple_of(where_ref[0] * width, width), width)
        scale = pa_ref[:, rows].astype(F32).T
        out_ref[...] = (dot(density, coupling_ref[...]) * scale).astype(BF16)

    return pl.pallas_call(
        kernel,
        out_shape=jax.ShapeDtypeStruct((width, pairs), BF16),
        in_specs=[SMEM] + [VMEM] * 4,
        out_specs=VMEM,
        compiler_params=pltpu.CompilerParams(vmem_limit_bytes=16 * MIB),
        cost_estimate=estimate(2 * pairs * pairs * width, 2 * MIB),
        name="excited_block",
    )(where, near, far, coupling, pair_alpha)


def mixed_parts(blocks, pair_own, pair_mate):
    width, pairs = blocks[0].shape

    def kernel(*refs):
        ins, (po_ref, pm_ref, mine, theirs) = refs[:4], refs[4:]
        right = jnp.concatenate([po_ref[...], pm_ref[...]], axis=1)
        for k, block in enumerate(ins):
            both = dot(block[...], right)
            mine[k] = both[:, :width]
            theirs[k] = both[:, width:].astype(BF16)

    return pl.pallas_call(
        kernel,
        out_shape=[
            jax.ShapeDtypeStruct((4, width, width), F32),
            jax.ShapeDtypeStruct((4, width, width), BF16),
        ],
        in_specs=[VMEM] * 6,
        out_specs=[VMEM] * 2,
        compiler_params=pltpu.CompilerParams(vmem_limit_bytes=16 * MIB),
        cost_estimate=estimate(16 * pairs * width * width, 1 * MIB),
        name="mixed_parts",
    )(*blocks, pair_own, pair_mate)


def finished(where, same, mine, theirs, denominators):
    rows, width = same.shape

    def kernel(where_ref, same_ref, mine_ref, theirs_ref, den_ref, out_ref):
        for k in range(4):
            at = pl.ds(pl.multiple_of(where_ref[k] * width, width), width)
            out_ref[at, :] = (same_ref[at, :] + mine_ref[k]) / den_ref[at, :]
            at = pl.ds(pl.multiple_of(where_ref[4 + k] * width, width), width)
            out_ref[at, :] = (same_ref[at, :] + theirs_ref[k].astype(F32)) / den_ref[at, :]

    return pl.pallas_call(
        kernel,
        out_shape=jax.ShapeDtypeStruct((rows, width), F32),
        in_specs=[SMEM] + [VMEM] * 4,
        out_specs=VMEM,
        compiler_params=pltpu.CompilerParams(vmem_limit_bytes=16 * MIB),
        cost_estimate=estimate(rows * width * 2, 2 * MIB),
        name="finished",
    )(where, same, mine, theirs, denominators)


def same_spin_beta(codes, blocks, beta_ops):
    rows, width = blocks[0].shape
    listed = beta_ops.shape[1] // width

    def kernel(codes_ref, *refs):
        ins, (ops_ref, out_ref) = refs[:5], refs[5:]
        placed = []
        for n in range(5):
            tile = jnp.zeros((width, width), F32)
            for k in range(listed):
                part = ops_ref[:, k * width : (k + 1) * width].astype(F32)
                tile = jnp.where(codes_ref[k] == n, part, tile)
            placed.append(tile.astype(BF16))
        left = jnp.concatenate([block[...] for block in ins], axis=1)
        right = jnp.concatenate(placed, axis=1)
        out_ref[...] = dot(left, right, ((1,), (1,)))

    return pl.pallas_call(
        kernel,
        out_shape=jax.ShapeDtypeStruct((rows, width), F32),
        in_specs=[SMEM] + [VMEM] * 6,
        out_specs=VMEM,
        compiler_params=pltpu.CompilerParams(vmem_limit_bytes=24 * MIB),
        cost_estimate=estimate(2 * rows * width * width * 5, 2 * MIB),
        name="same_spin_beta",
    )(codes, *blocks, beta_ops)


def same_spin_alpha(codes, blocks, alpha_ops, start):
    rows, width = start.shape
    depth = blocks[0].shape[0]
    listed = alpha_ops.shape[1] // depth
    half = depth // 2

    def kernel(codes_ref, own_ref, near_ref, far_ref, ops_ref, start_ref, out_ref):
        step = pl.program_id(0)
        code = codes_ref[step // 2]
        at = pl.ds(pl.multiple_of((step % 2) * half, half), half)
        picked = jnp.where(
            code == 0, own_ref[at, :], jnp.where(code == 1, near_ref[at, :], far_ref[at, :])
        )
        term = dot(ops_ref[...], picked)

        @pl.when(step == 0)
        def _():
            out_ref[...] = start_ref[...] + term

        @pl.when(step > 0)
        def _():
            out_ref[...] += term

    whole = lambda shape: pl.BlockSpec(shape, lambda s: (0, 0))
    return pl.pallas_call(
        kernel,
        out_shape=jax.ShapeDtypeStruct((rows, width), F32),
        grid=(listed * 2,),
        in_specs=[
            SMEM,
            whole((depth, width)),
            whole((depth, width)),
            whole((depth, width)),
            pl.BlockSpec((rows, half), lambda s: (0, s)),
            whole((rows, width)),
        ],
        out_specs=whole((rows, width)),
        compiler_params=pltpu.CompilerParams(vmem_limit_bytes=24 * MIB),
        cost_estimate=estimate(2 * rows * width * depth * listed, 10 * MIB),
        name="same_spin_alpha",
    )(codes, *blocks, alpha_ops, start)


def local(
    coef,
    beta_ops,
    beta_cols,
    alpha_ops,
    alpha_cols,
    pair_alpha,
    pair_beta,
    pair_coupling,
    denominators,
):
    beta_count = lax.axis_size(BETA)
    alpha_count = lax.axis_size(ALPHA)
    y, core = lax.axis_index("y"), lax.axis_index("c")
    row_blocks = [(y ^ k) * 2 for k in range(4)]
    where = jnp.stack([r + core for r in row_blocks] + [r + 1 - core for r in row_blocks])
    where = where.astype(jnp.int32)

    pair_t = pair_beta.T
    mate = swapped(coef, "c", 1)
    pair_mate = swapped(pair_t, "c", 1)

    below = rotated(coef, BETA, 2)
    above = rotated(coef, BETA, -2)
    near = swapped(coef, "zl", 1)
    xs, route = lax.axis_size("x"), []
    for i in range(xs):
        route += [(2 * i, 2 * ((i + 1) % xs)), (2 * i + 1, 2 * ((i - 1) % xs) + 1)]
    far = lax.ppermute(near, ALPHA, route)
    crossed = swapped(jnp.where(core == 0, above, below), "c", 1)

    parts = density_parts(where, coef, mate, pair_t, pair_mate)
    got = [swapped(parts[k], "y", k) for k in (1, 3, 2)]
    total = parts[0].astype(F32)
    for part in got:
        total = total + part.astype(F32)
    total = total.astype(BF16)
    total = (total.astype(F32) + swapped(total, "zh", 1).astype(F32)).astype(BF16)
    excited = excited_block(where, total, swapped(total, "zh", 3), pair_coupling, pair_alpha.T)
    blocks = [excited] + [swapped(excited, "y", k) for k in (1, 2, 3)]

    offset = (beta_cols[0] - lax.axis_index(BETA) + 2 + beta_count) % beta_count
    left = jnp.where(core == 0, 1, 3)
    beta_codes = jnp.where(offset == left, 1, jnp.where(offset == 4 - left, 3, offset))
    beta_codes = beta_codes.astype(jnp.int32)
    same = same_spin_beta(beta_codes, [below, crossed, coef, mate, above], beta_ops)

    offset = (alpha_cols[0] - lax.axis_index(ALPHA) + 1 + alpha_count) % alpha_count
    partner = jnp.where(lax.axis_index("zl") == 0, 2, 0)
    alpha_codes = jnp.where(offset == 1, 0, jnp.where(offset == partner, 1, 2)).astype(jnp.int32)
    same = same_spin_alpha(alpha_codes, [coef, near, far], alpha_ops, same)

    mine, theirs = mixed_parts(blocks, pair_t, pair_mate)
    return finished(where, same, mine, swapped(theirs, "c", 1), denominators)


def solution(mesh):
    finer = Mesh(mesh.devices.reshape(4, 2, 4, 4, 2), (*ALPHA, *BETA))
    placed = (
        P(ALPHA, BETA),
        P(BETA, None),
        P(BETA, None),
        P(ALPHA, None),
        P(ALPHA, None),
        P(ALPHA, None),
        P(BETA, None),
        P(),
        P(ALPHA, BETA),
    )
    return jax.shard_map(
        local, mesh=finer, in_specs=placed, out_specs=P(ALPHA, BETA), check_vma=False
    )
```

```python
import jax
import jax.numpy as jnp
from jax import lax
from jax.experimental import pallas as pl
from jax.experimental.pallas import tpu as pltpu
from jax.sharding import Mesh
from jax.sharding import PartitionSpec as P

ALPHA = ("x", "zl")
BETA = ("y", "zh", "c")
F32 = jnp.float32
BF16 = jnp.bfloat16
SMEM = pl.BlockSpec(memory_space=pltpu.SMEM)
VMEM = pl.BlockSpec(memory_space=pltpu.VMEM)
HBM = pl.BlockSpec(memory_space=pltpu.HBM)
ANY = pl.BlockSpec(memory_space=pl.ANY)
MIB = 1 << 20


def dot(a, b, dims=((1,), (0,))):
    return lax.dot_general(a, b, (dims, ((), ())), preferred_element_type=F32)


def swapped(block, axis, mask):
    count = lax.axis_size(axis)
    return lax.ppermute(block, axis, [(i, i ^ mask) for i in range(count)])


def rotated(block, axis, distance):
    count = lax.axis_size(axis)
    return lax.ppermute(block, axis, [(i, (i + distance) % count) for i in range(count)])


def call(kernel, outs, args, specs, cost, scratch=(), aliases=None, out_specs=None, limit=16):
    return pl.pallas_call(
        kernel,
        out_shape=outs,
        in_specs=specs,
        out_specs=out_specs or [VMEM] * len(outs),
        scratch_shapes=list(scratch),
        input_output_aliases=aliases or {},
        compiler_params=pltpu.CompilerParams(vmem_limit_bytes=limit * MIB),
        cost_estimate=pl.CostEstimate(flops=cost[0], bytes_accessed=cost[1], transcendentals=0),
        name=kernel.__name__,
    )(*args)


def shape(dims, kind=BF16):
    return jax.ShapeDtypeStruct(dims, kind)


def block_rows(where_ref, k, width):
    return pl.ds(pl.multiple_of(where_ref[k] * width, width), width)


def own_density(where, coef, pair_t):
    pairs, width = pair_t.shape

    def own_density_kernel(where_ref, coef_ref, pair_ref, coef_out, pair_out, acc_out, sems):
        copies = [
            pltpu.make_async_copy(coef_ref, coef_out, sems.at[0]),
            pltpu.make_async_copy(pair_ref, pair_out, sems.at[1]),
        ]
        for copy in copies:
            copy.start()
        for copy in copies:
            copy.wait()
        left = pair_out[...]
        for k in range(4):
            right = coef_out[block_rows(where_ref, k, width), :]
            acc_out[k] = dot(left, right, ((1,), (1,)))

    return call(
        own_density_kernel,
        [shape(coef.shape), shape(pair_t.shape), shape((4, pairs, width), F32)],
        (where, coef, pair_t),
        [SMEM, HBM, HBM],
        (8 * pairs * width * width, 1 * MIB),
        [pltpu.SemaphoreType.DMA((2,))],
        limit=16,
    )


def density_parts(where, acc, mate, pair_mate):
    pairs, width = pair_mate.shape

    def density_parts_kernel(where_ref, acc_ref, mate_ref, pair_ref, *outs):
        left = pair_ref[...]
        for k, out in enumerate(outs):
            right = mate_ref[block_rows(where_ref, k, width), :]
            out[...] = (acc_ref[k] + dot(left, right, ((1,), (1,)))).astype(BF16)

    return call(
        density_parts_kernel,
        [shape((pairs, width))] * 4,
        (where, acc, mate, pair_mate),
        [SMEM] + [VMEM] * 3,
        (8 * pairs * width * width, 1 * MIB),
    )


def staged(where, cols, coupling, pair_alpha_t, beta_ops, tie):
    pairs, width = coupling.shape[0], beta_ops.shape[0]
    listed = beta_ops.shape[1] // width
    count = lax.axis_size(BETA)

    def staged_kernel(
        where_ref, cols_ref, c_ref, pa_ref, ops_ref, tie_ref, c_out, pa_out, w_out, pa_v, ops_v, sems
    ):
        rows = block_rows(where_ref, 0, width)
        copies = [
            pltpu.make_async_copy(ops_ref, ops_v, sems.at[0]),
            pltpu.make_async_copy(pa_ref.at[:, rows], pa_v, sems.at[1]),
            pltpu.make_async_copy(c_ref, c_out, sems.at[2]),
        ]
        for copy in copies:
            copy.start()
        copies[0].wait()
        core = where_ref[8]
        for n in range(5):
            offset = n if n in (0, 2, 4) else jnp.where(core == 0, n, 4 - n)
            tile = jnp.zeros((width, width), F32)
            for k in range(listed):
                here = lax.rem(cols_ref[0, k] - where_ref[9] + 2 + count, count)
                part = ops_v[:, k * width : (k + 1) * width].astype(F32)
                tile = jnp.where(here == offset, part, tile)
            w_out[:, n * width : (n + 1) * width] = tile.astype(BF16)
        copies[1].wait()
        pa_out[...] = pa_v[...].astype(F32).T
        copies[2].wait()

    return call(
        staged_kernel,
        [shape(coupling.shape), shape((width, pairs), F32), shape((width, 5 * width))],
        (where, cols, coupling, pair_alpha_t, beta_ops, tie),
        [SMEM, SMEM, HBM, HBM, HBM, ANY],
        (pairs * pairs, 2 * MIB),
        [
            pltpu.VMEM((pairs, width), BF16),
            pltpu.VMEM(beta_ops.shape, BF16),
            pltpu.SemaphoreType.DMA((3,)),
        ],
    )


def excited_block(near, far, coupling, scale):
    pairs, width = near.shape

    def excited_block_kernel(near_ref, far_ref, coupling_ref, scale_ref, out_ref):
        total = near_ref[...].astype(F32) + far_ref[...].astype(F32)
        density = total.T.astype(BF16)
        out_ref[...] = (dot(density, coupling_ref[...]) * scale_ref[...]).astype(BF16)

    return call(
        excited_block_kernel,
        [shape((width, pairs))],
        (near, far, coupling, scale),
        [VMEM] * 4,
        (2 * pairs * pairs * width, 2 * MIB),
    )[0]


def mixed_mate(blocks, pair_mate):
    width = blocks[0].shape[0]
    pairs = blocks[0].shape[1]

    def mixed_mate_kernel(*refs):
        right = refs[4][...]
        for k in range(4):
            refs[5][k] = dot(refs[k][...], right).astype(BF16)

    return call(
        mixed_mate_kernel,
        [shape((4, width, width))],
        (*blocks, pair_mate),
        [VMEM] * 5,
        (8 * pairs * width * width, 1 * MIB),
    )[0]


def finished_own(where, same, blocks, pair_own, denominators):
    rows, width = same.shape

    def finished_own_kernel(where_ref, same_ref, e0, e1, e2, e3, pair_ref, den_ref, out, part, sems):
        right = pair_ref[...]
        copies = []
        for k, block in enumerate((e0, e1, e2, e3)):
            at = block_rows(where_ref, k, width)
            part[k] = (same_ref[at, :] + dot(block[...], right)) / den_ref[at, :]
            copies.append(pltpu.make_async_copy(part.at[k], out.at[at, :], sems.at[k]))
            copies[-1].start()
        for copy in copies:
            copy.wait()

    return call(
        finished_own_kernel,
        [shape((rows, width), F32)],
        (where, same, *blocks, pair_own, denominators),
        [SMEM] + [VMEM] * 7,
        (rows * width * 600, 2 * MIB),
        [pltpu.VMEM((4, width, width), F32), pltpu.SemaphoreType.DMA((4,))],
        out_specs=[HBM],
    )[0]


def finished_mate(where, same, theirs, denominators, begun):
    rows, width = same.shape

    def finished_mate_kernel(where_ref, same_ref, theirs_ref, den_ref, begun_ref, out, part, sems):
        copies = []
        for k in range(4):
            at = block_rows(where_ref, 4 + k, width)
            part[k] = (same_ref[at, :] + theirs_ref[k].astype(F32)) / den_ref[at, :]
            copies.append(pltpu.make_async_copy(part.at[k], out.at[at, :], sems.at[k]))
            copies[-1].start()
        for copy in copies:
            copy.wait()

    return call(
        finished_mate_kernel,
        [shape((rows, width), F32)],
        (where, same, theirs, denominators, begun),
        [SMEM] + [VMEM] * 3 + [HBM],
        (rows * width * 2, 2 * MIB),
        [pltpu.VMEM((4, width, width), F32), pltpu.SemaphoreType.DMA((4,))],
        aliases={4: 0},
        out_specs=[HBM],
    )[0]


def same_spin_beta(blocks, placed):
    rows, width = blocks[0].shape

    def same_spin_beta_kernel(b0, b1, b2, b3, b4, w_ref, out_ref):
        left = jnp.concatenate([b[...] for b in (b0, b1, b2, b3, b4)], axis=1)
        out_ref[...] = dot(left, w_ref[...], ((1,), (1,)))

    return call(
        same_spin_beta_kernel,
        [shape((rows, width), F32)],
        (*blocks, placed),
        [VMEM] * 6,
        (2 * rows * width * width * 5, 2 * MIB),
        limit=24,
    )[0]


def same_spin_alpha(where, cols, blocks, alpha_ops, start):
    rows, width = start.shape
    depth = blocks[0].shape[0]
    step = depth // 2
    steps = alpha_ops.shape[1] // step
    count = lax.axis_size(ALPHA)

    def same_spin_alpha_kernel(
        where_ref, cols_ref, own_ref, near_ref, far_ref, ops_ref, start_ref, out_ref, ops_v, sems
    ):
        copies = [
            pltpu.make_async_copy(ops_ref.at[:, s * step : (s + 1) * step], ops_v.at[s], sems.at[s])
            for s in range(steps)
        ]
        for copy in copies:
            copy.start()
        for s, copy in enumerate(copies):
            offset = lax.rem(cols_ref[0, s // 2] - where_ref[10] + 1 + count, count)
            at = slice((s % 2) * step, (s % 2 + 1) * step)
            picked = jnp.where(
                offset == 1,
                own_ref[at, :],
                jnp.where(offset == where_ref[11], near_ref[at, :], far_ref[at, :]),
            )
            copy.wait()
            before = start_ref[...] if s == 0 else out_ref[...]
            out_ref[...] = before + dot(ops_v[s], picked)

    return call(
        same_spin_alpha_kernel,
        [shape((rows, width), F32)],
        (where, cols, *blocks, alpha_ops, start),
        [SMEM, SMEM] + [VMEM] * 3 + [HBM, VMEM],
        (2 * rows * width * depth * 4, 10 * MIB),
        [pltpu.VMEM((steps, rows, step), BF16), pltpu.SemaphoreType.DMA((steps,))],
        limit=48,
    )[0]


def local(
    coef,
    beta_ops,
    beta_cols,
    alpha_ops,
    alpha_cols,
    pair_alpha,
    pair_beta,
    pair_coupling,
    denominators,
):
    y, core = lax.axis_index("y"), lax.axis_index("c")
    low = lax.axis_index("zl")
    row_blocks = [(y ^ k) * 2 for k in range(4)]
    where = [r + core for r in row_blocks] + [r + 1 - core for r in row_blocks]
    where += [core, lax.axis_index(BETA), lax.axis_index(ALPHA), 2 - 2 * low]
    where = jnp.stack(where).astype(jnp.int32)

    pair_t = pair_beta.T
    mate = swapped(coef, "c", 1)
    pair_mate = swapped(pair_t, "c", 1)
    coef_v, pair_v, acc = own_density(where, coef, pair_t)

    below = rotated(coef, BETA, 2)
    above = rotated(coef, BETA, -2)
    near = swapped(coef, "zl", 1)
    xs, route = lax.axis_size("x"), []
    for i in range(xs):
        route += [(2 * i, 2 * ((i + 1) % xs)), (2 * i + 1, 2 * ((i - 1) % xs) + 1)]
    far = lax.ppermute(near, ALPHA, route)

    parts = density_parts(where, acc, mate, pair_mate)
    coupling, scale, placed = staged(
        where, beta_cols, pair_coupling, pair_alpha.T, beta_ops, parts[0]
    )
    got = [swapped(parts[k], "y", k) for k in (1, 3, 2)]
    total = parts[0].astype(F32)
    for part in got:
        total = total + part.astype(F32)
    total = total.astype(BF16)
    total, coupling, scale, placed = lax.optimization_barrier((total, coupling, scale, placed))

    zs = lax.axis_size("zh")
    steps = [[(2 * i + h, 2 * (i ^ m[h]) + h) for i in range(zs) for h in (0, 1)] for m in ((1, 3), (3, 1))]
    first = lax.ppermute(total, ("zh", "c"), steps[0])
    total = (total.astype(F32) + first.astype(F32)).astype(BF16)
    passed = jnp.where(core == 0, above, below)
    total, passed = lax.optimization_barrier((total, passed))
    crossed = swapped(passed, "c", 1)
    second = lax.ppermute(total, ("zh", "c"), steps[1])
    same = same_spin_beta([below, crossed, coef_v, mate, above], placed)
    second, same = lax.optimization_barrier((second, same))

    excited = excited_block(total, second, coupling, scale)
    blocks = [excited] + [swapped(excited, "y", k) for k in (1, 2, 3)]
    same = same_spin_alpha(where, alpha_cols, [coef_v, near, far], alpha_ops, same)
    *blocks, same = lax.optimization_barrier((*blocks, same))

    theirs = mixed_mate(blocks, pair_mate)
    begun = finished_own(where, same, blocks, pair_v, denominators)
    return finished_mate(where, same, swapped(theirs, "c", 1), denominators, begun)


def solution(mesh):
    finer = Mesh(mesh.devices.reshape(4, 2, 4, 4, 2), (*ALPHA, *BETA))
    placed = (
        P(ALPHA, BETA),
        P(BETA, None),
        P(BETA, None),
        P(ALPHA, None),
        P(ALPHA, None),
        P(ALPHA, None),
        P(BETA, None),
        P(),
        P(ALPHA, BETA),
    )
    return jax.shard_map(
        local, mesh=finer, in_specs=placed, out_specs=P(ALPHA, BETA), check_vma=False
    )
```

```python
import jax
import jax.numpy as jnp
from jax import lax
from jax.experimental import pallas as pl
from jax.experimental.pallas import tpu as pltpu
from jax.sharding import Mesh
from jax.sharding import PartitionSpec as P

ALPHA = ("x", "zl")
BETA = ("y", "zh", "c")
F32 = jnp.float32
BF16 = jnp.bfloat16
SMEM = pl.BlockSpec(memory_space=pltpu.SMEM)
VMEM = pl.BlockSpec(memory_space=pltpu.VMEM)
HBM = pl.BlockSpec(memory_space=pltpu.HBM)
ANY = pl.BlockSpec(memory_space=pl.ANY)
MIB = 1 << 20


def dot(a, b, dims=((1,), (0,))):
    return lax.dot_general(a, b, (dims, ((), ())), preferred_element_type=F32)


def swapped(block, axis, mask):
    count = lax.axis_size(axis)
    return lax.ppermute(block, axis, [(i, i ^ mask) for i in range(count)])


def rotated(block, axis, distance):
    count = lax.axis_size(axis)
    return lax.ppermute(block, axis, [(i, (i + distance) % count) for i in range(count)])


def call(kernel, outs, args, specs, cost, scratch=(), aliases=None, out_specs=None, limit=16):
    args = [
        pltpu.with_memory_space_constraint(arg, pltpu.HBM) if spec is HBM else arg
        for arg, spec in zip(args, specs)
    ]
    return pl.pallas_call(
        kernel,
        out_shape=outs,
        in_specs=specs,
        out_specs=out_specs or [VMEM] * len(outs),
        scratch_shapes=list(scratch),
        input_output_aliases=aliases or {},
        compiler_params=pltpu.CompilerParams(vmem_limit_bytes=limit * MIB),
        cost_estimate=pl.CostEstimate(flops=cost[0], bytes_accessed=cost[1], transcendentals=0),
        name=kernel.__name__,
    )(*args)


def shape(dims, kind=BF16):
    return jax.ShapeDtypeStruct(dims, kind)


def block_rows(where_ref, k, width):
    return pl.ds(pl.multiple_of(where_ref[k] * width, width), width)


def loaded(coef, pair_t):
    def loaded_kernel(coef_ref, pair_ref, coef_out, pair_out, sems):
        copies = [
            pltpu.make_async_copy(coef_ref, coef_out, sems.at[0]),
            pltpu.make_async_copy(pair_ref, pair_out, sems.at[1]),
        ]
        for copy in copies:
            copy.start()
        for copy in copies:
            copy.wait()

    return call(
        loaded_kernel,
        [shape(coef.shape), shape(pair_t.shape)],
        (coef, pair_t),
        [HBM, HBM],
        (0, 1 * MIB),
        [pltpu.SemaphoreType.DMA((2,))],
    )


def density_parts(where, own, mate, pair_own, pair_mate):
    pairs, width = pair_mate.shape

    def density_parts_kernel(where_ref, own_ref, mate_ref, po_ref, pm_ref, *outs):
        left = jnp.concatenate([po_ref[...], pm_ref[...]], axis=1)
        for k, out in enumerate(outs):
            rows = block_rows(where_ref, k, width)
            right = jnp.concatenate([own_ref[rows, :], mate_ref[rows, :]], axis=1)
            out[...] = dot(left, right, ((1,), (1,))).astype(BF16)

    return call(
        density_parts_kernel,
        [shape((pairs, width))] * 4,
        (where, own, mate, pair_own, pair_mate),
        [SMEM] + [VMEM] * 4,
        (16 * pairs * width * width, 1 * MIB),
    )


def staged(where, cols, coupling, pair_alpha_t, beta_ops, tie):
    pairs, width = coupling.shape[0], beta_ops.shape[0]
    listed = beta_ops.shape[1] // width
    count = lax.axis_size(BETA)

    def staged_kernel(
        where_ref, cols_ref, c_ref, pa_ref, ops_ref, tie_ref, c_out, pa_out, w_out, pa_v, ops_v, sems
    ):
        rows = block_rows(where_ref, 0, width)
        copies = [
            pltpu.make_async_copy(ops_ref, ops_v, sems.at[0]),
            pltpu.make_async_copy(pa_ref.at[:, rows], pa_v, sems.at[1]),
            pltpu.make_async_copy(c_ref, c_out, sems.at[2]),
        ]
        for copy in copies:
            copy.start()
        copies[0].wait()
        core = where_ref[8]
        for n in range(5):
            offset = n if n in (0, 2, 4) else jnp.where(core == 0, n, 4 - n)
            tile = jnp.zeros((width, width), F32)
            for k in range(listed):
                here = lax.rem(cols_ref[0, k] - where_ref[9] + 2 + count, count)
                part = ops_v[:, k * width : (k + 1) * width].astype(F32)
                tile = jnp.where(here == offset, part, tile)
            w_out[:, n * width : (n + 1) * width] = tile.astype(BF16)
        copies[1].wait()
        pa_out[...] = pa_v[...].astype(F32).T
        copies[2].wait()

    return call(
        staged_kernel,
        [shape(coupling.shape), shape((width, pairs), F32), shape((width, 5 * width))],
        (where, cols, coupling, pair_alpha_t, beta_ops, tie),
        [SMEM, SMEM, HBM, HBM, HBM, ANY],
        (pairs * pairs, 2 * MIB),
        [
            pltpu.VMEM((pairs, width), BF16),
            pltpu.VMEM(beta_ops.shape, BF16),
            pltpu.SemaphoreType.DMA((3,)),
        ],
    )


def excited_block(near, far, coupling, scale):
    pairs, width = near.shape

    def excited_block_kernel(near_ref, far_ref, coupling_ref, scale_ref, out_ref):
        total = near_ref[...].astype(F32) + far_ref[...].astype(F32)
        density = total.T.astype(BF16)
        out_ref[...] = (dot(density, coupling_ref[...]) * scale_ref[...]).astype(BF16)

    return call(
        excited_block_kernel,
        [shape((width, pairs))],
        (near, far, coupling, scale),
        [VMEM] * 4,
        (2 * pairs * pairs * width, 2 * MIB),
    )[0]


def mixed_mate(blocks, pair_mate):
    width = blocks[0].shape[0]
    pairs = blocks[0].shape[1]

    def mixed_mate_kernel(*refs):
        right = refs[4][...]
        for k in range(4):
            refs[5][k] = dot(refs[k][...], right).astype(BF16)

    return call(
        mixed_mate_kernel,
        [shape((4, width, width))],
        (*blocks, pair_mate),
        [VMEM] * 5,
        (8 * pairs * width * width, 1 * MIB),
    )[0]


def finished_own(where, same, blocks, pair_own, denominators):
    rows, width = same.shape

    def finished_own_kernel(where_ref, same_ref, e0, e1, e2, e3, pair_ref, den_ref, out, part, sems):
        right = pair_ref[...]
        copies = []
        for k, block in enumerate((e0, e1, e2, e3)):
            at = block_rows(where_ref, k, width)
            part[k] = (same_ref[at, :] + dot(block[...], right)) / den_ref[at, :]
            copies.append(pltpu.make_async_copy(part.at[k], out.at[at, :], sems.at[k]))
            copies[-1].start()
        for copy in copies:
            copy.wait()

    return call(
        finished_own_kernel,
        [shape((rows, width), F32)],
        (where, same, *blocks, pair_own, denominators),
        [SMEM] + [VMEM] * 7,
        (rows * width * 600, 2 * MIB),
        [pltpu.VMEM((4, width, width), F32), pltpu.SemaphoreType.DMA((4,))],
        out_specs=[HBM],
    )[0]


def finished_mate(where, same, theirs, denominators, begun):
    rows, width = same.shape

    def finished_mate_kernel(where_ref, same_ref, theirs_ref, den_ref, begun_ref, out, part, sems):
        copies = []
        for k in range(4):
            at = block_rows(where_ref, 4 + k, width)
            part[k] = (same_ref[at, :] + theirs_ref[k].astype(F32)) / den_ref[at, :]
            copies.append(pltpu.make_async_copy(part.at[k], out.at[at, :], sems.at[k]))
            copies[-1].start()
        for copy in copies:
            copy.wait()

    return call(
        finished_mate_kernel,
        [shape((rows, width), F32)],
        (where, same, theirs, denominators, begun),
        [SMEM] + [VMEM] * 3 + [ANY],
        (rows * width * 2, 2 * MIB),
        [pltpu.VMEM((4, width, width), F32), pltpu.SemaphoreType.DMA((4,))],
        aliases={4: 0},
        out_specs=[HBM],
    )[0]


def same_spin_beta(blocks, placed):
    rows, width = blocks[0].shape

    def same_spin_beta_kernel(b0, b1, b2, b3, b4, w_ref, out_ref):
        left = jnp.concatenate([b[...] for b in (b0, b1, b2, b3, b4)], axis=1)
        out_ref[...] = dot(left, w_ref[...], ((1,), (1,)))

    return call(
        same_spin_beta_kernel,
        [shape((rows, width), F32)],
        (*blocks, placed),
        [VMEM] * 6,
        (2 * rows * width * width * 5, 2 * MIB),
        limit=24,
    )[0]


def same_spin_alpha(where, cols, blocks, alpha_ops, start):
    rows, width = start.shape
    depth = blocks[0].shape[0]
    step = depth // 2
    steps = alpha_ops.shape[1] // step
    count = lax.axis_size(ALPHA)

    def same_spin_alpha_kernel(
        where_ref, cols_ref, own_ref, near_ref, far_ref, ops_ref, start_ref, out_ref, ops_v, sems
    ):
        copies = [
            pltpu.make_async_copy(ops_ref.at[:, s * step : (s + 1) * step], ops_v.at[s], sems.at[s])
            for s in range(steps)
        ]
        for copy in copies:
            copy.start()
        for s, copy in enumerate(copies):
            offset = lax.rem(cols_ref[0, s // 2] - where_ref[10] + 1 + count, count)
            at = slice((s % 2) * step, (s % 2 + 1) * step)
            picked = jnp.where(
                offset == 1,
                own_ref[at, :],
                jnp.where(offset == where_ref[11], near_ref[at, :], far_ref[at, :]),
            )
            copy.wait()
            before = start_ref[...] if s == 0 else out_ref[...]
            out_ref[...] = before + dot(ops_v[s], picked)

    return call(
        same_spin_alpha_kernel,
        [shape((rows, width), F32)],
        (where, cols, *blocks, alpha_ops, start),
        [SMEM, SMEM] + [VMEM] * 3 + [HBM, VMEM],
        (2 * rows * width * depth * 4, 10 * MIB),
        [pltpu.VMEM((steps, rows, step), BF16), pltpu.SemaphoreType.DMA((steps,))],
        limit=24,
    )[0]


def local(
    coef,
    beta_ops,
    beta_cols,
    alpha_ops,
    alpha_cols,
    pair_alpha,
    pair_beta,
    pair_coupling,
    denominators,
):
    y, core = lax.axis_index("y"), lax.axis_index("c")
    low = lax.axis_index("zl")
    row_blocks = [(y ^ k) * 2 for k in range(4)]
    where = [r + core for r in row_blocks] + [r + 1 - core for r in row_blocks]
    where += [core, lax.axis_index(BETA), lax.axis_index(ALPHA), 2 - 2 * low]
    where = jnp.stack(where).astype(jnp.int32)

    pair_t = pair_beta.T
    mate = swapped(coef, "c", 1)
    pair_mate = swapped(pair_t, "c", 1)
    coef_v, pair_v = loaded(coef, pair_t)

    below = rotated(coef, BETA, 2)
    above = rotated(coef, BETA, -2)
    near = swapped(coef, "zl", 1)
    xs, route = lax.axis_size("x"), []
    for i in range(xs):
        route += [(2 * i, 2 * ((i + 1) % xs)), (2 * i + 1, 2 * ((i - 1) % xs) + 1)]
    far = lax.ppermute(near, ALPHA, route)

    parts = density_parts(where, coef_v, mate, pair_v, pair_mate)
    coupling, scale, placed = staged(
        where, beta_cols, pair_coupling, pair_alpha.T, beta_ops, parts[0]
    )
    got = [swapped(parts[k], "y", k) for k in (1, 3, 2)]
    *got, below, above = lax.optimization_barrier((*got, below, above))
    total = parts[0].astype(F32)
    for part in got:
        total = total + part.astype(F32)
    total = total.astype(BF16)
    total, coupling, scale, placed = lax.optimization_barrier((total, coupling, scale, placed))

    zs = lax.axis_size("zh")
    steps = [[(2 * i + h, 2 * (i ^ m[h]) + h) for i in range(zs) for h in (0, 1)] for m in ((1, 3), (3, 1))]
    first = lax.ppermute(total, ("zh", "c"), steps[0])
    total = (total.astype(F32) + first.astype(F32)).astype(BF16)
    passed = jnp.where(core == 0, above, below)
    total, passed = lax.optimization_barrier((total, passed))
    crossed = swapped(passed, "c", 1)
    second = lax.ppermute(total, ("zh", "c"), steps[1])
    same = same_spin_beta([below, crossed, coef_v, mate, above], placed)
    second, same = lax.optimization_barrier((second, same))

    excited = excited_block(total, second, coupling, scale)
    blocks = [excited] + [swapped(excited, "y", k) for k in (1, 2, 3)]
    same = same_spin_alpha(where, alpha_cols, [coef_v, near, far], alpha_ops, same)
    *blocks, same = lax.optimization_barrier((*blocks, same))

    theirs = mixed_mate(blocks, pair_mate)
    begun = finished_own(where, same, blocks, pair_v, denominators)
    return finished_mate(where, same, swapped(theirs, "c", 1), denominators, begun)


def solution(mesh):
    finer = Mesh(mesh.devices.reshape(4, 2, 4, 4, 2), (*ALPHA, *BETA))
    placed = (
        P(ALPHA, BETA),
        P(BETA, None),
        P(BETA, None),
        P(ALPHA, None),
        P(ALPHA, None),
        P(ALPHA, None),
        P(BETA, None),
        P(),
        P(ALPHA, BETA),
    )
    return jax.shard_map(
        local, mesh=finer, in_specs=placed, out_specs=P(ALPHA, BETA), check_vma=False
    )
```

```python
import jax
import jax.numpy as jnp
from jax import lax
from jax.experimental import pallas as pl
from jax.experimental.pallas import tpu as pltpu
from jax.sharding import Mesh
from jax.sharding import PartitionSpec as P

ALPHA = ("x", "zl")
BETA = ("y", "zh", "c")
F32 = jnp.float32
BF16 = jnp.bfloat16
SMEM = pl.BlockSpec(memory_space=pltpu.SMEM)
VMEM = pl.BlockSpec(memory_space=pltpu.VMEM)
HBM = pl.BlockSpec(memory_space=pltpu.HBM)
ANY = pl.BlockSpec(memory_space=pl.ANY)
MIB = 1 << 20


def dot(a, b, dims=((1,), (0,))):
    return lax.dot_general(a, b, (dims, ((), ())), preferred_element_type=F32)


def swapped(block, axis, mask):
    count = lax.axis_size(axis)
    return lax.ppermute(block, axis, [(i, i ^ mask) for i in range(count)])


def rotated(block, axis, distance):
    count = lax.axis_size(axis)
    return lax.ppermute(block, axis, [(i, (i + distance) % count) for i in range(count)])


def call(kernel, outs, args, specs, cost, scratch=(), aliases=None, out_specs=None, limit=16):
    args = [
        pltpu.with_memory_space_constraint(arg, pltpu.HBM) if spec is HBM else arg
        for arg, spec in zip(args, specs)
    ]
    return pl.pallas_call(
        kernel,
        out_shape=outs,
        in_specs=specs,
        out_specs=out_specs or [VMEM] * len(outs),
        scratch_shapes=list(scratch),
        input_output_aliases=aliases or {},
        compiler_params=pltpu.CompilerParams(vmem_limit_bytes=limit * MIB),
        cost_estimate=pl.CostEstimate(flops=cost[0], bytes_accessed=cost[1], transcendentals=0),
        name=kernel.__name__,
    )(*args)


def shape(dims, kind=BF16):
    return jax.ShapeDtypeStruct(dims, kind)


def block_rows(where_ref, k, width):
    return pl.ds(pl.multiple_of(where_ref[k] * width, width), width)


def loaded(coef, pair_t):
    def loaded_kernel(coef_ref, pair_ref, coef_out, pair_out, sems):
        copies = [
            pltpu.make_async_copy(coef_ref, coef_out, sems.at[0]),
            pltpu.make_async_copy(pair_ref, pair_out, sems.at[1]),
        ]
        for copy in copies:
            copy.start()
        for copy in copies:
            copy.wait()

    return call(
        loaded_kernel,
        [shape(coef.shape), shape(pair_t.shape)],
        (coef, pair_t),
        [HBM, HBM],
        (0, 1 * MIB),
        [pltpu.SemaphoreType.DMA((2,))],
    )


def density_parts(where, own, mate, pair_own, pair_mate):
    pairs, width = pair_mate.shape

    def density_parts_kernel(where_ref, own_ref, mate_ref, po_ref, pm_ref, *outs):
        left = jnp.concatenate([po_ref[...], pm_ref[...]], axis=1)
        for k, out in enumerate(outs):
            rows = block_rows(where_ref, k, width)
            right = jnp.concatenate([own_ref[rows, :], mate_ref[rows, :]], axis=1)
            out[...] = dot(left, right, ((1,), (1,))).astype(BF16)

    return call(
        density_parts_kernel,
        [shape((pairs, width))] * 4,
        (where, own, mate, pair_own, pair_mate),
        [SMEM] + [VMEM] * 4,
        (16 * pairs * width * width, 1 * MIB),
    )


def staged(where, cols, coupling, pair_alpha_t, beta_ops, tie):
    pairs, width = coupling.shape[0], beta_ops.shape[0]
    listed = beta_ops.shape[1] // width
    count = lax.axis_size(BETA)

    def staged_kernel(
        where_ref, cols_ref, c_ref, pa_ref, ops_ref, tie_ref, c_out, pa_out, w_out, pa_v, ops_v, sems
    ):
        rows = block_rows(where_ref, 0, width)
        copies = [
            pltpu.make_async_copy(ops_ref, ops_v, sems.at[0]),
            pltpu.make_async_copy(pa_ref.at[:, rows], pa_v, sems.at[1]),
            pltpu.make_async_copy(c_ref, c_out, sems.at[2]),
        ]
        for copy in copies:
            copy.start()
        copies[0].wait()
        core = where_ref[8]
        for n in range(5):
            offset = n if n in (0, 2, 4) else jnp.where(core == 0, n, 4 - n)
            tile = jnp.zeros((width, width), F32)
            for k in range(listed):
                here = lax.rem(cols_ref[0, k] - where_ref[9] + 2 + count, count)
                part = ops_v[:, k * width : (k + 1) * width].astype(F32)
                tile = jnp.where(here == offset, part, tile)
            w_out[:, n * width : (n + 1) * width] = tile.astype(BF16)
        copies[1].wait()
        pa_out[...] = pa_v[...].astype(F32).T
        copies[2].wait()

    return call(
        staged_kernel,
        [shape(coupling.shape), shape((width, pairs), F32), shape((width, 5 * width))],
        (where, cols, coupling, pair_alpha_t, beta_ops, tie),
        [SMEM, SMEM, HBM, HBM, HBM, ANY],
        (pairs * pairs, 2 * MIB),
        [
            pltpu.VMEM((pairs, width), BF16),
            pltpu.VMEM(beta_ops.shape, BF16),
            pltpu.SemaphoreType.DMA((3,)),
        ],
    )


def excited_block(near, far, coupling, scale):
    pairs, width = near.shape

    def excited_block_kernel(near_ref, far_ref, coupling_ref, scale_ref, out_ref):
        total = near_ref[...].astype(F32) + far_ref[...].astype(F32)
        density = total.T.astype(BF16)
        out_ref[...] = (dot(density, coupling_ref[...]) * scale_ref[...]).astype(BF16)

    return call(
        excited_block_kernel,
        [shape((width, pairs))],
        (near, far, coupling, scale),
        [VMEM] * 4,
        (2 * pairs * pairs * width, 2 * MIB),
    )[0]


def mixed_mate(blocks, pair_mate):
    width = blocks[0].shape[0]
    pairs = blocks[0].shape[1]

    def mixed_mate_kernel(*refs):
        right = refs[4][...]
        for k in range(4):
            refs[5][k] = dot(refs[k][...], right).astype(BF16)

    return call(
        mixed_mate_kernel,
        [shape((4, width, width))],
        (*blocks, pair_mate),
        [VMEM] * 5,
        (8 * pairs * width * width, 1 * MIB),
    )[0]


def finished_own(where, same, blocks, pair_own, denominators):
    rows, width = same.shape

    def finished_own_kernel(where_ref, same_ref, e0, e1, e2, e3, pair_ref, den_ref, out, part, sems):
        right = pair_ref[...]
        copies = []
        for k, block in enumerate((e0, e1, e2, e3)):
            at = block_rows(where_ref, k, width)
            part[k] = (same_ref[at, :] + dot(block[...], right)) / den_ref[at, :]
            copies.append(pltpu.make_async_copy(part.at[k], out.at[at, :], sems.at[k]))
            copies[-1].start()
        for copy in copies:
            copy.wait()

    return call(
        finished_own_kernel,
        [shape((rows, width), F32)],
        (where, same, *blocks, pair_own, denominators),
        [SMEM] + [VMEM] * 7,
        (rows * width * 600, 2 * MIB),
        [pltpu.VMEM((4, width, width), F32), pltpu.SemaphoreType.DMA((4,))],
        out_specs=[HBM],
    )[0]


def finished_mate(where, same, theirs, denominators, begun):
    rows, width = same.shape

    def finished_mate_kernel(where_ref, same_ref, theirs_ref, den_ref, begun_ref, out, part, sems):
        copies = []
        for k in range(4):
            at = block_rows(where_ref, 4 + k, width)
            part[k] = (same_ref[at, :] + theirs_ref[k].astype(F32)) / den_ref[at, :]
            copies.append(pltpu.make_async_copy(part.at[k], out.at[at, :], sems.at[k]))
            copies[-1].start()
        for copy in copies:
            copy.wait()

    return call(
        finished_mate_kernel,
        [shape((rows, width), F32)],
        (where, same, theirs, denominators, begun),
        [SMEM] + [VMEM] * 3 + [ANY],
        (rows * width * 2, 2 * MIB),
        [pltpu.VMEM((4, width, width), F32), pltpu.SemaphoreType.DMA((4,))],
        aliases={4: 0},
        out_specs=[HBM],
    )[0]


def same_spin_beta(blocks, placed):
    rows, width = blocks[0].shape

    def same_spin_beta_kernel(b0, b1, b2, b3, b4, w_ref, out_ref):
        left = jnp.concatenate([b[...] for b in (b0, b1, b2, b3, b4)], axis=1)
        out_ref[...] = dot(left, w_ref[...], ((1,), (1,)))

    return call(
        same_spin_beta_kernel,
        [shape((rows, width), F32)],
        (*blocks, placed),
        [VMEM] * 6,
        (2 * rows * width * width * 5, 2 * MIB),
        limit=24,
    )[0]


def same_spin_alpha(where, cols, blocks, alpha_ops, start):
    rows, width = start.shape
    depth = blocks[0].shape[0]
    span = alpha_ops.shape[1]
    step = 256
    count = lax.axis_size(ALPHA)

    def same_spin_alpha_kernel(
        where_ref, cols_ref, own_ref, near_ref, far_ref, ops_ref, start_ref, out_ref, ops_v, picked, sems
    ):
        copies = [
            pltpu.make_async_copy(ops_ref.at[r : r + step, :], ops_v.at[r : r + step, :], sems.at[n])
            for n, r in enumerate(range(0, rows, step))
        ]
        for copy in copies:
            copy.start()
        for k in range(span // depth):
            offset = lax.rem(cols_ref[0, k] - where_ref[10] + 1 + count, count)
            picked[k * depth : (k + 1) * depth, :] = jnp.where(
                offset == 1,
                own_ref[...],
                jnp.where(offset == where_ref[11], near_ref[...], far_ref[...]),
            )
        for copy, r in zip(copies, range(0, rows, step)):
            copy.wait()
            at = slice(r, r + step)
            out_ref[at, :] = start_ref[at, :] + dot(ops_v[at, :], picked[...])

    return call(
        same_spin_alpha_kernel,
        [shape((rows, width), F32)],
        (where, cols, *blocks, alpha_ops, start),
        [SMEM, SMEM] + [VMEM] * 3 + [HBM, VMEM],
        (2 * rows * width * depth * 4, 10 * MIB),
        [
            pltpu.VMEM((rows, span), BF16),
            pltpu.VMEM((span, width), BF16),
            pltpu.SemaphoreType.DMA((rows // step,)),
        ],
        limit=24,
    )[0]


def local(
    coef,
    beta_ops,
    beta_cols,
    alpha_ops,
    alpha_cols,
    pair_alpha,
    pair_beta,
    pair_coupling,
    denominators,
):
    y, core = lax.axis_index("y"), lax.axis_index("c")
    low = lax.axis_index("zl")
    row_blocks = [(y ^ k) * 2 for k in range(4)]
    where = [r + core for r in row_blocks] + [r + 1 - core for r in row_blocks]
    where += [core, lax.axis_index(BETA), lax.axis_index(ALPHA), 2 - 2 * low]
    where = jnp.stack(where).astype(jnp.int32)

    pair_t = pair_beta.T
    mate = swapped(coef, "c", 1)
    pair_mate = swapped(pair_t, "c", 1)
    coef_v, pair_v = loaded(coef, pair_t)

    below = rotated(coef_v, BETA, 2)
    above = rotated(coef_v, BETA, -2)
    xs, route = lax.axis_size("x"), []
    for i in range(xs):
        route += [(2 * i, 2 * ((i + 1) % xs)), (2 * i + 1, 2 * ((i - 1) % xs) + 1)]

    parts = density_parts(where, coef_v, mate, pair_v, pair_mate)
    coupling, scale, placed = staged(
        where, beta_cols, pair_coupling, pair_alpha.T, beta_ops, parts[0]
    )
    got = [swapped(parts[k], "y", k) for k in (1, 3, 2)]
    got_first = got[0]
    *got, below, above = lax.optimization_barrier((*got, below, above))
    start, _ = lax.optimization_barrier((coef_v, got_first))
    near = swapped(start, "zl", 1)
    total = parts[0].astype(F32)
    for part in got:
        total = total + part.astype(F32)
    total = total.astype(BF16)
    total, coupling, scale, placed = lax.optimization_barrier((total, coupling, scale, placed))

    far = lax.ppermute(near, ALPHA, route)
    zs = lax.axis_size("zh")
    steps = [[(2 * i + h, 2 * (i ^ m[h]) + h) for i in range(zs) for h in (0, 1)] for m in ((1, 3), (3, 1))]
    first = lax.ppermute(total, ("zh", "c"), steps[0])
    total = (total.astype(F32) + first.astype(F32)).astype(BF16)
    passed = jnp.where(core == 0, above, below)
    total, passed = lax.optimization_barrier((total, passed))
    crossed = swapped(passed, "c", 1)
    second = lax.ppermute(total, ("zh", "c"), steps[1])
    same = same_spin_beta([below, crossed, coef_v, mate, above], placed)
    second, same = lax.optimization_barrier((second, same))

    excited = excited_block(total, second, coupling, scale)
    blocks = [excited] + [swapped(excited, "y", k) for k in (1, 2, 3)]
    same = same_spin_alpha(where, alpha_cols, [coef_v, near, far], alpha_ops, same)
    *blocks, same = lax.optimization_barrier((*blocks, same))

    theirs = mixed_mate(blocks, pair_mate)
    begun = finished_own(where, same, blocks, pair_v, denominators)
    return finished_mate(where, same, swapped(theirs, "c", 1), denominators, begun)


def solution(mesh):
    finer = Mesh(mesh.devices.reshape(4, 2, 4, 4, 2), (*ALPHA, *BETA))
    placed = (
        P(ALPHA, BETA),
        P(BETA, None),
        P(BETA, None),
        P(ALPHA, None),
        P(ALPHA, None),
        P(ALPHA, None),
        P(BETA, None),
        P(),
        P(ALPHA, BETA),
    )
    return jax.shard_map(
        local, mesh=finer, in_specs=placed, out_specs=P(ALPHA, BETA), check_vma=False
    )
```

```python
import jax
import jax.numpy as jnp
from jax import lax
from jax.experimental import pallas as pl
from jax.experimental.pallas import tpu as pltpu
from jax.sharding import Mesh
from jax.sharding import PartitionSpec as P

ALPHA = ("x", "zl")
BETA = ("y", "zh", "c")
F32 = jnp.float32
BF16 = jnp.bfloat16
SMEM = pl.BlockSpec(memory_space=pltpu.SMEM)
VMEM = pl.BlockSpec(memory_space=pltpu.VMEM)
HBM = pl.BlockSpec(memory_space=pltpu.HBM)
ANY = pl.BlockSpec(memory_space=pl.ANY)
MIB = 1 << 20


def dot(a, b, dims=((1,), (0,))):
    return lax.dot_general(a, b, (dims, ((), ())), preferred_element_type=F32)


def swapped(block, axis, mask):
    count = lax.axis_size(axis)
    return lax.ppermute(block, axis, [(i, i ^ mask) for i in range(count)])


def call(kernel, outs, args, specs, cost, scratch=(), aliases=None, out_specs=None, limit=16):
    args = [
        pltpu.with_memory_space_constraint(arg, pltpu.HBM) if spec is HBM else arg
        for arg, spec in zip(args, specs)
    ]
    return pl.pallas_call(
        kernel,
        out_shape=outs,
        in_specs=specs,
        out_specs=out_specs or [VMEM] * len(outs),
        scratch_shapes=list(scratch),
        input_output_aliases=aliases or {},
        compiler_params=pltpu.CompilerParams(vmem_limit_bytes=limit * MIB),
        cost_estimate=pl.CostEstimate(flops=cost[0], bytes_accessed=cost[1], transcendentals=0),
        name=kernel.__name__,
    )(*args)


def shape(dims, kind=BF16):
    return jax.ShapeDtypeStruct(dims, kind)


def block_rows(where_ref, k, width):
    return pl.ds(pl.multiple_of(where_ref[k] * width, width), width)


def loaded(coef, pair_t):
    def loaded_kernel(coef_ref, pair_ref, coef_out, pair_out, sems):
        copies = [
            pltpu.make_async_copy(coef_ref, coef_out, sems.at[0]),
            pltpu.make_async_copy(pair_ref, pair_out, sems.at[1]),
        ]
        for copy in copies:
            copy.start()
        for copy in copies:
            copy.wait()

    return call(
        loaded_kernel,
        [shape(coef.shape), shape(pair_t.shape)],
        (coef, pair_t),
        [HBM, HBM],
        (0, 1 * MIB),
        [pltpu.SemaphoreType.DMA((2,))],
    )


def density_parts(where, own, mate, pair_own, pair_mate):
    pairs, width = pair_mate.shape

    def density_parts_kernel(where_ref, own_ref, mate_ref, po_ref, pm_ref, *outs):
        left = jnp.concatenate([po_ref[...], pm_ref[...]], axis=1)
        for k, out in enumerate(outs):
            rows = block_rows(where_ref, k, width)
            right = jnp.concatenate([own_ref[rows, :], mate_ref[rows, :]], axis=1)
            out[...] = dot(left, right, ((1,), (1,))).astype(BF16)

    return call(
        density_parts_kernel,
        [shape((pairs, width))] * 4,
        (where, own, mate, pair_own, pair_mate),
        [SMEM] + [VMEM] * 4,
        (16 * pairs * width * width, 1 * MIB),
    )


def staged(where, cols, coupling, pair_alpha_t, beta_ops, tie):
    pairs, width = coupling.shape[0], beta_ops.shape[0]
    listed = beta_ops.shape[1] // width
    count = lax.axis_size(BETA)

    def staged_kernel(
        where_ref, cols_ref, c_ref, pa_ref, ops_ref, tie_ref, c_out, pa_out, w_out, pa_v, ops_v, sems
    ):
        rows = block_rows(where_ref, 0, width)
        copies = [
            pltpu.make_async_copy(ops_ref, ops_v, sems.at[0]),
            pltpu.make_async_copy(pa_ref.at[:, rows], pa_v, sems.at[1]),
            pltpu.make_async_copy(c_ref, c_out, sems.at[2]),
        ]
        for copy in copies:
            copy.start()
        copies[0].wait()
        core = where_ref[8]
        for n in range(5):
            side = 2 - where_ref[11] if n in (0, 4) else 2 * core
            offset = jnp.where(side == 0, n, 4 - n)
            tile = jnp.zeros((width, width), F32)
            for k in range(listed):
                here = lax.rem(cols_ref[0, k] - where_ref[9] + 2 + count, count)
                part = ops_v[:, k * width : (k + 1) * width].astype(F32)
                tile = jnp.where(here == offset, part, tile)
            w_out[:, n * width : (n + 1) * width] = tile.astype(BF16)
        copies[1].wait()
        pa_out[...] = pa_v[...].astype(F32).T
        copies[2].wait()

    return call(
        staged_kernel,
        [shape(coupling.shape), shape((width, pairs), F32), shape((width, 5 * width))],
        (where, cols, coupling, pair_alpha_t, beta_ops, tie),
        [SMEM, SMEM, HBM, HBM, HBM, ANY],
        (pairs * pairs, 2 * MIB),
        [
            pltpu.VMEM((pairs, width), BF16),
            pltpu.VMEM(beta_ops.shape, BF16),
            pltpu.SemaphoreType.DMA((3,)),
        ],
    )


def excited_block(near, far, coupling, scale):
    pairs, width = near.shape

    def excited_block_kernel(near_ref, far_ref, coupling_ref, scale_ref, out_ref):
        total = near_ref[...].astype(F32) + far_ref[...].astype(F32)
        density = total.T.astype(BF16)
        out_ref[...] = (dot(density, coupling_ref[...]) * scale_ref[...]).astype(BF16)

    return call(
        excited_block_kernel,
        [shape((width, pairs))],
        (near, far, coupling, scale),
        [VMEM] * 4,
        (2 * pairs * pairs * width, 2 * MIB),
    )[0]


def mixed_mate(blocks, pair_mate):
    width = blocks[0].shape[0]
    pairs = blocks[0].shape[1]

    def mixed_mate_kernel(*refs):
        right = refs[4][...]
        for k in range(4):
            refs[5][k] = dot(refs[k][...], right).astype(BF16)

    return call(
        mixed_mate_kernel,
        [shape((4, width, width))],
        (*blocks, pair_mate),
        [VMEM] * 5,
        (8 * pairs * width * width, 1 * MIB),
    )[0]


def finished_own(where, same, blocks, pair_own, denominators):
    rows, width = same.shape

    def finished_own_kernel(where_ref, same_ref, e0, e1, e2, e3, pair_ref, den_ref, out, part, sems):
        right = pair_ref[...]
        copies = []
        for k, block in enumerate((e0, e1, e2, e3)):
            at = block_rows(where_ref, k, width)
            part[k] = (same_ref[at, :] + dot(block[...], right)) / den_ref[at, :]
            copies.append(pltpu.make_async_copy(part.at[k], out.at[at, :], sems.at[k]))
            copies[-1].start()
        for copy in copies:
            copy.wait()

    return call(
        finished_own_kernel,
        [shape((rows, width), F32)],
        (where, same, *blocks, pair_own, denominators),
        [SMEM] + [VMEM] * 7,
        (rows * width * 600, 2 * MIB),
        [pltpu.VMEM((4, width, width), F32), pltpu.SemaphoreType.DMA((4,))],
        out_specs=[HBM],
    )[0]


def finished_mate(where, same, theirs, denominators, begun):
    rows, width = same.shape

    def finished_mate_kernel(where_ref, same_ref, theirs_ref, den_ref, begun_ref, out, part, sems):
        copies = []
        for k in range(4):
            at = block_rows(where_ref, 4 + k, width)
            part[k] = (same_ref[at, :] + theirs_ref[k].astype(F32)) / den_ref[at, :]
            copies.append(pltpu.make_async_copy(part.at[k], out.at[at, :], sems.at[k]))
            copies[-1].start()
        for copy in copies:
            copy.wait()

    return call(
        finished_mate_kernel,
        [shape((rows, width), F32)],
        (where, same, theirs, denominators, begun),
        [SMEM] + [VMEM] * 3 + [ANY],
        (rows * width * 2, 2 * MIB),
        [pltpu.VMEM((4, width, width), F32), pltpu.SemaphoreType.DMA((4,))],
        aliases={4: 0},
        out_specs=[HBM],
    )[0]


def same_spin_beta(blocks, placed):
    rows, width = blocks[0].shape

    def same_spin_beta_kernel(b0, b1, b2, b3, b4, w_ref, out_ref):
        left = jnp.concatenate([b[...] for b in (b0, b1, b2, b3, b4)], axis=1)
        out_ref[...] = dot(left, w_ref[...], ((1,), (1,)))

    return call(
        same_spin_beta_kernel,
        [shape((rows, width), F32)],
        (*blocks, placed),
        [VMEM] * 6,
        (2 * rows * width * width * 5, 2 * MIB),
        limit=24,
    )[0]


def same_spin_alpha(where, cols, blocks, alpha_ops, start):
    rows, width = start.shape
    depth = blocks[0].shape[0]
    span = alpha_ops.shape[1]
    step = 256
    count = lax.axis_size(ALPHA)

    def same_spin_alpha_kernel(
        where_ref, cols_ref, own_ref, near_ref, far_ref, ops_ref, start_ref, out_ref, ops_v, picked, sems
    ):
        copies = [
            pltpu.make_async_copy(ops_ref.at[r : r + step, :], ops_v.at[r : r + step, :], sems.at[n])
            for n, r in enumerate(range(0, rows, step))
        ]
        for copy in copies:
            copy.start()
        for k in range(span // depth):
            offset = lax.rem(cols_ref[0, k] - where_ref[10] + 1 + count, count)
            picked[k * depth : (k + 1) * depth, :] = jnp.where(
                offset == 1,
                own_ref[...],
                jnp.where(offset == where_ref[11], near_ref[...], far_ref[...]),
            )
        for copy, r in zip(copies, range(0, rows, step)):
            copy.wait()
            at = slice(r, r + step)
            out_ref[at, :] = start_ref[at, :] + dot(ops_v[at, :], picked[...])

    return call(
        same_spin_alpha_kernel,
        [shape((rows, width), F32)],
        (where, cols, *blocks, alpha_ops, start),
        [SMEM, SMEM] + [VMEM] * 3 + [HBM, VMEM],
        (2 * rows * width * depth * 4, 10 * MIB),
        [
            pltpu.VMEM((rows, span), BF16),
            pltpu.VMEM((span, width), BF16),
            pltpu.SemaphoreType.DMA((rows // step,)),
        ],
        limit=24,
    )[0]


def local(
    coef,
    beta_ops,
    beta_cols,
    alpha_ops,
    alpha_cols,
    pair_alpha,
    pair_beta,
    pair_coupling,
    denominators,
):
    y, core = lax.axis_index("y"), lax.axis_index("c")
    low = lax.axis_index("zl")
    row_blocks = [(y ^ k) * 2 for k in range(4)]
    where = [r + core for r in row_blocks] + [r + 1 - core for r in row_blocks]
    where += [core, lax.axis_index(BETA), lax.axis_index(ALPHA), 2 - 2 * low]
    where = jnp.stack(where).astype(jnp.int32)

    pair_t = pair_beta.T
    mate = swapped(coef, "c", 1)
    pair_mate = swapped(pair_t, "c", 1)
    coef_v, pair_v = loaded(coef, pair_t)

    near = swapped(coef_v, "zl", 1)
    chips = lax.axis_size("y") * lax.axis_size("zh")
    border = []
    for q in range(chips):
        for h in (0, 1):
            low_at, high_at = (2 * q + h, 2 * chips + 2 * ((q - 1) % chips) + h)
            border += [(low_at, high_at), (high_at, low_at)]
    over = ("zl", *BETA)
    across = lax.ppermute(coef_v, over, border)
    xs, route = lax.axis_size("x"), []
    for i in range(xs):
        route += [(2 * i, 2 * ((i + 1) % xs)), (2 * i + 1, 2 * ((i - 1) % xs) + 1)]

    parts = density_parts(where, coef_v, mate, pair_v, pair_mate)
    coupling, scale, placed = staged(
        where, beta_cols, pair_coupling, pair_alpha.T, beta_ops, parts[0]
    )
    got = [swapped(parts[k], "y", k) for k in (1, 3, 2)]
    *got, _, _ = lax.optimization_barrier((*got, near, across))
    onward = lax.ppermute(near, over, border)
    returned = swapped(across, "zl", 1)
    total = parts[0].astype(F32)
    for part in got:
        total = total + part.astype(F32)
    total = total.astype(BF16)
    total, coupling, scale, placed = lax.optimization_barrier((total, coupling, scale, placed))

    far = lax.ppermute(near, ALPHA, route)
    zs = lax.axis_size("zh")
    steps = [[(2 * i + h, 2 * (i ^ m[h]) + h) for i in range(zs) for h in (0, 1)] for m in ((1, 3), (3, 1))]
    first = lax.ppermute(total, ("zh", "c"), steps[0])
    total = (total.astype(F32) + first.astype(F32)).astype(BF16)
    passed = jnp.where(core == low, returned, onward)
    total, passed = lax.optimization_barrier((total, passed))
    crossed = swapped(passed, "c", 1)
    second = lax.ppermute(total, ("zh", "c"), steps[1])
    same = same_spin_beta([onward, crossed, coef_v, mate, returned], placed)
    second, same = lax.optimization_barrier((second, same))

    excited = excited_block(total, second, coupling, scale)
    blocks = [excited] + [swapped(excited, "y", k) for k in (1, 2, 3)]
    same = same_spin_alpha(where, alpha_cols, [coef_v, near, far], alpha_ops, same)
    *blocks, same = lax.optimization_barrier((*blocks, same))

    theirs = mixed_mate(blocks, pair_mate)
    begun = finished_own(where, same, blocks, pair_v, denominators)
    return finished_mate(where, same, swapped(theirs, "c", 1), denominators, begun)


def solution(mesh):
    finer = Mesh(mesh.devices.reshape(4, 2, 4, 4, 2), (*ALPHA, *BETA))
    placed = (
        P(ALPHA, BETA),
        P(BETA, None),
        P(BETA, None),
        P(ALPHA, None),
        P(ALPHA, None),
        P(ALPHA, None),
        P(BETA, None),
        P(),
        P(ALPHA, BETA),
    )
    return jax.shard_map(
        local, mesh=finer, in_specs=placed, out_specs=P(ALPHA, BETA), check_vma=False
    )
```

```python
import jax
import jax.numpy as jnp
from jax import lax
from jax.experimental import pallas as pl
from jax.experimental.pallas import tpu as pltpu
from jax.sharding import Mesh
from jax.sharding import PartitionSpec as P

ALPHA = ("x", "zl")
BETA = ("y", "zh", "c")
F32 = jnp.float32
BF16 = jnp.bfloat16
SMEM = pl.BlockSpec(memory_space=pltpu.SMEM)
VMEM = pl.BlockSpec(memory_space=pltpu.VMEM)
HBM = pl.BlockSpec(memory_space=pltpu.HBM)
ANY = pl.BlockSpec(memory_space=pl.ANY)
MIB = 1 << 20


def dot(a, b, dims=((1,), (0,))):
    return lax.dot_general(a, b, (dims, ((), ())), preferred_element_type=F32)


def swapped(block, axis, mask):
    count = lax.axis_size(axis)
    return lax.ppermute(block, axis, [(i, i ^ mask) for i in range(count)])


def crossing(count, masks):
    return [(2 * i + h, 2 * (i ^ masks[h]) + h) for i in range(count) for h in (0, 1)]


def call(kernel, outs, args, specs, cost, scratch=(), aliases=None, out_specs=None, limit=16):
    args = [
        pltpu.with_memory_space_constraint(arg, pltpu.HBM) if spec is HBM else arg
        for arg, spec in zip(args, specs)
    ]
    return pl.pallas_call(
        kernel,
        out_shape=outs,
        in_specs=specs,
        out_specs=out_specs or [VMEM] * len(outs),
        scratch_shapes=list(scratch),
        input_output_aliases=aliases or {},
        compiler_params=pltpu.CompilerParams(vmem_limit_bytes=limit * MIB),
        cost_estimate=pl.CostEstimate(flops=cost[0], bytes_accessed=cost[1], transcendentals=0),
        name=kernel.__name__,
    )(*args)


def shape(dims, kind=BF16):
    return jax.ShapeDtypeStruct(dims, kind)


def block_rows(where_ref, k, width):
    return pl.ds(pl.multiple_of(where_ref[k] * width, width), width)


def loaded(coef, pair_t):
    def loaded_kernel(coef_ref, pair_ref, coef_out, pair_out, sems):
        copies = [
            pltpu.make_async_copy(coef_ref, coef_out, sems.at[0]),
            pltpu.make_async_copy(pair_ref, pair_out, sems.at[1]),
        ]
        for copy in copies:
            copy.start()
        for copy in copies:
            copy.wait()

    return call(
        loaded_kernel,
        [shape(coef.shape), shape(pair_t.shape)],
        (coef, pair_t),
        [HBM, HBM],
        (0, 1 * MIB),
        [pltpu.SemaphoreType.DMA((2,))],
    )


def density_parts(where, own, mate, pair_own, pair_mate):
    pairs, width = pair_mate.shape

    def density_parts_kernel(where_ref, own_ref, mate_ref, po_ref, pm_ref, sent, kept, passing):
        left = jnp.concatenate([po_ref[...], pm_ref[...]], axis=1)
        for k in range(4):
            rows = block_rows(where_ref, 12 + k, width)
            right = jnp.concatenate([own_ref[rows, :], mate_ref[rows, :]], axis=1)
            part = dot(left, right, ((1,), (1,))).astype(BF16)
            if k < 2:
                sent[k] = part
            else:
                (kept, passing)[k - 2][...] = part

    return call(
        density_parts_kernel,
        [shape((2, pairs, width)), shape((pairs, width)), shape((pairs, width))],
        (where, own, mate, pair_own, pair_mate),
        [SMEM] + [VMEM] * 4,
        (16 * pairs * width * width, 1 * MIB),
    )


def staged(where, cols, coupling, pair_alpha_t, beta_ops, tie):
    pairs, width = coupling.shape[0], beta_ops.shape[0]
    listed = beta_ops.shape[1] // width
    count = lax.axis_size(BETA)

    def staged_kernel(
        where_ref, cols_ref, c_ref, pa_ref, ops_ref, tie_ref, c_out, pa_out, w_out, pa_v, ops_v, sems
    ):
        rows = block_rows(where_ref, 0, width)
        copies = [
            pltpu.make_async_copy(ops_ref, ops_v, sems.at[0]),
            pltpu.make_async_copy(pa_ref.at[:, rows], pa_v, sems.at[1]),
            pltpu.make_async_copy(c_ref, c_out, sems.at[2]),
        ]
        for copy in copies:
            copy.start()
        copies[0].wait()
        core = where_ref[8]
        for n in range(5):
            side = 2 - where_ref[11] if n in (0, 4) else 2 * core
            offset = jnp.where(side == 0, n, 4 - n)
            tile = jnp.zeros((width, width), F32)
            for k in range(listed):
                here = lax.rem(cols_ref[0, k] - where_ref[9] + 2 + count, count)
                part = ops_v[:, k * width : (k + 1) * width].astype(F32)
                tile = jnp.where(here == offset, part, tile)
            w_out[:, n * width : (n + 1) * width] = tile.astype(BF16)
        copies[1].wait()
        pa_out[...] = pa_v[...].astype(F32).T
        copies[2].wait()

    return call(
        staged_kernel,
        [shape(coupling.shape), shape((width, pairs), F32), shape((width, 5 * width))],
        (where, cols, coupling, pair_alpha_t, beta_ops, tie),
        [SMEM, SMEM, HBM, HBM, HBM, ANY],
        (pairs * pairs, 2 * MIB),
        [
            pltpu.VMEM((pairs, width), BF16),
            pltpu.VMEM(beta_ops.shape, BF16),
            pltpu.SemaphoreType.DMA((3,)),
        ],
    )


def excited_block(near, far, coupling, scale):
    pairs, width = near.shape

    def excited_block_kernel(near_ref, far_ref, coupling_ref, scale_ref, out_ref):
        total = near_ref[...].astype(F32) + far_ref[...].astype(F32)
        density = total.T.astype(BF16)
        out_ref[...] = (dot(density, coupling_ref[...]) * scale_ref[...]).astype(BF16)

    return call(
        excited_block_kernel,
        [shape((width, pairs))],
        (near, far, coupling, scale),
        [VMEM] * 4,
        (2 * pairs * pairs * width, 2 * MIB),
    )[0]


def mixed_mate(blocks, pair_mate):
    width = blocks[0].shape[0]
    pairs = blocks[0].shape[1]

    def mixed_mate_kernel(*refs):
        right = refs[4][...]
        for k in range(4):
            refs[5][k] = dot(refs[k][...], right).astype(BF16)

    return call(
        mixed_mate_kernel,
        [shape((4, width, width))],
        (*blocks, pair_mate),
        [VMEM] * 5,
        (8 * pairs * width * width, 1 * MIB),
    )[0]


def finished_own(where, same, blocks, pair_own, denominators):
    rows, width = same.shape

    def finished_own_kernel(where_ref, same_ref, e0, e1, e2, e3, pair_ref, den_ref, out, part, sems):
        right = pair_ref[...]
        copies = []
        for k, block in enumerate((e0, e1, e2, e3)):
            at = block_rows(where_ref, k, width)
            part[k] = (same_ref[at, :] + dot(block[...], right)) / den_ref[at, :]
            copies.append(pltpu.make_async_copy(part.at[k], out.at[at, :], sems.at[k]))
            copies[-1].start()
        for copy in copies:
            copy.wait()

    return call(
        finished_own_kernel,
        [shape((rows, width), F32)],
        (where, same, *blocks, pair_own, denominators),
        [SMEM] + [VMEM] * 7,
        (rows * width * 600, 2 * MIB),
        [pltpu.VMEM((4, width, width), F32), pltpu.SemaphoreType.DMA((4,))],
        out_specs=[HBM],
    )[0]


def finished_mate(where, same, theirs, denominators, begun):
    rows, width = same.shape

    def finished_mate_kernel(where_ref, same_ref, theirs_ref, den_ref, begun_ref, out, part, sems):
        copies = []
        for k in range(4):
            at = block_rows(where_ref, 4 + k, width)
            part[k] = (same_ref[at, :] + theirs_ref[k].astype(F32)) / den_ref[at, :]
            copies.append(pltpu.make_async_copy(part.at[k], out.at[at, :], sems.at[k]))
            copies[-1].start()
        for copy in copies:
            copy.wait()

    return call(
        finished_mate_kernel,
        [shape((rows, width), F32)],
        (where, same, theirs, denominators, begun),
        [SMEM] + [VMEM] * 3 + [ANY],
        (rows * width * 2, 2 * MIB),
        [pltpu.VMEM((4, width, width), F32), pltpu.SemaphoreType.DMA((4,))],
        aliases={4: 0},
        out_specs=[HBM],
    )[0]


def same_spin_beta(blocks, placed):
    rows, width = blocks[0].shape

    def same_spin_beta_kernel(b0, b1, b2, b3, b4, w_ref, out_ref):
        left = jnp.concatenate([b[...] for b in (b0, b1, b2, b3, b4)], axis=1)
        out_ref[...] = dot(left, w_ref[...], ((1,), (1,)))

    return call(
        same_spin_beta_kernel,
        [shape((rows, width), F32)],
        (*blocks, placed),
        [VMEM] * 6,
        (2 * rows * width * width * 5, 2 * MIB),
        limit=24,
    )[0]


def same_spin_alpha(where, cols, blocks, alpha_ops, start):
    rows, width = start.shape
    depth = blocks[0].shape[0]
    span = alpha_ops.shape[1]
    step = 256
    count = lax.axis_size(ALPHA)

    def same_spin_alpha_kernel(
        where_ref, cols_ref, own_ref, near_ref, far_ref, ops_ref, start_ref, out_ref, ops_v, picked, sems
    ):
        copies = [
            pltpu.make_async_copy(ops_ref.at[r : r + step, :], ops_v.at[r : r + step, :], sems.at[n])
            for n, r in enumerate(range(0, rows, step))
        ]
        for copy in copies:
            copy.start()
        for k in range(span // depth):
            offset = lax.rem(cols_ref[0, k] - where_ref[10] + 1 + count, count)
            picked[k * depth : (k + 1) * depth, :] = jnp.where(
                offset == 1,
                own_ref[...],
                jnp.where(offset == where_ref[11], near_ref[...], far_ref[...]),
            )
        for copy, r in zip(copies, range(0, rows, step)):
            copy.wait()
            at = slice(r, r + step)
            out_ref[at, :] = start_ref[at, :] + dot(ops_v[at, :], picked[...])

    return call(
        same_spin_alpha_kernel,
        [shape((rows, width), F32)],
        (where, cols, *blocks, alpha_ops, start),
        [SMEM, SMEM] + [VMEM] * 3 + [HBM, VMEM],
        (2 * rows * width * depth * 4, 10 * MIB),
        [
            pltpu.VMEM((rows, span), BF16),
            pltpu.VMEM((span, width), BF16),
            pltpu.SemaphoreType.DMA((rows // step,)),
        ],
        limit=24,
    )[0]


def local(
    coef,
    beta_ops,
    beta_cols,
    alpha_ops,
    alpha_cols,
    pair_alpha,
    pair_beta,
    pair_coupling,
    denominators,
):
    y, core = lax.axis_index("y"), lax.axis_index("c")
    low = lax.axis_index("zl")
    row_blocks = [(y ^ k) * 2 for k in range(4)]
    where = [r + core for r in row_blocks] + [r + 1 - core for r in row_blocks]
    where += [core, lax.axis_index(BETA), lax.axis_index(ALPHA), 2 - 2 * low]
    side = 1 + 2 * core
    where += [(y ^ m) * 2 + core for m in (side, 2, 0, 4 - side)]
    where = jnp.stack(where).astype(jnp.int32)

    pair_t = pair_beta.T
    mate = swapped(coef, "c", 1)
    pair_mate = swapped(pair_t, "c", 1)
    coef_v, pair_v = loaded(coef, pair_t)

    near = swapped(coef_v, "zl", 1)
    chips = lax.axis_size("y") * lax.axis_size("zh")
    border = []
    for q in range(chips):
        for h in (0, 1):
            low_at, high_at = (2 * q + h, 2 * chips + 2 * ((q - 1) % chips) + h)
            border += [(low_at, high_at), (high_at, low_at)]
    over = ("zl", *BETA)
    across = lax.ppermute(coef_v, over, border)
    xs, route = lax.axis_size("x"), []
    for i in range(xs):
        route += [(2 * i, 2 * ((i + 1) % xs)), (2 * i + 1, 2 * ((i - 1) % xs) + 1)]

    sent, kept, passing = density_parts(where, coef_v, mate, pair_v, pair_mate)
    coupling, scale, placed = staged(
        where, beta_cols, pair_coupling, pair_alpha.T, beta_ops, kept
    )
    arrived = lax.ppermute(sent, ("y", "c"), crossing(4, (1, 3)))
    arrived, _, _ = lax.optimization_barrier((arrived, near, across))
    passing = (passing.astype(F32) + arrived[1].astype(F32)).astype(BF16)
    total = kept.astype(F32) + arrived[0].astype(F32)
    total = total + lax.ppermute(passing, ("y", "c"), crossing(4, (3, 1))).astype(F32)
    total = total.astype(BF16)
    onward = lax.ppermute(near, over, border)
    returned = swapped(across, "zl", 1)
    total, coupling, scale, placed = lax.optimization_barrier((total, coupling, scale, placed))

    far = lax.ppermute(near, ALPHA, route)
    first = lax.ppermute(total, ("zh", "c"), crossing(4, (1, 3)))
    total = (total.astype(F32) + first.astype(F32)).astype(BF16)
    passed = jnp.where(core == low, returned, onward)
    total, passed = lax.optimization_barrier((total, passed))
    crossed = swapped(passed, "c", 1)
    second = lax.ppermute(total, ("zh", "c"), crossing(4, (3, 1)))
    same = same_spin_beta([onward, crossed, coef_v, mate, returned], placed)
    second, same = lax.optimization_barrier((second, same))

    excited = excited_block(total, second, coupling, scale)
    blocks = [excited] + [swapped(excited, "y", k) for k in (1, 2, 3)]
    same = same_spin_alpha(where, alpha_cols, [coef_v, near, far], alpha_ops, same)
    *blocks, same = lax.optimization_barrier((*blocks, same))

    theirs = mixed_mate(blocks, pair_mate)
    begun = finished_own(where, same, blocks, pair_v, denominators)
    return finished_mate(where, same, swapped(theirs, "c", 1), denominators, begun)


def solution(mesh):
    finer = Mesh(mesh.devices.reshape(4, 2, 4, 4, 2), (*ALPHA, *BETA))
    placed = (
        P(ALPHA, BETA),
        P(BETA, None),
        P(BETA, None),
        P(ALPHA, None),
        P(ALPHA, None),
        P(ALPHA, None),
        P(BETA, None),
        P(),
        P(ALPHA, BETA),
    )
    return jax.shard_map(
        local, mesh=finer, in_specs=placed, out_specs=P(ALPHA, BETA), check_vma=False
    )
```

```python
import jax
import jax.numpy as jnp
from jax import lax
from jax.experimental import pallas as pl
from jax.experimental.pallas import tpu as pltpu
from jax.sharding import Mesh
from jax.sharding import PartitionSpec as P

ALPHA = ("x", "zl")
BETA = ("y", "zh", "c")
F32 = jnp.float32
BF16 = jnp.bfloat16
SMEM = pl.BlockSpec(memory_space=pltpu.SMEM)
VMEM = pl.BlockSpec(memory_space=pltpu.VMEM)
HBM = pl.BlockSpec(memory_space=pltpu.HBM)
ANY = pl.BlockSpec(memory_space=pl.ANY)
MIB = 1 << 20


def dot(a, b, dims=((1,), (0,))):
    return lax.dot_general(a, b, (dims, ((), ())), preferred_element_type=F32)


def swapped(block, axis, mask):
    count = lax.axis_size(axis)
    return lax.ppermute(block, axis, [(i, i ^ mask) for i in range(count)])


def crossing(count, masks):
    return [(2 * i + h, 2 * (i ^ masks[h]) + h) for i in range(count) for h in (0, 1)]


def call(kernel, outs, args, specs, cost, scratch=(), aliases=None, out_specs=None, limit=16):
    args = [
        pltpu.with_memory_space_constraint(arg, pltpu.HBM) if spec is HBM else arg
        for arg, spec in zip(args, specs)
    ]
    return pl.pallas_call(
        kernel,
        out_shape=outs,
        in_specs=specs,
        out_specs=out_specs or [VMEM] * len(outs),
        scratch_shapes=list(scratch),
        input_output_aliases=aliases or {},
        compiler_params=pltpu.CompilerParams(vmem_limit_bytes=limit * MIB),
        cost_estimate=pl.CostEstimate(flops=cost[0], bytes_accessed=cost[1], transcendentals=0),
        name=kernel.__name__,
    )(*args)


def shape(dims, kind=BF16):
    return jax.ShapeDtypeStruct(dims, kind)


def block_rows(where_ref, k, width):
    return pl.ds(pl.multiple_of(where_ref[k] * width, width), width)


def loaded(coef, pair_t):
    def loaded_kernel(coef_ref, pair_ref, coef_out, pair_out, sems):
        copies = [
            pltpu.make_async_copy(coef_ref, coef_out, sems.at[0]),
            pltpu.make_async_copy(pair_ref, pair_out, sems.at[1]),
        ]
        for copy in copies:
            copy.start()
        for copy in copies:
            copy.wait()

    return call(
        loaded_kernel,
        [shape(coef.shape), shape(pair_t.shape)],
        (coef, pair_t),
        [HBM, HBM],
        (0, 1 * MIB),
        [pltpu.SemaphoreType.DMA((2,))],
    )


def density_parts(where, own, mate, pair_own, pair_mate):
    pairs, width = pair_mate.shape

    def density_parts_kernel(where_ref, own_ref, mate_ref, po_ref, pm_ref, sent, kept, passing):
        left = jnp.concatenate([po_ref[...], pm_ref[...]], axis=1)
        for k in range(4):
            rows = block_rows(where_ref, 12 + k, width)
            right = jnp.concatenate([own_ref[rows, :], mate_ref[rows, :]], axis=1)
            part = dot(left, right, ((1,), (1,))).astype(BF16)
            if k < 2:
                sent[k] = part
            else:
                (kept, passing)[k - 2][...] = part

    return call(
        density_parts_kernel,
        [shape((2, pairs, width)), shape((pairs, width)), shape((pairs, width))],
        (where, own, mate, pair_own, pair_mate),
        [SMEM] + [VMEM] * 4,
        (16 * pairs * width * width, 1 * MIB),
    )


def staged(where, cols, coupling, pair_alpha_t, beta_ops, tie):
    pairs, width = coupling.shape[0], beta_ops.shape[0]
    listed = beta_ops.shape[1] // width
    count = lax.axis_size(BETA)

    def staged_kernel(
        where_ref, cols_ref, c_ref, pa_ref, ops_ref, tie_ref, c_out, pa_out, w_out, pa_v, ops_v, sems
    ):
        rows = block_rows(where_ref, 0, width)
        copies = [
            pltpu.make_async_copy(ops_ref, ops_v, sems.at[0]),
            pltpu.make_async_copy(pa_ref.at[:, rows], pa_v, sems.at[1]),
            pltpu.make_async_copy(c_ref, c_out, sems.at[2]),
        ]
        for copy in copies:
            copy.start()
        copies[0].wait()
        core = where_ref[8]
        for n in range(5):
            side = 2 - where_ref[11] if n in (0, 4) else 2 * core
            offset = jnp.where(side == 0, n, 4 - n)
            tile = jnp.zeros((width, width), F32)
            for k in range(listed):
                here = lax.rem(cols_ref[0, k] - where_ref[9] + 2 + count, count)
                part = ops_v[:, k * width : (k + 1) * width].astype(F32)
                tile = jnp.where(here == offset, part, tile)
            w_out[:, n * width : (n + 1) * width] = tile.astype(BF16)
        copies[1].wait()
        pa_out[...] = pa_v[...].astype(F32).T
        copies[2].wait()

    return call(
        staged_kernel,
        [shape(coupling.shape), shape((width, pairs), F32), shape((width, 5 * width))],
        (where, cols, coupling, pair_alpha_t, beta_ops, tie),
        [SMEM, SMEM, HBM, HBM, HBM, ANY],
        (pairs * pairs, 2 * MIB),
        [
            pltpu.VMEM((pairs, width), BF16),
            pltpu.VMEM(beta_ops.shape, BF16),
            pltpu.SemaphoreType.DMA((3,)),
        ],
    )


def excited_block(near, far, coupling, scale):
    pairs, width = near.shape

    def excited_block_kernel(near_ref, far_ref, coupling_ref, scale_ref, out_ref):
        total = near_ref[...].astype(F32) + far_ref[...].astype(F32)
        density = total.T.astype(BF16)
        out_ref[...] = (dot(density, coupling_ref[...]) * scale_ref[...]).astype(BF16)

    return call(
        excited_block_kernel,
        [shape((width, pairs))],
        (near, far, coupling, scale),
        [VMEM] * 4,
        (2 * pairs * pairs * width, 2 * MIB),
    )[0]


def mixed_mate(blocks, pair_mate):
    width = blocks[0].shape[0]
    pairs = blocks[0].shape[1]

    def mixed_mate_kernel(*refs):
        right = refs[4][...]
        for k in range(4):
            refs[5][k] = dot(refs[k][...], right).astype(BF16)

    return call(
        mixed_mate_kernel,
        [shape((4, width, width))],
        (*blocks, pair_mate),
        [VMEM] * 5,
        (8 * pairs * width * width, 1 * MIB),
    )[0]


def finished_own(where, same, blocks, pair_own, denominators):
    rows, width = same.shape

    def finished_own_kernel(where_ref, same_ref, e0, e1, e2, e3, pair_ref, den_ref, out, part, sems):
        right = pair_ref[...]
        copies = []
        for k, block in enumerate((e0, e1, e2, e3)):
            at = block_rows(where_ref, k, width)
            part[k] = (same_ref[at, :] + dot(block[...], right)) / den_ref[at, :]
            copies.append(pltpu.make_async_copy(part.at[k], out.at[at, :], sems.at[k]))
            copies[-1].start()
        for copy in copies:
            copy.wait()

    return call(
        finished_own_kernel,
        [shape((rows, width), F32)],
        (where, same, *blocks, pair_own, denominators),
        [SMEM] + [VMEM] * 7,
        (rows * width * 600, 2 * MIB),
        [pltpu.VMEM((4, width, width), F32), pltpu.SemaphoreType.DMA((4,))],
        out_specs=[HBM],
    )[0]


def finished_mate(where, same, theirs, denominators, begun):
    rows, width = same.shape

    def finished_mate_kernel(where_ref, same_ref, theirs_ref, den_ref, begun_ref, out, part, sems):
        copies = []
        for k in range(4):
            at = block_rows(where_ref, 4 + k, width)
            part[k] = (same_ref[at, :] + theirs_ref[k].astype(F32)) / den_ref[at, :]
            copies.append(pltpu.make_async_copy(part.at[k], out.at[at, :], sems.at[k]))
            copies[-1].start()
        for copy in copies:
            copy.wait()

    return call(
        finished_mate_kernel,
        [shape((rows, width), F32)],
        (where, same, theirs, denominators, begun),
        [SMEM] + [VMEM] * 3 + [ANY],
        (rows * width * 2, 2 * MIB),
        [pltpu.VMEM((4, width, width), F32), pltpu.SemaphoreType.DMA((4,))],
        aliases={4: 0},
        out_specs=[HBM],
    )[0]


def same_spin_beta(blocks, placed):
    rows, width = blocks[0].shape

    def same_spin_beta_kernel(b0, b1, b2, b3, b4, w_ref, out_ref):
        left = jnp.concatenate([b[...] for b in (b0, b1, b2, b3, b4)], axis=1)
        out_ref[...] = dot(left, w_ref[...], ((1,), (1,)))

    return call(
        same_spin_beta_kernel,
        [shape((rows, width), F32)],
        (*blocks, placed),
        [VMEM] * 6,
        (2 * rows * width * width * 5, 2 * MIB),
        limit=24,
    )[0]


def same_spin_alpha(where, cols, blocks, alpha_ops, start):
    rows, width = start.shape
    depth = blocks[0].shape[0]
    span = alpha_ops.shape[1]
    step = 256
    count = lax.axis_size(ALPHA)

    def same_spin_alpha_kernel(
        where_ref, cols_ref, own_ref, near_ref, far_ref, ops_ref, start_ref, out_ref, ops_v, picked, sems
    ):
        copies = [
            pltpu.make_async_copy(ops_ref.at[r : r + step, :], ops_v.at[r : r + step, :], sems.at[n])
            for n, r in enumerate(range(0, rows, step))
        ]
        for copy in copies:
            copy.start()
        for k in range(span // depth):
            offset = lax.rem(cols_ref[0, k] - where_ref[10] + 1 + count, count)
            picked[k * depth : (k + 1) * depth, :] = jnp.where(
                offset == 1,
                own_ref[...],
                jnp.where(offset == where_ref[11], near_ref[...], far_ref[...]),
            )
        for copy, r in zip(copies, range(0, rows, step)):
            copy.wait()
            at = slice(r, r + step)
            out_ref[at, :] = start_ref[at, :] + dot(ops_v[at, :], picked[...])

    return call(
        same_spin_alpha_kernel,
        [shape((rows, width), F32)],
        (where, cols, *blocks, alpha_ops, start),
        [SMEM, SMEM] + [VMEM] * 3 + [HBM, VMEM],
        (2 * rows * width * depth * 4, 10 * MIB),
        [
            pltpu.VMEM((rows, span), BF16),
            pltpu.VMEM((span, width), BF16),
            pltpu.SemaphoreType.DMA((rows // step,)),
        ],
        limit=24,
    )[0]


def local(
    coef,
    beta_ops,
    beta_cols,
    alpha_ops,
    alpha_cols,
    pair_alpha,
    pair_beta,
    pair_coupling,
    denominators,
):
    y, core = lax.axis_index("y"), lax.axis_index("c")
    low = lax.axis_index("zl")
    row_blocks = [(y ^ k) * 2 for k in range(4)]
    where = [r + core for r in row_blocks] + [r + 1 - core for r in row_blocks]
    where += [core, lax.axis_index(BETA), lax.axis_index(ALPHA), 2 - 2 * low]
    side = 1 + 2 * core
    where += [(y ^ m) * 2 + core for m in (side, 2, 0, 4 - side)]
    where = jnp.stack(where).astype(jnp.int32)

    pair_t = pair_beta.T
    mate = swapped(coef, "c", 1)
    pair_mate = swapped(pair_t, "c", 1)
    coef_v, pair_v = loaded(coef, pair_t)

    near = swapped(coef_v, "zl", 1)
    chips = lax.axis_size("y") * lax.axis_size("zh")
    border = []
    for q in range(chips):
        for h in (0, 1):
            low_at, high_at = (2 * q + h, 2 * chips + 2 * ((q - 1) % chips) + h)
            border += [(low_at, high_at), (high_at, low_at)]
    over = ("zl", *BETA)
    across = lax.ppermute(coef_v, over, border)
    xs, route = lax.axis_size("x"), []
    for i in range(xs):
        route += [(2 * i, 2 * ((i + 1) % xs)), (2 * i + 1, 2 * ((i - 1) % xs) + 1)]

    sent, kept, passing = density_parts(where, coef_v, mate, pair_v, pair_mate)
    coupling, scale, placed = staged(
        where, beta_cols, pair_coupling, pair_alpha.T, beta_ops, kept
    )
    arrived = lax.ppermute(sent, ("y", "c"), crossing(4, (1, 3)))
    arrived, coupling, scale, placed = lax.optimization_barrier(
        (arrived, coupling, scale, placed)
    )
    passing = (passing.astype(F32) + arrived[1].astype(F32)).astype(BF16)
    total = kept.astype(F32) + arrived[0].astype(F32)
    passed = lax.ppermute(passing, ("y", "c"), crossing(4, (3, 1)))
    passed, _, _ = lax.optimization_barrier((passed, near, across))
    total = (total + passed.astype(F32)).astype(BF16)
    onward = lax.ppermute(near, over, border)
    returned = swapped(across, "zl", 1)

    far = lax.ppermute(near, ALPHA, route)
    first = lax.ppermute(total, ("zh", "c"), crossing(4, (1, 3)))
    total = (total.astype(F32) + first.astype(F32)).astype(BF16)
    passed = jnp.where(core == low, returned, onward)
    total, passed = lax.optimization_barrier((total, passed))
    crossed = swapped(passed, "c", 1)
    second = lax.ppermute(total, ("zh", "c"), crossing(4, (3, 1)))
    same = same_spin_beta([onward, crossed, coef_v, mate, returned], placed)
    second, same = lax.optimization_barrier((second, same))

    excited = excited_block(total, second, coupling, scale)
    blocks = [excited] + [swapped(excited, "y", k) for k in (1, 2, 3)]
    same = same_spin_alpha(where, alpha_cols, [coef_v, near, far], alpha_ops, same)
    *blocks, same = lax.optimization_barrier((*blocks, same))

    theirs = mixed_mate(blocks, pair_mate)
    begun = finished_own(where, same, blocks, pair_v, denominators)
    return finished_mate(where, same, swapped(theirs, "c", 1), denominators, begun)


def solution(mesh):
    finer = Mesh(mesh.devices.reshape(4, 2, 4, 4, 2), (*ALPHA, *BETA))
    placed = (
        P(ALPHA, BETA),
        P(BETA, None),
        P(BETA, None),
        P(ALPHA, None),
        P(ALPHA, None),
        P(ALPHA, None),
        P(BETA, None),
        P(),
        P(ALPHA, BETA),
    )
    return jax.shard_map(
        local, mesh=finer, in_specs=placed, out_specs=P(ALPHA, BETA), check_vma=False
    )
```

```python
import jax
import jax.numpy as jnp
from jax import lax
from jax.experimental import pallas as pl
from jax.experimental.pallas import tpu as pltpu
from jax.sharding import Mesh
from jax.sharding import PartitionSpec as P

ALPHA = ("x", "zl")
BETA = ("y", "zh", "c")
F32 = jnp.float32
BF16 = jnp.bfloat16
SMEM = pl.BlockSpec(memory_space=pltpu.SMEM)
VMEM = pl.BlockSpec(memory_space=pltpu.VMEM)
HBM = pl.BlockSpec(memory_space=pltpu.HBM)
ANY = pl.BlockSpec(memory_space=pl.ANY)
MIB = 1 << 20


def dot(a, b, dims=((1,), (0,))):
    return lax.dot_general(a, b, (dims, ((), ())), preferred_element_type=F32)


def swapped(block, axis, mask):
    count = lax.axis_size(axis)
    return lax.ppermute(block, axis, [(i, i ^ mask) for i in range(count)])


def rotated(block, axis, distance):
    count = lax.axis_size(axis)
    return lax.ppermute(block, axis, [(i, (i + distance) % count) for i in range(count)])


def crossing(count, masks):
    return [(2 * i + h, 2 * (i ^ masks[h]) + h) for i in range(count) for h in (0, 1)]


def call(kernel, outs, args, specs, cost, scratch=(), aliases=None, out_specs=None, limit=16):
    args = [
        pltpu.with_memory_space_constraint(arg, pltpu.HBM) if spec is HBM else arg
        for arg, spec in zip(args, specs)
    ]
    return pl.pallas_call(
        kernel,
        out_shape=outs,
        in_specs=specs,
        out_specs=out_specs or [VMEM] * len(outs),
        scratch_shapes=list(scratch),
        input_output_aliases=aliases or {},
        compiler_params=pltpu.CompilerParams(vmem_limit_bytes=limit * MIB),
        cost_estimate=pl.CostEstimate(flops=cost[0], bytes_accessed=cost[1], transcendentals=0),
        name=kernel.__name__,
    )(*args)


def shape(dims, kind=BF16):
    return jax.ShapeDtypeStruct(dims, kind)


def block_rows(where_ref, k, width):
    return pl.ds(pl.multiple_of(where_ref[k] * width, width), width)


def loaded(coef, pair_t):
    def loaded_kernel(coef_ref, pair_ref, coef_out, pair_out, sems):
        copies = [
            pltpu.make_async_copy(coef_ref, coef_out, sems.at[0]),
            pltpu.make_async_copy(pair_ref, pair_out, sems.at[1]),
        ]
        for copy in copies:
            copy.start()
        for copy in copies:
            copy.wait()

    return call(
        loaded_kernel,
        [shape(coef.shape), shape(pair_t.shape)],
        (coef, pair_t),
        [HBM, HBM],
        (0, 1 * MIB),
        [pltpu.SemaphoreType.DMA((2,))],
    )


def density_parts(where, own, mate, pair_own, pair_mate):
    pairs, width = pair_mate.shape

    def density_parts_kernel(where_ref, own_ref, mate_ref, po_ref, pm_ref, sent, kept, passing):
        left = jnp.concatenate([po_ref[...], pm_ref[...]], axis=1)
        for k in range(4):
            rows = block_rows(where_ref, 12 + k, width)
            right = jnp.concatenate([own_ref[rows, :], mate_ref[rows, :]], axis=1)
            part = dot(left, right, ((1,), (1,))).astype(BF16)
            if k < 2:
                sent[k] = part
            else:
                (kept, passing)[k - 2][...] = part

    return call(
        density_parts_kernel,
        [shape((2, pairs, width)), shape((pairs, width)), shape((pairs, width))],
        (where, own, mate, pair_own, pair_mate),
        [SMEM] + [VMEM] * 4,
        (16 * pairs * width * width, 1 * MIB),
    )


def staged(where, cols, coupling, pair_alpha_t, beta_ops, tie):
    pairs, width = coupling.shape[0], beta_ops.shape[0]
    listed = beta_ops.shape[1] // width
    count = lax.axis_size(BETA)

    def staged_kernel(
        where_ref, cols_ref, c_ref, pa_ref, ops_ref, tie_ref, c_out, pa_out, w_out, pa_v, ops_v, sems
    ):
        rows = block_rows(where_ref, 0, width)
        copies = [
            pltpu.make_async_copy(ops_ref, ops_v, sems.at[0]),
            pltpu.make_async_copy(pa_ref.at[:, rows], pa_v, sems.at[1]),
            pltpu.make_async_copy(c_ref, c_out, sems.at[2]),
        ]
        for copy in copies:
            copy.start()
        copies[0].wait()
        core = where_ref[8]
        for n in range(5):
            offset = n if n in (0, 2, 4) else jnp.where(core == 0, n, 4 - n)
            tile = jnp.zeros((width, width), F32)
            for k in range(listed):
                here = lax.rem(cols_ref[0, k] - where_ref[9] + 2 + count, count)
                part = ops_v[:, k * width : (k + 1) * width].astype(F32)
                tile = jnp.where(here == offset, part, tile)
            w_out[:, n * width : (n + 1) * width] = tile.astype(BF16)
        copies[1].wait()
        pa_out[...] = pa_v[...].astype(F32).T
        copies[2].wait()

    return call(
        staged_kernel,
        [shape(coupling.shape), shape((width, pairs), F32), shape((width, 5 * width))],
        (where, cols, coupling, pair_alpha_t, beta_ops, tie),
        [SMEM, SMEM, HBM, HBM, HBM, ANY],
        (pairs * pairs, 2 * MIB),
        [
            pltpu.VMEM((pairs, width), BF16),
            pltpu.VMEM(beta_ops.shape, BF16),
            pltpu.SemaphoreType.DMA((3,)),
        ],
    )


def excited_block(near, far, coupling, scale):
    pairs, width = near.shape

    def excited_block_kernel(near_ref, far_ref, coupling_ref, scale_ref, out_ref):
        total = near_ref[...].astype(F32) + far_ref[...].astype(F32)
        density = total.T.astype(BF16)
        out_ref[...] = (dot(density, coupling_ref[...]) * scale_ref[...]).astype(BF16)

    return call(
        excited_block_kernel,
        [shape((width, pairs))],
        (near, far, coupling, scale),
        [VMEM] * 4,
        (2 * pairs * pairs * width, 2 * MIB),
    )[0]


def mixed_mate(blocks, pair_mate):
    width = blocks[0].shape[0]
    pairs = blocks[0].shape[1]

    def mixed_mate_kernel(*refs):
        right = refs[4][...]
        for k in range(4):
            refs[5][k] = dot(refs[k][...], right).astype(BF16)

    return call(
        mixed_mate_kernel,
        [shape((4, width, width))],
        (*blocks, pair_mate),
        [VMEM] * 5,
        (8 * pairs * width * width, 1 * MIB),
    )[0]


def finished_own(where, same, blocks, pair_own, denominators):
    rows, width = same.shape

    def finished_own_kernel(where_ref, same_ref, e0, e1, e2, e3, pair_ref, den_ref, out, part, sems):
        right = pair_ref[...]
        copies = []
        for k, block in enumerate((e0, e1, e2, e3)):
            at = block_rows(where_ref, k, width)
            part[k] = (same_ref[at, :] + dot(block[...], right)) / den_ref[at, :]
            copies.append(pltpu.make_async_copy(part.at[k], out.at[at, :], sems.at[k]))
            copies[-1].start()
        for copy in copies:
            copy.wait()

    return call(
        finished_own_kernel,
        [shape((rows, width), F32)],
        (where, same, *blocks, pair_own, denominators),
        [SMEM] + [VMEM] * 7,
        (rows * width * 600, 2 * MIB),
        [pltpu.VMEM((4, width, width), F32), pltpu.SemaphoreType.DMA((4,))],
        out_specs=[HBM],
    )[0]


def finished_mate(where, same, theirs, denominators, begun):
    rows, width = same.shape

    def finished_mate_kernel(where_ref, same_ref, theirs_ref, den_ref, begun_ref, out, part, sems):
        copies = []
        for k in range(4):
            at = block_rows(where_ref, 4 + k, width)
            part[k] = (same_ref[at, :] + theirs_ref[k].astype(F32)) / den_ref[at, :]
            copies.append(pltpu.make_async_copy(part.at[k], out.at[at, :], sems.at[k]))
            copies[-1].start()
        for copy in copies:
            copy.wait()

    return call(
        finished_mate_kernel,
        [shape((rows, width), F32)],
        (where, same, theirs, denominators, begun),
        [SMEM] + [VMEM] * 3 + [ANY],
        (rows * width * 2, 2 * MIB),
        [pltpu.VMEM((4, width, width), F32), pltpu.SemaphoreType.DMA((4,))],
        aliases={4: 0},
        out_specs=[HBM],
    )[0]


def same_spin_beta(blocks, placed):
    rows, width = blocks[0].shape

    def same_spin_beta_kernel(b0, b1, b2, b3, b4, w_ref, out_ref):
        left = jnp.concatenate([b[...] for b in (b0, b1, b2, b3, b4)], axis=1)
        out_ref[...] = dot(left, w_ref[...], ((1,), (1,)))

    return call(
        same_spin_beta_kernel,
        [shape((rows, width), F32)],
        (*blocks, placed),
        [VMEM] * 6,
        (2 * rows * width * width * 5, 2 * MIB),
        limit=24,
    )[0]


def same_spin_alpha(where, cols, blocks, alpha_ops, start):
    rows, width = start.shape
    depth = blocks[0].shape[0]
    span = alpha_ops.shape[1]
    step = 256
    count = lax.axis_size(ALPHA)

    def same_spin_alpha_kernel(
        where_ref, cols_ref, own_ref, near_ref, far_ref, ops_ref, start_ref, out_ref, ops_v, picked, sems
    ):
        copies = [
            pltpu.make_async_copy(ops_ref.at[r : r + step, :], ops_v.at[r : r + step, :], sems.at[n])
            for n, r in enumerate(range(0, rows, step))
        ]
        for copy in copies:
            copy.start()
        for k in range(span // depth):
            offset = lax.rem(cols_ref[0, k] - where_ref[10] + 1 + count, count)
            picked[k * depth : (k + 1) * depth, :] = jnp.where(
                offset == 1,
                own_ref[...],
                jnp.where(offset == where_ref[11], near_ref[...], far_ref[...]),
            )
        for copy, r in zip(copies, range(0, rows, step)):
            copy.wait()
            at = slice(r, r + step)
            out_ref[at, :] = start_ref[at, :] + dot(ops_v[at, :], picked[...])

    return call(
        same_spin_alpha_kernel,
        [shape((rows, width), F32)],
        (where, cols, *blocks, alpha_ops, start),
        [SMEM, SMEM] + [VMEM] * 3 + [HBM, VMEM],
        (2 * rows * width * depth * 4, 10 * MIB),
        [
            pltpu.VMEM((rows, span), BF16),
            pltpu.VMEM((span, width), BF16),
            pltpu.SemaphoreType.DMA((rows // step,)),
        ],
        limit=24,
    )[0]


def local(
    coef,
    beta_ops,
    beta_cols,
    alpha_ops,
    alpha_cols,
    pair_alpha,
    pair_beta,
    pair_coupling,
    denominators,
):
    y, core = lax.axis_index("y"), lax.axis_index("c")
    low = lax.axis_index("zl")
    row_blocks = [(y ^ k) * 2 for k in range(4)]
    where = [r + core for r in row_blocks] + [r + 1 - core for r in row_blocks]
    where += [core, lax.axis_index(BETA), lax.axis_index(ALPHA), 2 - 2 * low]
    side = 1 + 2 * core
    where += [(y ^ m) * 2 + core for m in (side, 2, 0, 4 - side)]
    where = jnp.stack(where).astype(jnp.int32)

    pair_t = pair_beta.T
    mate = swapped(coef, "c", 1)
    pair_mate = swapped(pair_t, "c", 1)
    coef_v, pair_v = loaded(coef, pair_t)

    near = swapped(coef_v, "zl", 1)
    below = rotated(coef_v, BETA, 2)
    above = rotated(coef_v, BETA, -2)
    xs, route = lax.axis_size("x"), []
    for i in range(xs):
        route += [(2 * i, 2 * ((i + 1) % xs)), (2 * i + 1, 2 * ((i - 1) % xs) + 1)]

    sent, kept, passing = density_parts(where, coef_v, mate, pair_v, pair_mate)
    coupling, scale, placed = staged(
        where, beta_cols, pair_coupling, pair_alpha.T, beta_ops, kept
    )
    arrived = lax.ppermute(sent, ("y", "c"), crossing(4, (1, 3)))
    arrived, coupling, scale, placed = lax.optimization_barrier(
        (arrived, coupling, scale, placed)
    )
    passing = (passing.astype(F32) + arrived[1].astype(F32)).astype(BF16)
    total = kept.astype(F32) + arrived[0].astype(F32)
    passed = lax.ppermute(passing, ("y", "c"), crossing(4, (3, 1)))
    total = (total + passed.astype(F32)).astype(BF16)

    far = lax.ppermute(near, ALPHA, route)
    first = lax.ppermute(total, ("zh", "c"), crossing(4, (1, 3)))
    crossed = swapped(jnp.where(core == 0, above, below), "c", 1)
    first, crossed = lax.optimization_barrier((first, crossed))
    total = (total.astype(F32) + first.astype(F32)).astype(BF16)
    second = lax.ppermute(total, ("zh", "c"), crossing(4, (3, 1)))
    same = same_spin_beta([below, crossed, coef_v, mate, above], placed)
    second, same = lax.optimization_barrier((second, same))

    excited = excited_block(total, second, coupling, scale)
    blocks = [excited] + [swapped(excited, "y", k) for k in (1, 2, 3)]
    same = same_spin_alpha(where, alpha_cols, [coef_v, near, far], alpha_ops, same)
    *blocks, same = lax.optimization_barrier((*blocks, same))

    theirs = mixed_mate(blocks, pair_mate)
    begun = finished_own(where, same, blocks, pair_v, denominators)
    return finished_mate(where, same, swapped(theirs, "c", 1), denominators, begun)


def solution(mesh):
    finer = Mesh(mesh.devices.reshape(4, 2, 4, 4, 2), (*ALPHA, *BETA))
    placed = (
        P(ALPHA, BETA),
        P(BETA, None),
        P(BETA, None),
        P(ALPHA, None),
        P(ALPHA, None),
        P(ALPHA, None),
        P(BETA, None),
        P(),
        P(ALPHA, BETA),
    )
    return jax.shard_map(
        local, mesh=finer, in_specs=placed, out_specs=P(ALPHA, BETA), check_vma=False
    )
```

```python
import jax
import jax.numpy as jnp
from jax import lax
from jax.experimental import pallas as pl
from jax.experimental.pallas import tpu as pltpu
from jax.sharding import Mesh
from jax.sharding import PartitionSpec as P

ALPHA = ("x", "zl")
BETA = ("y", "zh", "c")
F32 = jnp.float32
BF16 = jnp.bfloat16
SMEM = pl.BlockSpec(memory_space=pltpu.SMEM)
VMEM = pl.BlockSpec(memory_space=pltpu.VMEM)
HBM = pl.BlockSpec(memory_space=pltpu.HBM)
ANY = pl.BlockSpec(memory_space=pl.ANY)
MIB = 1 << 20


def dot(a, b, dims=((1,), (0,))):
    return lax.dot_general(a, b, (dims, ((), ())), preferred_element_type=F32)


def swapped(block, axis, mask):
    count = lax.axis_size(axis)
    return lax.ppermute(block, axis, [(i, i ^ mask) for i in range(count)])


def rotated(block, axis, distance):
    count = lax.axis_size(axis)
    return lax.ppermute(block, axis, [(i, (i + distance) % count) for i in range(count)])


def call(kernel, outs, args, specs, cost, scratch=(), aliases=None, out_specs=None, limit=16):
    args = [
        pltpu.with_memory_space_constraint(arg, pltpu.HBM) if spec is HBM else arg
        for arg, spec in zip(args, specs)
    ]
    return pl.pallas_call(
        kernel,
        out_shape=outs,
        in_specs=specs,
        out_specs=out_specs or [VMEM] * len(outs),
        scratch_shapes=list(scratch),
        input_output_aliases=aliases or {},
        compiler_params=pltpu.CompilerParams(vmem_limit_bytes=limit * MIB),
        cost_estimate=pl.CostEstimate(flops=cost[0], bytes_accessed=cost[1], transcendentals=0),
        name=kernel.__name__,
    )(*args)


def shape(dims, kind=BF16):
    return jax.ShapeDtypeStruct(dims, kind)


def block_rows(where_ref, k, width):
    return pl.ds(pl.multiple_of(where_ref[k] * width, width), width)


def loaded(coef, pair_t):
    def loaded_kernel(coef_ref, pair_ref, coef_out, pair_out, sems):
        copies = [
            pltpu.make_async_copy(coef_ref, coef_out, sems.at[0]),
            pltpu.make_async_copy(pair_ref, pair_out, sems.at[1]),
        ]
        for copy in copies:
            copy.start()
        for copy in copies:
            copy.wait()

    return call(
        loaded_kernel,
        [shape(coef.shape), shape(pair_t.shape)],
        (coef, pair_t),
        [HBM, HBM],
        (0, 1 * MIB),
        [pltpu.SemaphoreType.DMA((2,))],
    )


def density_parts(where, own, mate, pair_own, pair_mate):
    pairs, width = pair_mate.shape

    def density_parts_kernel(where_ref, own_ref, mate_ref, po_ref, pm_ref, *outs):
        left = jnp.concatenate([po_ref[...], pm_ref[...]], axis=1)
        for k, out in enumerate(outs):
            rows = block_rows(where_ref, k, width)
            right = jnp.concatenate([own_ref[rows, :], mate_ref[rows, :]], axis=1)
            out[...] = dot(left, right, ((1,), (1,))).astype(BF16)

    return call(
        density_parts_kernel,
        [shape((pairs, width))] * 4,
        (where, own, mate, pair_own, pair_mate),
        [SMEM] + [VMEM] * 4,
        (16 * pairs * width * width, 1 * MIB),
    )


def staged(where, cols, coupling, pair_alpha_t, beta_ops, tie):
    pairs, width = coupling.shape[0], beta_ops.shape[0]
    listed = beta_ops.shape[1] // width
    count = lax.axis_size(BETA)

    def staged_kernel(
        where_ref, cols_ref, c_ref, pa_ref, ops_ref, tie_ref, c_out, pa_out, w_out, pa_v, ops_v, sems
    ):
        rows = block_rows(where_ref, 0, width)
        copies = [
            pltpu.make_async_copy(ops_ref, ops_v, sems.at[0]),
            pltpu.make_async_copy(pa_ref.at[:, rows], pa_v, sems.at[1]),
            pltpu.make_async_copy(c_ref, c_out, sems.at[2]),
        ]
        for copy in copies:
            copy.start()
        copies[0].wait()
        core = where_ref[8]
        for n in range(5):
            offset = n if n in (0, 2, 4) else jnp.where(core == 0, n, 4 - n)
            tile = jnp.zeros((width, width), F32)
            for k in range(listed):
                here = lax.rem(cols_ref[0, k] - where_ref[9] + 2 + count, count)
                part = ops_v[:, k * width : (k + 1) * width].astype(F32)
                tile = jnp.where(here == offset, part, tile)
            w_out[:, n * width : (n + 1) * width] = tile.astype(BF16)
        copies[1].wait()
        pa_out[...] = pa_v[...].astype(F32).T
        copies[2].wait()

    return call(
        staged_kernel,
        [shape(coupling.shape), shape((width, pairs), F32), shape((width, 5 * width))],
        (where, cols, coupling, pair_alpha_t, beta_ops, tie),
        [SMEM, SMEM, HBM, HBM, HBM, ANY],
        (pairs * pairs, 2 * MIB),
        [
            pltpu.VMEM((pairs, width), BF16),
            pltpu.VMEM(beta_ops.shape, BF16),
            pltpu.SemaphoreType.DMA((3,)),
        ],
    )


def excited_block(near, far, coupling, scale):
    pairs, width = near.shape

    def excited_block_kernel(near_ref, far_ref, coupling_ref, scale_ref, out_ref):
        total = near_ref[...].astype(F32) + far_ref[...].astype(F32)
        density = total.T.astype(BF16)
        out_ref[...] = (dot(density, coupling_ref[...]) * scale_ref[...]).astype(BF16)

    return call(
        excited_block_kernel,
        [shape((width, pairs))],
        (near, far, coupling, scale),
        [VMEM] * 4,
        (2 * pairs * pairs * width, 2 * MIB),
    )[0]


def mixed_blocks(own, mate, pairs_of):
    width = own.shape[0]

    def mixed_blocks_kernel(own_ref, mate_ref, p0, p1, p2, p3, *outs):
        for half, rows in enumerate((own_ref, mate_ref)):
            for out, right in zip(outs, (p0, p1, p2, p3)):
                out[half] = dot(rows[...], right[...]).astype(out.dtype)

    return call(
        mixed_blocks_kernel,
        [shape((2, width, width), F32)] + [shape((2, width, width))] * 3,
        (own, mate, *pairs_of),
        [VMEM] * 6,
        (16 * own.size * width, 1 * MIB),
    )


def finished(where, same, parts, denominators):
    rows, width = same.shape

    def finished_kernel(where_ref, same_ref, m0, m1, m2, m3, den_ref, out, held, sems):
        copies = []
        for k, part in enumerate((m0, m1, m2, m3)):
            for half in (0, 1):
                n = 2 * k + half
                at = block_rows(where_ref, k + 4 * half, width)
                held[n] = (same_ref[at, :] + part[half].astype(F32)) / den_ref[at, :]
                copies.append(pltpu.make_async_copy(held.at[n], out.at[at, :], sems.at[n]))
                copies[-1].start()
        for copy in copies:
            copy.wait()

    return call(
        finished_kernel,
        [shape((rows, width), F32)],
        (where, same, *parts, denominators),
        [SMEM] + [VMEM] * 6,
        (rows * width * 2, 2 * MIB),
        [pltpu.VMEM((8, width, width), F32), pltpu.SemaphoreType.DMA((8,))],
        out_specs=[HBM],
    )[0]


def same_spin_beta(blocks, placed):
    rows, width = blocks[0].shape

    def same_spin_beta_kernel(b0, b1, b2, b3, b4, w_ref, out_ref):
        left = jnp.concatenate([b[...] for b in (b0, b1, b2, b3, b4)], axis=1)
        out_ref[...] = dot(left, w_ref[...], ((1,), (1,)))

    return call(
        same_spin_beta_kernel,
        [shape((rows, width), F32)],
        (*blocks, placed),
        [VMEM] * 6,
        (2 * rows * width * width * 5, 2 * MIB),
        limit=24,
    )[0]


def same_spin_alpha(where, cols, blocks, alpha_ops, start):
    rows, width = start.shape
    depth = blocks[0].shape[0]
    span = alpha_ops.shape[1]
    step = 256
    count = lax.axis_size(ALPHA)

    def same_spin_alpha_kernel(
        where_ref, cols_ref, own_ref, near_ref, far_ref, ops_ref, start_ref, out_ref, ops_v, picked, sems
    ):
        copies = [
            pltpu.make_async_copy(ops_ref.at[r : r + step, :], ops_v.at[r : r + step, :], sems.at[n])
            for n, r in enumerate(range(0, rows, step))
        ]
        for copy in copies:
            copy.start()
        for k in range(span // depth):
            offset = lax.rem(cols_ref[0, k] - where_ref[10] + 1 + count, count)
            picked[k * depth : (k + 1) * depth, :] = jnp.where(
                offset == 1,
                own_ref[...],
                jnp.where(offset == where_ref[11], near_ref[...], far_ref[...]),
            )
        for copy, r in zip(copies, range(0, rows, step)):
            copy.wait()
            at = slice(r, r + step)
            out_ref[at, :] = start_ref[at, :] + dot(ops_v[at, :], picked[...])

    return call(
        same_spin_alpha_kernel,
        [shape((rows, width), F32)],
        (where, cols, *blocks, alpha_ops, start),
        [SMEM, SMEM] + [VMEM] * 3 + [HBM, VMEM],
        (2 * rows * width * depth * 4, 10 * MIB),
        [
            pltpu.VMEM((rows, span), BF16),
            pltpu.VMEM((span, width), BF16),
            pltpu.SemaphoreType.DMA((rows // step,)),
        ],
        limit=24,
    )[0]


def local(
    coef,
    beta_ops,
    beta_cols,
    alpha_ops,
    alpha_cols,
    pair_alpha,
    pair_beta,
    pair_coupling,
    denominators,
):
    y, core = lax.axis_index("y"), lax.axis_index("c")
    low = lax.axis_index("zl")
    row_blocks = [(y ^ k) * 2 for k in range(4)]
    where = [r + core for r in row_blocks] + [r + 1 - core for r in row_blocks]
    where += [core, lax.axis_index(BETA), lax.axis_index(ALPHA), 2 - 2 * low]
    where = jnp.stack(where).astype(jnp.int32)

    pair_t = pair_beta.T
    mate = swapped(coef, "c", 1)
    pair_mate = swapped(pair_t, "c", 1)
    coef_v, pair_v = loaded(coef, pair_t)

    below = rotated(coef_v, BETA, 2)
    above = rotated(coef_v, BETA, -2)
    xs, route = lax.axis_size("x"), []
    for i in range(xs):
        route += [(2 * i, 2 * ((i + 1) % xs)), (2 * i + 1, 2 * ((i - 1) % xs) + 1)]

    parts = density_parts(where, coef_v, mate, pair_v, pair_mate)
    coupling, scale, placed = staged(
        where, beta_cols, pair_coupling, pair_alpha.T, beta_ops, parts[0]
    )
    got = [swapped(parts[k], "y", k) for k in (1, 3, 2)]
    *got, below, above = lax.optimization_barrier((*got, below, above))
    near = swapped(coef_v, "zl", 1)
    total = parts[0].astype(F32)
    for part in got:
        total = total + part.astype(F32)
    total = total.astype(BF16)
    total, coupling, scale, placed = lax.optimization_barrier((total, coupling, scale, placed))

    far = lax.ppermute(near, ALPHA, route)
    zs = lax.axis_size("zh")
    steps = [[(2 * i + h, 2 * (i ^ m[h]) + h) for i in range(zs) for h in (0, 1)] for m in ((1, 3), (3, 1))]
    first = lax.ppermute(total, ("zh", "c"), steps[0])
    sent, _ = lax.optimization_barrier((pair_v, total))
    pairs = [pair_v] + [swapped(sent, "y", k) for k in (1, 2, 3)]
    crossed = swapped(jnp.where(core == 0, above, below), "c", 1)
    total = (total.astype(F32) + first.astype(F32)).astype(BF16)
    total, crossed, pairs[1], pairs[3] = lax.optimization_barrier(
        (total, crossed, pairs[1], pairs[3])
    )
    second = lax.ppermute(total, ("zh", "c"), steps[1])
    same = same_spin_beta([below, crossed, coef_v, mate, above], placed)
    second, same, pairs[2] = lax.optimization_barrier((second, same, pairs[2]))

    excited = excited_block(total, second, coupling, scale)
    mine, *out = mixed_blocks(excited, swapped(excited, "c", 1), pairs)
    back = [swapped(block, "y", k) for k, block in zip((1, 2, 3), out)]
    same = same_spin_alpha(where, alpha_cols, [coef_v, near, far], alpha_ops, same)
    *back, same = lax.optimization_barrier((*back, same))
    return finished(where, same, [mine, *back], denominators)


def solution(mesh):
    finer = Mesh(mesh.devices.reshape(4, 2, 4, 4, 2), (*ALPHA, *BETA))
    placed = (
        P(ALPHA, BETA),
        P(BETA, None),
        P(BETA, None),
        P(ALPHA, None),
        P(ALPHA, None),
        P(ALPHA, None),
        P(BETA, None),
        P(),
        P(ALPHA, BETA),
    )
    return jax.shard_map(
        local, mesh=finer, in_specs=placed, out_specs=P(ALPHA, BETA), check_vma=False
    )
```

```python
import jax
import jax.numpy as jnp
from jax import lax
from jax.experimental import pallas as pl
from jax.experimental.pallas import tpu as pltpu
from jax.sharding import Mesh
from jax.sharding import PartitionSpec as P

ALPHA = ("x", "zl")
BETA = ("y", "zh", "c")
F32 = jnp.float32
BF16 = jnp.bfloat16
SMEM = pl.BlockSpec(memory_space=pltpu.SMEM)
VMEM = pl.BlockSpec(memory_space=pltpu.VMEM)
HBM = pl.BlockSpec(memory_space=pltpu.HBM)
ANY = pl.BlockSpec(memory_space=pl.ANY)
MIB = 1 << 20


def dot(a, b, dims=((1,), (0,))):
    return lax.dot_general(a, b, (dims, ((), ())), preferred_element_type=F32)


def swapped(block, axis, mask):
    count = lax.axis_size(axis)
    return lax.ppermute(block, axis, [(i, i ^ mask) for i in range(count)])


def rotated(block, axis, distance):
    count = lax.axis_size(axis)
    return lax.ppermute(block, axis, [(i, (i + distance) % count) for i in range(count)])


def crossing(masks):
    return [(2 * i + h, 2 * (i ^ masks[h]) + h) for i in range(4) for h in (0, 1)]


def call(kernel, outs, args, specs, cost, scratch=(), aliases=None, out_specs=None, limit=16):
    args = [
        pltpu.with_memory_space_constraint(arg, pltpu.HBM) if spec is HBM else arg
        for arg, spec in zip(args, specs)
    ]
    return pl.pallas_call(
        kernel,
        out_shape=outs,
        in_specs=specs,
        out_specs=out_specs or [VMEM] * len(outs),
        scratch_shapes=list(scratch),
        input_output_aliases=aliases or {},
        compiler_params=pltpu.CompilerParams(vmem_limit_bytes=limit * MIB),
        cost_estimate=pl.CostEstimate(flops=cost[0], bytes_accessed=cost[1], transcendentals=0),
        name=kernel.__name__,
    )(*args)


def shape(dims, kind=BF16):
    return jax.ShapeDtypeStruct(dims, kind)


def block_rows(where_ref, k, width):
    return pl.ds(pl.multiple_of(where_ref[k] * width, width), width)


def loaded(coef, pair_t):
    def loaded_kernel(coef_ref, pair_ref, coef_out, pair_out, sems):
        copies = [
            pltpu.make_async_copy(coef_ref, coef_out, sems.at[0]),
            pltpu.make_async_copy(pair_ref, pair_out, sems.at[1]),
        ]
        for copy in copies:
            copy.start()
        for copy in copies:
            copy.wait()

    return call(
        loaded_kernel,
        [shape(coef.shape), shape(pair_t.shape)],
        (coef, pair_t),
        [HBM, HBM],
        (0, 1 * MIB),
        [pltpu.SemaphoreType.DMA((2,))],
    )


def density_parts(where, own, mate, pair_own, pair_mate):
    pairs, width = pair_mate.shape

    def density_parts_kernel(where_ref, own_ref, mate_ref, po_ref, pm_ref, *outs):
        left = jnp.concatenate([po_ref[...], pm_ref[...]], axis=1)
        for k, out in enumerate(outs):
            rows = block_rows(where_ref, k, width)
            right = jnp.concatenate([own_ref[rows, :], mate_ref[rows, :]], axis=1)
            out[...] = dot(left, right, ((1,), (1,))).astype(BF16)

    return call(
        density_parts_kernel,
        [shape((pairs, width))] * 4,
        (where, own, mate, pair_own, pair_mate),
        [SMEM] + [VMEM] * 4,
        (16 * pairs * width * width, 1 * MIB),
    )


def staged(where, cols, coupling, pair_alpha_t, beta_ops, tie):
    pairs, width = coupling.shape[0], beta_ops.shape[0]
    listed = beta_ops.shape[1] // width
    count = lax.axis_size(BETA)

    def staged_kernel(
        where_ref, cols_ref, c_ref, pa_ref, ops_ref, tie_ref, c_out, pa_out, w_out, pa_v, ops_v, sems
    ):
        rows = block_rows(where_ref, 0, width)
        copies = [
            pltpu.make_async_copy(ops_ref, ops_v, sems.at[0]),
            pltpu.make_async_copy(pa_ref.at[:, rows], pa_v, sems.at[1]),
            pltpu.make_async_copy(c_ref, c_out, sems.at[2]),
        ]
        for copy in copies:
            copy.start()
        copies[0].wait()
        core = where_ref[8]
        for n in range(5):
            offset = n if n in (0, 2, 4) else jnp.where(core == 0, n, 4 - n)
            tile = jnp.zeros((width, width), F32)
            for k in range(listed):
                here = lax.rem(cols_ref[0, k] - where_ref[9] + 2 + count, count)
                part = ops_v[:, k * width : (k + 1) * width].astype(F32)
                tile = jnp.where(here == offset, part, tile)
            w_out[:, n * width : (n + 1) * width] = tile.astype(BF16)
        copies[1].wait()
        pa_out[...] = pa_v[...].astype(F32).T
        copies[2].wait()

    return call(
        staged_kernel,
        [shape(coupling.shape), shape((width, pairs), F32), shape((width, 5 * width))],
        (where, cols, coupling, pair_alpha_t, beta_ops, tie),
        [SMEM, SMEM, HBM, HBM, HBM, ANY],
        (pairs * pairs, 2 * MIB),
        [
            pltpu.VMEM((pairs, width), BF16),
            pltpu.VMEM(beta_ops.shape, BF16),
            pltpu.SemaphoreType.DMA((3,)),
        ],
    )


def excited_block(near, far, coupling, scale):
    pairs, width = near.shape

    def excited_block_kernel(near_ref, far_ref, coupling_ref, scale_ref, out_ref):
        total = near_ref[...].astype(F32) + far_ref[...].astype(F32)
        density = total.T.astype(BF16)
        out_ref[...] = (dot(density, coupling_ref[...]) * scale_ref[...]).astype(BF16)

    return call(
        excited_block_kernel,
        [shape((width, pairs))],
        (near, far, coupling, scale),
        [VMEM] * 4,
        (2 * pairs * pairs * width, 2 * MIB),
    )[0]


def mixed_blocks(own, mate, pair_own, beside, beyond):
    width = own.shape[0]

    def mixed_blocks_kernel(own_ref, mate_ref, pair_ref, beside_ref, beyond_ref, *outs):
        rights = (pair_ref[...], beside_ref[...], beyond_ref[1], beyond_ref[0])
        for half, rows in enumerate((own_ref, mate_ref)):
            for out, right in zip(outs, rights):
                out[half] = dot(rows[...], right).astype(out.dtype)

    return call(
        mixed_blocks_kernel,
        [shape((2, width, width), F32)] + [shape((2, width, width))] * 3,
        (own, mate, pair_own, beside, beyond),
        [VMEM] * 5,
        (16 * own.size * width, 1 * MIB),
    )


def finished(where, same, parts, denominators):
    rows, width = same.shape

    def finished_kernel(where_ref, same_ref, m0, m1, m2, m3, den_ref, out, held, sems):
        copies = []
        for k, part in enumerate((m0, m1, m2, m3)):
            for half in (0, 1):
                n = 2 * k + half
                at = block_rows(where_ref, k + 4 * half, width)
                held[n] = (same_ref[at, :] + part[half].astype(F32)) / den_ref[at, :]
                copies.append(pltpu.make_async_copy(held.at[n], out.at[at, :], sems.at[n]))
                copies[-1].start()
        for copy in copies:
            copy.wait()

    return call(
        finished_kernel,
        [shape((rows, width), F32)],
        (where, same, *parts, denominators),
        [SMEM] + [VMEM] * 6,
        (rows * width * 2, 2 * MIB),
        [pltpu.VMEM((8, width, width), F32), pltpu.SemaphoreType.DMA((8,))],
        out_specs=[HBM],
    )[0]


def same_spin_beta(blocks, placed):
    rows, width = blocks[0].shape

    def same_spin_beta_kernel(b0, b1, b2, b3, b4, w_ref, out_ref):
        left = jnp.concatenate([b[...] for b in (b0, b1, b2, b3, b4)], axis=1)
        out_ref[...] = dot(left, w_ref[...], ((1,), (1,)))

    return call(
        same_spin_beta_kernel,
        [shape((rows, width), F32)],
        (*blocks, placed),
        [VMEM] * 6,
        (2 * rows * width * width * 5, 2 * MIB),
        limit=24,
    )[0]


def same_spin_alpha(where, cols, blocks, alpha_ops, start):
    rows, width = start.shape
    depth = blocks[0].shape[0]
    span = alpha_ops.shape[1]
    step = 256
    count = lax.axis_size(ALPHA)

    def same_spin_alpha_kernel(
        where_ref, cols_ref, own_ref, near_ref, far_ref, ops_ref, start_ref, out_ref, ops_v, picked, sems
    ):
        copies = [
            pltpu.make_async_copy(ops_ref.at[r : r + step, :], ops_v.at[r : r + step, :], sems.at[n])
            for n, r in enumerate(range(0, rows, step))
        ]
        for copy in copies:
            copy.start()
        for k in range(span // depth):
            offset = lax.rem(cols_ref[0, k] - where_ref[10] + 1 + count, count)
            picked[k * depth : (k + 1) * depth, :] = jnp.where(
                offset == 1,
                own_ref[...],
                jnp.where(offset == where_ref[11], near_ref[...], far_ref[...]),
            )
        for copy, r in zip(copies, range(0, rows, step)):
            copy.wait()
            at = slice(r, r + step)
            out_ref[at, :] = start_ref[at, :] + dot(ops_v[at, :], picked[...])

    return call(
        same_spin_alpha_kernel,
        [shape((rows, width), F32)],
        (where, cols, *blocks, alpha_ops, start),
        [SMEM, SMEM] + [VMEM] * 3 + [HBM, VMEM],
        (2 * rows * width * depth * 4, 10 * MIB),
        [
            pltpu.VMEM((rows, span), BF16),
            pltpu.VMEM((span, width), BF16),
            pltpu.SemaphoreType.DMA((rows // step,)),
        ],
        limit=24,
    )[0]


def local(
    coef,
    beta_ops,
    beta_cols,
    alpha_ops,
    alpha_cols,
    pair_alpha,
    pair_beta,
    pair_coupling,
    denominators,
):
    y, core = lax.axis_index("y"), lax.axis_index("c")
    low = lax.axis_index("zl")
    side = 1 + 2 * core
    row_blocks = [(y ^ m) * 2 for m in (0, side, 2, 4 - side)]
    where = [r + core for r in row_blocks] + [r + 1 - core for r in row_blocks]
    where += [core, lax.axis_index(BETA), lax.axis_index(ALPHA), 2 - 2 * low]
    where = jnp.stack(where).astype(jnp.int32)

    pair_t = pair_beta.T
    mate = swapped(coef, "c", 1)
    pair_mate = swapped(pair_t, "c", 1)
    coef_v, pair_v = loaded(coef, pair_t)

    below = rotated(coef_v, BETA, 2)
    above = rotated(coef_v, BETA, -2)
    xs, route = lax.axis_size("x"), []
    for i in range(xs):
        route += [(2 * i, 2 * ((i + 1) % xs)), (2 * i + 1, 2 * ((i - 1) % xs) + 1)]

    parts = density_parts(where, coef_v, mate, pair_v, pair_mate)
    coupling, scale, placed = staged(
        where, beta_cols, pair_coupling, pair_alpha.T, beta_ops, parts[0]
    )
    turns = (None, crossing((1, 3)), crossing((2, 2)), crossing((3, 1)))
    got = [lax.ppermute(parts[k], ("y", "c"), turns[k]) for k in (1, 3, 2)]
    *got, below, above = lax.optimization_barrier((*got, below, above))
    near = swapped(coef_v, "zl", 1)
    total = parts[0].astype(F32)
    for part in got:
        total = total + part.astype(F32)
    total = total.astype(BF16)
    total, coupling, scale, placed = lax.optimization_barrier((total, coupling, scale, placed))

    far = lax.ppermute(near, ALPHA, route)
    first = lax.ppermute(total, ("zh", "c"), turns[1])
    sent, _ = lax.optimization_barrier((pair_v, total))
    beside = lax.ppermute(sent, ("y", "c"), turns[1])
    crossed = swapped(jnp.where(core == 0, above, below), "c", 1)
    total = (total.astype(F32) + first.astype(F32)).astype(BF16)
    total, crossed, beside = lax.optimization_barrier((total, crossed, beside))
    beyond = lax.ppermute(jnp.stack([pair_v, beside]), ("y", "c"), turns[3])
    second = lax.ppermute(total, ("zh", "c"), turns[3])
    same = same_spin_beta([below, crossed, coef_v, mate, above], placed)
    same = same_spin_alpha(where, alpha_cols, [coef_v, near, far], alpha_ops, same)
    second, same = lax.optimization_barrier((second, same))

    excited = excited_block(total, second, coupling, scale)
    mine, *out = mixed_blocks(excited, swapped(excited, "c", 1), pair_v, beside, beyond)
    back = [lax.ppermute(out[k - 1], ("y", "c"), turns[k]) for k in (1, 2, 3)]
    return finished(where, same, [mine, *back], denominators)


def solution(mesh):
    finer = Mesh(mesh.devices.reshape(4, 2, 4, 4, 2), (*ALPHA, *BETA))
    placed = (
        P(ALPHA, BETA),
        P(BETA, None),
        P(BETA, None),
        P(ALPHA, None),
        P(ALPHA, None),
        P(ALPHA, None),
        P(BETA, None),
        P(),
        P(ALPHA, BETA),
    )
    return jax.shard_map(
        local, mesh=finer, in_specs=placed, out_specs=P(ALPHA, BETA), check_vma=False
    )
```

```python
import jax
import jax.numpy as jnp
from jax import lax
from jax.experimental import pallas as pl
from jax.experimental.pallas import tpu as pltpu
from jax.sharding import Mesh
from jax.sharding import PartitionSpec as P

ALPHA = ("x", "zl")
BETA = ("y", "zh", "c")
F32 = jnp.float32
BF16 = jnp.bfloat16
SMEM = pl.BlockSpec(memory_space=pltpu.SMEM)
VMEM = pl.BlockSpec(memory_space=pltpu.VMEM)
HBM = pl.BlockSpec(memory_space=pltpu.HBM)
ANY = pl.BlockSpec(memory_space=pl.ANY)
MIB = 1 << 20


def dot(a, b, dims=((1,), (0,))):
    return lax.dot_general(a, b, (dims, ((), ())), preferred_element_type=F32)


def swapped(block, axis, mask):
    count = lax.axis_size(axis)
    return lax.ppermute(block, axis, [(i, i ^ mask) for i in range(count)])


def rotated(block, axis, distance):
    count = lax.axis_size(axis)
    return lax.ppermute(block, axis, [(i, (i + distance) % count) for i in range(count)])


def crossing(masks):
    return [(2 * i + h, 2 * (i ^ masks[h]) + h) for i in range(4) for h in (0, 1)]


def call(kernel, outs, args, specs, cost, scratch=(), aliases=None, out_specs=None, limit=16):
    args = [
        pltpu.with_memory_space_constraint(arg, pltpu.HBM) if spec is HBM else arg
        for arg, spec in zip(args, specs)
    ]
    return pl.pallas_call(
        kernel,
        out_shape=outs,
        in_specs=specs,
        out_specs=out_specs or [VMEM] * len(outs),
        scratch_shapes=list(scratch),
        input_output_aliases=aliases or {},
        compiler_params=pltpu.CompilerParams(vmem_limit_bytes=limit * MIB),
        cost_estimate=pl.CostEstimate(flops=cost[0], bytes_accessed=cost[1], transcendentals=0),
        name=kernel.__name__,
    )(*args)


def shape(dims, kind=BF16):
    return jax.ShapeDtypeStruct(dims, kind)


def block_rows(where_ref, k, width):
    return pl.ds(pl.multiple_of(where_ref[k] * width, width), width)


def loaded(coef, pair_t):
    def loaded_kernel(coef_ref, pair_ref, coef_out, pair_out, sems):
        copies = [
            pltpu.make_async_copy(coef_ref, coef_out, sems.at[0]),
            pltpu.make_async_copy(pair_ref, pair_out, sems.at[1]),
        ]
        for copy in copies:
            copy.start()
        for copy in copies:
            copy.wait()

    return call(
        loaded_kernel,
        [shape(coef.shape), shape(pair_t.shape)],
        (coef, pair_t),
        [HBM, HBM],
        (0, 1 * MIB),
        [pltpu.SemaphoreType.DMA((2,))],
    )


def density_parts(where, own, mate, pair_own, pair_mate):
    pairs, width = pair_mate.shape

    def density_parts_kernel(where_ref, own_ref, mate_ref, po_ref, pm_ref, *outs):
        left = jnp.concatenate([po_ref[...], pm_ref[...]], axis=1)
        for k, out in enumerate(outs):
            rows = block_rows(where_ref, k, width)
            right = jnp.concatenate([own_ref[rows, :], mate_ref[rows, :]], axis=1)
            out[...] = dot(left, right, ((1,), (1,))).astype(BF16)

    return call(
        density_parts_kernel,
        [shape((pairs, width))] * 4,
        (where, own, mate, pair_own, pair_mate),
        [SMEM] + [VMEM] * 4,
        (16 * pairs * width * width, 1 * MIB),
    )


def staged(where, cols, coupling, pair_alpha_t, beta_ops, tie):
    pairs, width = coupling.shape[0], beta_ops.shape[0]
    listed = beta_ops.shape[1] // width
    count = lax.axis_size(BETA)

    def staged_kernel(
        where_ref, cols_ref, c_ref, pa_ref, ops_ref, tie_ref, c_out, pa_out, w_out, pa_v, ops_v, sems
    ):
        rows = block_rows(where_ref, 0, width)
        copies = [
            pltpu.make_async_copy(ops_ref, ops_v, sems.at[0]),
            pltpu.make_async_copy(pa_ref.at[:, rows], pa_v, sems.at[1]),
            pltpu.make_async_copy(c_ref, c_out, sems.at[2]),
        ]
        for copy in copies:
            copy.start()
        copies[0].wait()
        core = where_ref[8]
        for n in range(5):
            offset = n if n in (0, 2, 4) else jnp.where(core == 0, n, 4 - n)
            tile = jnp.zeros((width, width), F32)
            for k in range(listed):
                here = lax.rem(cols_ref[0, k] - where_ref[9] + 2 + count, count)
                part = ops_v[:, k * width : (k + 1) * width].astype(F32)
                tile = jnp.where(here == offset, part, tile)
            w_out[:, n * width : (n + 1) * width] = tile.astype(BF16)
        copies[1].wait()
        pa_out[...] = pa_v[...].astype(F32).T
        copies[2].wait()

    return call(
        staged_kernel,
        [shape(coupling.shape), shape((width, pairs), F32), shape((width, 5 * width))],
        (where, cols, coupling, pair_alpha_t, beta_ops, tie),
        [SMEM, SMEM, HBM, HBM, HBM, ANY],
        (pairs * pairs, 2 * MIB),
        [
            pltpu.VMEM((pairs, width), BF16),
            pltpu.VMEM(beta_ops.shape, BF16),
            pltpu.SemaphoreType.DMA((3,)),
        ],
    )


def excited_block(near, far, coupling, scale):
    pairs, width = near.shape

    def excited_block_kernel(near_ref, far_ref, coupling_ref, scale_ref, out_ref):
        total = near_ref[...].astype(F32) + far_ref[...].astype(F32)
        density = total.T.astype(BF16)
        out_ref[...] = (dot(density, coupling_ref[...]) * scale_ref[...]).astype(BF16)

    return call(
        excited_block_kernel,
        [shape((width, pairs))],
        (near, far, coupling, scale),
        [VMEM] * 4,
        (2 * pairs * pairs * width, 2 * MIB),
    )[0]


def mixed_blocks(own, mate, pair_own, beside, beyond):
    width = own.shape[0]

    def mixed_blocks_kernel(own_ref, mate_ref, pair_ref, beside_ref, beyond_ref, *outs):
        rights = (pair_ref[...], beside_ref[...], beyond_ref[1], beyond_ref[0])
        for half, rows in enumerate((own_ref, mate_ref)):
            for out, right in zip(outs, rights):
                out[half] = dot(rows[...], right).astype(out.dtype)

    return call(
        mixed_blocks_kernel,
        [shape((2, width, width), F32)] + [shape((2, width, width))] * 3,
        (own, mate, pair_own, beside, beyond),
        [VMEM] * 5,
        (16 * own.size * width, 1 * MIB),
    )


def finished(where, same, parts, denominators):
    rows, width = same.shape

    def finished_kernel(where_ref, same_ref, m0, m1, m2, m3, den_ref, out, held, sems):
        copies = []
        for k, part in enumerate((m0, m1, m2, m3)):
            for half in (0, 1):
                n = 2 * k + half
                at = block_rows(where_ref, k + 4 * half, width)
                held[n] = (same_ref[at, :] + part[half].astype(F32)) / den_ref[at, :]
                copies.append(pltpu.make_async_copy(held.at[n], out.at[at, :], sems.at[n]))
                copies[-1].start()
        for copy in copies:
            copy.wait()

    return call(
        finished_kernel,
        [shape((rows, width), F32)],
        (where, same, *parts, denominators),
        [SMEM] + [VMEM] * 6,
        (rows * width * 2, 2 * MIB),
        [pltpu.VMEM((8, width, width), F32), pltpu.SemaphoreType.DMA((8,))],
        out_specs=[HBM],
    )[0]


def same_spin_beta(blocks, placed):
    rows, width = blocks[0].shape

    def same_spin_beta_kernel(b0, b1, b2, b3, b4, w_ref, out_ref):
        left = jnp.concatenate([b[...] for b in (b0, b1, b2, b3, b4)], axis=1)
        out_ref[...] = dot(left, w_ref[...], ((1,), (1,)))

    return call(
        same_spin_beta_kernel,
        [shape((rows, width), F32)],
        (*blocks, placed),
        [VMEM] * 6,
        (2 * rows * width * width * 5, 2 * MIB),
        limit=24,
    )[0]


def same_spin_alpha(where, cols, blocks, alpha_ops, start, part):
    rows, width = start.shape
    depth = blocks[0].shape[0]
    span = alpha_ops.shape[1]
    step = 256
    half = rows // 2
    mine = range(part * half, (part + 1) * half, step)
    rest = slice((1 - part) * half, (2 - part) * half)
    count = lax.axis_size(ALPHA)

    def same_spin_alpha_kernel(
        where_ref, cols_ref, own_ref, near_ref, far_ref, ops_ref, start_ref, out_ref, ops_v, picked, sems
    ):
        copies = [
            pltpu.make_async_copy(ops_ref.at[r : r + step, :], ops_v.at[n], sems.at[n])
            for n, r in enumerate(mine)
        ]
        for copy in copies:
            copy.start()
        for k in range(span // depth):
            offset = lax.rem(cols_ref[0, k] - where_ref[10] + 1 + count, count)
            picked[k * depth : (k + 1) * depth, :] = jnp.where(
                offset == 1,
                own_ref[...],
                jnp.where(offset == where_ref[11], near_ref[...], far_ref[...]),
            )
        out_ref[rest, :] = start_ref[rest, :]
        for n, r in enumerate(mine):
            copies[n].wait()
            at = slice(r, r + step)
            out_ref[at, :] = start_ref[at, :] + dot(ops_v[n], picked[...])

    return call(
        same_spin_alpha_kernel,
        [shape((rows, width), F32)],
        (where, cols, *blocks, alpha_ops, start),
        [SMEM, SMEM] + [VMEM] * 3 + [HBM, VMEM],
        (rows * width * depth * 4, 5 * MIB),
        [
            pltpu.VMEM((half // step, step, span), BF16),
            pltpu.VMEM((span, width), BF16),
            pltpu.SemaphoreType.DMA((half // step,)),
        ],
        limit=16,
    )[0]


def local(
    coef,
    beta_ops,
    beta_cols,
    alpha_ops,
    alpha_cols,
    pair_alpha,
    pair_beta,
    pair_coupling,
    denominators,
):
    y, core = lax.axis_index("y"), lax.axis_index("c")
    low = lax.axis_index("zl")
    side = 1 + 2 * core
    row_blocks = [(y ^ m) * 2 for m in (0, side, 2, 4 - side)]
    where = [r + core for r in row_blocks] + [r + 1 - core for r in row_blocks]
    where += [core, lax.axis_index(BETA), lax.axis_index(ALPHA), 2 - 2 * low]
    where = jnp.stack(where).astype(jnp.int32)

    pair_t = pair_beta.T
    mate = swapped(coef, "c", 1)
    pair_mate = swapped(pair_t, "c", 1)
    coef_v, pair_v = loaded(coef, pair_t)

    below = rotated(coef_v, BETA, 2)
    above = rotated(coef_v, BETA, -2)
    xs, route = lax.axis_size("x"), []
    for i in range(xs):
        route += [(2 * i, 2 * ((i + 1) % xs)), (2 * i + 1, 2 * ((i - 1) % xs) + 1)]

    parts = density_parts(where, coef_v, mate, pair_v, pair_mate)
    coupling, scale, placed = staged(
        where, beta_cols, pair_coupling, pair_alpha.T, beta_ops, parts[0]
    )
    turns = (None, crossing((1, 3)), crossing((2, 2)), crossing((3, 1)))
    got = [lax.ppermute(parts[k], ("y", "c"), turns[k]) for k in (1, 3, 2)]
    *got, below, above = lax.optimization_barrier((*got, below, above))
    near = swapped(coef_v, "zl", 1)
    total = parts[0].astype(F32)
    for part in got:
        total = total + part.astype(F32)
    total = total.astype(BF16)
    total, coupling, scale, placed = lax.optimization_barrier((total, coupling, scale, placed))

    far = lax.ppermute(near, ALPHA, route)
    first = lax.ppermute(total, ("zh", "c"), turns[1])
    sent, _ = lax.optimization_barrier((pair_v, total))
    beside = lax.ppermute(sent, ("y", "c"), turns[1])
    crossed = swapped(jnp.where(core == 0, above, below), "c", 1)
    first, beside = lax.optimization_barrier((first, beside))
    total = (total.astype(F32) + first.astype(F32)).astype(BF16)
    total, crossed = lax.optimization_barrier((total, crossed))
    beyond = lax.ppermute(jnp.stack([pair_v, beside]), ("y", "c"), turns[3])
    second = lax.ppermute(total, ("zh", "c"), turns[3])
    same = same_spin_beta([below, crossed, coef_v, mate, above], placed)
    around = [coef_v, near, far]
    same = same_spin_alpha(where, alpha_cols, around, alpha_ops, same, 0)
    second, same = lax.optimization_barrier((second, same))

    excited = excited_block(total, second, coupling, scale)
    mine, *out = mixed_blocks(excited, swapped(excited, "c", 1), pair_v, beside, beyond)
    back = [lax.ppermute(out[k - 1], ("y", "c"), turns[k]) for k in (1, 2, 3)]
    same = same_spin_alpha(where, alpha_cols, around, alpha_ops, same, 1)
    *back, same = lax.optimization_barrier((*back, same))
    return finished(where, same, [mine, *back], denominators)


def solution(mesh):
    finer = Mesh(mesh.devices.reshape(4, 2, 4, 4, 2), (*ALPHA, *BETA))
    placed = (
        P(ALPHA, BETA),
        P(BETA, None),
        P(BETA, None),
        P(ALPHA, None),
        P(ALPHA, None),
        P(ALPHA, None),
        P(BETA, None),
        P(),
        P(ALPHA, BETA),
    )
    return jax.shard_map(
        local, mesh=finer, in_specs=placed, out_specs=P(ALPHA, BETA), check_vma=False
    )
```

```python
import jax
import jax.numpy as jnp
from jax import lax
from jax.experimental import pallas as pl
from jax.experimental.pallas import tpu as pltpu
from jax.sharding import Mesh
from jax.sharding import PartitionSpec as P

ALPHA = ("x", "zl")
BETA = ("y", "zh", "c")
F32 = jnp.float32
BF16 = jnp.bfloat16
SMEM = pl.BlockSpec(memory_space=pltpu.SMEM)
VMEM = pl.BlockSpec(memory_space=pltpu.VMEM)
HBM = pl.BlockSpec(memory_space=pltpu.HBM)
ANY = pl.BlockSpec(memory_space=pl.ANY)
MIB = 1 << 20


def dot(a, b, dims=((1,), (0,))):
    return lax.dot_general(a, b, (dims, ((), ())), preferred_element_type=F32)


def swapped(block, axis, mask):
    count = lax.axis_size(axis)
    return lax.ppermute(block, axis, [(i, i ^ mask) for i in range(count)])


def rotated(block, axis, distance):
    count = lax.axis_size(axis)
    return lax.ppermute(block, axis, [(i, (i + distance) % count) for i in range(count)])


def crossing(masks):
    return [(2 * i + h, 2 * (i ^ masks[h]) + h) for i in range(4) for h in (0, 1)]


def call(kernel, outs, args, specs, cost, scratch=(), aliases=None, out_specs=None, limit=16):
    args = [
        pltpu.with_memory_space_constraint(arg, pltpu.HBM) if spec is HBM else arg
        for arg, spec in zip(args, specs)
    ]
    return pl.pallas_call(
        kernel,
        out_shape=outs,
        in_specs=specs,
        out_specs=out_specs or [VMEM] * len(outs),
        scratch_shapes=list(scratch),
        input_output_aliases=aliases or {},
        compiler_params=pltpu.CompilerParams(vmem_limit_bytes=limit * MIB),
        cost_estimate=pl.CostEstimate(flops=cost[0], bytes_accessed=cost[1], transcendentals=0),
        name=kernel.__name__,
    )(*args)


def shape(dims, kind=BF16):
    return jax.ShapeDtypeStruct(dims, kind)


def block_rows(where_ref, k, width):
    return pl.ds(pl.multiple_of(where_ref[k] * width, width), width)


def loaded(coef, pair_t):
    def loaded_kernel(coef_ref, pair_ref, coef_out, pair_out, sems):
        copies = [
            pltpu.make_async_copy(coef_ref, coef_out, sems.at[0]),
            pltpu.make_async_copy(pair_ref, pair_out, sems.at[1]),
        ]
        for copy in copies:
            copy.start()
        for copy in copies:
            copy.wait()

    return call(
        loaded_kernel,
        [shape(coef.shape), shape(pair_t.shape)],
        (coef, pair_t),
        [HBM, HBM],
        (0, 1 * MIB),
        [pltpu.SemaphoreType.DMA((2,))],
    )


def density_parts(where, own, mate, pair_own, pair_mate):
    pairs, width = pair_mate.shape

    def density_parts_kernel(where_ref, own_ref, mate_ref, po_ref, pm_ref, *outs):
        left = jnp.concatenate([po_ref[...], pm_ref[...]], axis=1)
        for k, out in enumerate(outs):
            rows = block_rows(where_ref, k, width)
            right = jnp.concatenate([own_ref[rows, :], mate_ref[rows, :]], axis=1)
            out[...] = dot(left, right, ((1,), (1,))).astype(BF16)

    return call(
        density_parts_kernel,
        [shape((pairs, width))] * 4,
        (where, own, mate, pair_own, pair_mate),
        [SMEM] + [VMEM] * 4,
        (16 * pairs * width * width, 1 * MIB),
    )


def staged(where, cols, coupling, pair_alpha_t, beta_ops, tie):
    pairs, width = coupling.shape[0], beta_ops.shape[0]
    listed = beta_ops.shape[1] // width
    count = lax.axis_size(BETA)

    def staged_kernel(
        where_ref, cols_ref, c_ref, pa_ref, ops_ref, tie_ref, c_out, pa_out, w_out, pa_v, ops_v, sems
    ):
        rows = block_rows(where_ref, 0, width)
        copies = [
            pltpu.make_async_copy(ops_ref, ops_v, sems.at[0]),
            pltpu.make_async_copy(pa_ref.at[:, rows], pa_v, sems.at[1]),
            pltpu.make_async_copy(c_ref, c_out, sems.at[2]),
        ]
        for copy in copies:
            copy.start()
        copies[0].wait()
        core = where_ref[8]
        for n in range(5):
            offset = n if n in (0, 2, 4) else jnp.where(core == 0, n, 4 - n)
            tile = jnp.zeros((width, width), F32)
            for k in range(listed):
                here = lax.rem(cols_ref[k] - where_ref[9] + 2 + count, count)
                part = ops_v[:, k * width : (k + 1) * width].astype(F32)
                tile = jnp.where(here == offset, part, tile)
            w_out[:, n * width : (n + 1) * width] = tile.astype(BF16)
        copies[1].wait()
        pa_out[...] = pa_v[...].astype(F32).T
        copies[2].wait()

    return call(
        staged_kernel,
        [shape(coupling.shape), shape((width, pairs), F32), shape((width, 5 * width))],
        (where, cols, coupling, pair_alpha_t, beta_ops, tie),
        [SMEM, SMEM, HBM, HBM, HBM, ANY],
        (pairs * pairs, 2 * MIB),
        [
            pltpu.VMEM((pairs, width), BF16),
            pltpu.VMEM(beta_ops.shape, BF16),
            pltpu.SemaphoreType.DMA((3,)),
        ],
    )


def excited_block(near, far, coupling, scale):
    pairs, width = near.shape

    def excited_block_kernel(near_ref, far_ref, coupling_ref, scale_ref, out_ref):
        total = near_ref[...].astype(F32) + far_ref[...].astype(F32)
        density = total.T.astype(BF16)
        out_ref[...] = (dot(density, coupling_ref[...]) * scale_ref[...]).astype(BF16)

    return call(
        excited_block_kernel,
        [shape((width, pairs))],
        (near, far, coupling, scale),
        [VMEM] * 4,
        (2 * pairs * pairs * width, 2 * MIB),
    )[0]


def mixed_blocks(own, mate, pair_own, beside, beyond):
    width = own.shape[0]

    def mixed_blocks_kernel(own_ref, mate_ref, pair_ref, beside_ref, beyond_ref, *outs):
        rights = (pair_ref[...], beside_ref[...], beyond_ref[1], beyond_ref[0])
        for half, rows in enumerate((own_ref, mate_ref)):
            for out, right in zip(outs, rights):
                out[half] = dot(rows[...], right).astype(out.dtype)

    return call(
        mixed_blocks_kernel,
        [shape((2, width, width), F32)] + [shape((2, width, width))] * 3,
        (own, mate, pair_own, beside, beyond),
        [VMEM] * 5,
        (16 * own.size * width, 1 * MIB),
    )


def finished(where, same, parts, denominators):
    rows, width = same.shape

    def finished_kernel(where_ref, same_ref, m0, m1, m2, m3, den_ref, out, held, sems):
        copies = []
        for k, part in enumerate((m0, m1, m2, m3)):
            for half in (0, 1):
                n = 2 * k + half
                at = block_rows(where_ref, k + 4 * half, width)
                held[n] = (same_ref[at, :] + part[half].astype(F32)) / den_ref[at, :]
                copies.append(pltpu.make_async_copy(held.at[n], out.at[at, :], sems.at[n]))
                copies[-1].start()
        for copy in copies:
            copy.wait()

    return call(
        finished_kernel,
        [shape((rows, width), F32)],
        (where, same, *parts, denominators),
        [SMEM] + [VMEM] * 6,
        (rows * width * 2, 2 * MIB),
        [pltpu.VMEM((8, width, width), F32), pltpu.SemaphoreType.DMA((8,))],
        out_specs=[HBM],
    )[0]


def same_spin_beta(blocks, placed):
    rows, width = blocks[0].shape

    def same_spin_beta_kernel(b0, b1, b2, b3, b4, w_ref, out_ref):
        left = jnp.concatenate([b[...] for b in (b0, b1, b2, b3, b4)], axis=1)
        out_ref[...] = dot(left, w_ref[...], ((1,), (1,)))

    return call(
        same_spin_beta_kernel,
        [shape((rows, width), F32)],
        (*blocks, placed),
        [VMEM] * 6,
        (2 * rows * width * width * 5, 2 * MIB),
        limit=24,
    )[0]


def alpha_rows(ops_ref, picked, start_ref, out_ref, ops_v, sems, part, select):
    step = ops_v.shape[1]
    half = start_ref.shape[0] // 2
    mine = range(part * half, (part + 1) * half, step)
    rest = slice((1 - part) * half, (2 - part) * half)
    copies = [
        pltpu.make_async_copy(ops_ref.at[r : r + step, :], ops_v.at[n], sems.at[n])
        for n, r in enumerate(mine)
    ]
    for copy in copies:
        copy.start()
    select()
    out_ref[rest, :] = start_ref[rest, :]
    for n, r in enumerate(mine):
        copies[n].wait()
        at = slice(r, r + step)
        out_ref[at, :] = start_ref[at, :] + dot(ops_v[n], picked[...])


def same_spin_alpha(where, cols, blocks, alpha_ops, start):
    rows, width = start.shape
    depth = blocks[0].shape[0]
    span = alpha_ops.shape[1]
    count = lax.axis_size(ALPHA)

    def same_spin_alpha_kernel(
        where_ref, cols_ref, own_ref, near_ref, far_ref, ops_ref, start_ref, out_ref, picked, ops_v, sems
    ):
        def select():
            for k in range(span // depth):
                offset = lax.rem(cols_ref[4 + k] - where_ref[10] + 1 + count, count)
                picked[k * depth : (k + 1) * depth, :] = jnp.where(
                    offset == 1,
                    own_ref[...],
                    jnp.where(offset == where_ref[11], near_ref[...], far_ref[...]),
                )

        alpha_rows(ops_ref, picked, start_ref, out_ref, ops_v, sems, 0, select)

    return call(
        same_spin_alpha_kernel,
        [shape((rows, width), F32), shape((span, width))],
        (where, cols, *blocks, alpha_ops, start),
        [SMEM, SMEM] + [VMEM] * 3 + [HBM, VMEM],
        (rows * width * depth * 4, 5 * MIB),
        [pltpu.VMEM((2, rows // 4, span), BF16), pltpu.SemaphoreType.DMA((2,))],
    )


def rest_of_alpha(picked, alpha_ops, start):
    rows, width = start.shape
    span = alpha_ops.shape[1]

    def rest_of_alpha_kernel(picked, ops_ref, start_ref, out_ref, ops_v, sems):
        alpha_rows(ops_ref, picked, start_ref, out_ref, ops_v, sems, 1, lambda: None)

    return call(
        rest_of_alpha_kernel,
        [shape((rows, width), F32)],
        (picked, alpha_ops, start),
        [VMEM, HBM, VMEM],
        (rows * width * span, 5 * MIB),
        [pltpu.VMEM((2, rows // 4, span), BF16), pltpu.SemaphoreType.DMA((2,))],
    )[0]


def local(
    coef,
    beta_ops,
    beta_cols,
    alpha_ops,
    alpha_cols,
    pair_alpha,
    pair_beta,
    pair_coupling,
    denominators,
):
    y, core = lax.axis_index("y"), lax.axis_index("c")
    low = lax.axis_index("zl")
    side = 1 + 2 * core
    row_blocks = [(y ^ m) * 2 for m in (0, side, 2, 4 - side)]
    where = [r + core for r in row_blocks] + [r + 1 - core for r in row_blocks]
    where += [core, lax.axis_index(BETA), lax.axis_index(ALPHA), 2 - 2 * low]
    where = jnp.stack(where).astype(jnp.int32)
    cols = jnp.concatenate([beta_cols[0], alpha_cols[0]])

    pair_t = pair_beta.T
    mate = swapped(coef, "c", 1)
    pair_mate = swapped(pair_t, "c", 1)
    coef_v, pair_v = loaded(coef, pair_t)

    below = rotated(coef_v, BETA, 2)
    above = rotated(coef_v, BETA, -2)
    xs, route = lax.axis_size("x"), []
    for i in range(xs):
        route += [(2 * i, 2 * ((i + 1) % xs)), (2 * i + 1, 2 * ((i - 1) % xs) + 1)]

    parts = density_parts(where, coef_v, mate, pair_v, pair_mate)
    coupling, scale, placed = staged(
        where, cols, pair_coupling, pair_alpha.T, beta_ops, parts[0]
    )
    turns = (None, crossing((1, 3)), crossing((2, 2)), crossing((3, 1)))
    got = [lax.ppermute(parts[k], ("y", "c"), turns[k]) for k in (1, 3, 2)]
    *got, below = lax.optimization_barrier((*got, below))
    near = swapped(coef_v, "zl", 1)
    total = parts[0].astype(F32)
    for part in got:
        total = total + part.astype(F32)
    total = total.astype(BF16)
    total, coupling, scale, placed = lax.optimization_barrier((total, coupling, scale, placed))

    far = lax.ppermute(near, ALPHA, route)
    first = lax.ppermute(total, ("zh", "c"), turns[1])
    sent, _ = lax.optimization_barrier((pair_v, total))
    beside = lax.ppermute(sent, ("y", "c"), turns[1])
    crossed = swapped(jnp.where(core == 0, above, below), "c", 1)
    first, beside = lax.optimization_barrier((first, beside))
    total = (total.astype(F32) + first.astype(F32)).astype(BF16)
    total, crossed = lax.optimization_barrier((total, crossed))
    beyond = lax.ppermute(jnp.stack([pair_v, beside]), ("y", "c"), turns[3])
    second = lax.ppermute(total, ("zh", "c"), turns[3])
    same = same_spin_beta([below, crossed, coef_v, mate, above], placed)
    around = [coef_v, near, far]
    same, picked = same_spin_alpha(where, cols, around, alpha_ops, same)
    second, same = lax.optimization_barrier((second, same))

    excited = excited_block(total, second, coupling, scale)
    mine, *out = mixed_blocks(excited, swapped(excited, "c", 1), pair_v, beside, beyond)
    back = [lax.ppermute(out[k - 1], ("y", "c"), turns[k]) for k in (1, 2, 3)]
    same = rest_of_alpha(picked, alpha_ops, same)
    *back, same = lax.optimization_barrier((*back, same))
    return finished(where, same, [mine, *back], denominators)


def solution(mesh):
    finer = Mesh(mesh.devices.reshape(4, 2, 4, 4, 2), (*ALPHA, *BETA))
    placed = (
        P(ALPHA, BETA),
        P(BETA, None),
        P(BETA, None),
        P(ALPHA, None),
        P(ALPHA, None),
        P(ALPHA, None),
        P(BETA, None),
        P(),
        P(ALPHA, BETA),
    )
    return jax.shard_map(
        local, mesh=finer, in_specs=placed, out_specs=P(ALPHA, BETA), check_vma=False
    )
```

```python
import jax
import jax.numpy as jnp
from jax import lax
from jax.experimental import pallas as pl
from jax.experimental.pallas import tpu as pltpu
from jax.sharding import Mesh
from jax.sharding import PartitionSpec as P

ALPHA = ("x", "zl")
BETA = ("y", "zh", "c")
F32 = jnp.float32
BF16 = jnp.bfloat16
SMEM = pl.BlockSpec(memory_space=pltpu.SMEM)
VMEM = pl.BlockSpec(memory_space=pltpu.VMEM)
HBM = pl.BlockSpec(memory_space=pltpu.HBM)
ANY = pl.BlockSpec(memory_space=pl.ANY)
MIB = 1 << 20


def dot(a, b, dims=((1,), (0,))):
    return lax.dot_general(a, b, (dims, ((), ())), preferred_element_type=F32)


def swapped(block, axis, mask):
    count = lax.axis_size(axis)
    return lax.ppermute(block, axis, [(i, i ^ mask) for i in range(count)])


def rotated(block, axis, distance):
    count = lax.axis_size(axis)
    return lax.ppermute(block, axis, [(i, (i + distance) % count) for i in range(count)])


def crossing(masks):
    return [(2 * i + h, 2 * (i ^ masks[h]) + h) for i in range(4) for h in (0, 1)]


def call(kernel, outs, args, specs, cost, scratch=(), aliases=None, out_specs=None, limit=16):
    args = [
        pltpu.with_memory_space_constraint(arg, pltpu.HBM) if spec is HBM else arg
        for arg, spec in zip(args, specs)
    ]
    return pl.pallas_call(
        kernel,
        out_shape=outs,
        in_specs=specs,
        out_specs=out_specs or [VMEM] * len(outs),
        scratch_shapes=list(scratch),
        input_output_aliases=aliases or {},
        compiler_params=pltpu.CompilerParams(vmem_limit_bytes=limit * MIB),
        cost_estimate=pl.CostEstimate(flops=cost[0], bytes_accessed=cost[1], transcendentals=0),
        name=kernel.__name__,
    )(*args)


def shape(dims, kind=BF16):
    return jax.ShapeDtypeStruct(dims, kind)


def block_rows(where_ref, k, width):
    return pl.ds(pl.multiple_of(where_ref[k] * width, width), width)


def loaded(coef, pair_t):
    def loaded_kernel(coef_ref, pair_ref, coef_out, pair_out, sems):
        copies = [
            pltpu.make_async_copy(coef_ref, coef_out, sems.at[0]),
            pltpu.make_async_copy(pair_ref, pair_out, sems.at[1]),
        ]
        for copy in copies:
            copy.start()
        for copy in copies:
            copy.wait()

    return call(
        loaded_kernel,
        [shape(coef.shape), shape(pair_t.shape)],
        (coef, pair_t),
        [HBM, HBM],
        (0, 1 * MIB),
        [pltpu.SemaphoreType.DMA((2,))],
    )


def density_parts(where, own, mate, pair_own, pair_mate):
    pairs, width = pair_mate.shape

    def density_parts_kernel(where_ref, own_ref, mate_ref, po_ref, pm_ref, *outs):
        left = jnp.concatenate([po_ref[...], pm_ref[...]], axis=1)
        for k, out in enumerate(outs):
            rows = block_rows(where_ref, k, width)
            right = jnp.concatenate([own_ref[rows, :], mate_ref[rows, :]], axis=1)
            out[...] = dot(left, right, ((1,), (1,))).astype(BF16)

    return call(
        density_parts_kernel,
        [shape((pairs, width))] * 4,
        (where, own, mate, pair_own, pair_mate),
        [SMEM] + [VMEM] * 4,
        (16 * pairs * width * width, 1 * MIB),
    )


def staged(where, cols, coupling, pair_alpha_t, beta_ops, tie):
    pairs, width = coupling.shape[0], beta_ops.shape[0]
    listed = beta_ops.shape[1] // width
    count = lax.axis_size(BETA)

    def staged_kernel(
        where_ref, cols_ref, c_ref, pa_ref, ops_ref, tie_ref, c_out, pa_out, w_out, pa_v, ops_v, sems
    ):
        rows = block_rows(where_ref, 0, width)
        copies = [
            pltpu.make_async_copy(ops_ref, ops_v, sems.at[0]),
            pltpu.make_async_copy(pa_ref.at[:, rows], pa_v, sems.at[1]),
            pltpu.make_async_copy(c_ref, c_out, sems.at[2]),
        ]
        for copy in copies:
            copy.start()
        copies[0].wait()
        core = where_ref[8]
        for n in range(5):
            offset = n if n in (0, 2, 4) else jnp.where(core == 0, n, 4 - n)
            tile = jnp.zeros((width, width), F32)
            for k in range(listed):
                here = lax.rem(cols_ref[k] - where_ref[9] + 2 + count, count)
                part = ops_v[:, k * width : (k + 1) * width].astype(F32)
                tile = jnp.where(here == offset, part, tile)
            w_out[:, n * width : (n + 1) * width] = tile.astype(BF16)
        copies[1].wait()
        pa_out[...] = pa_v[...].astype(F32).T
        copies[2].wait()

    return call(
        staged_kernel,
        [shape(coupling.shape), shape((width, pairs), F32), shape((width, 5 * width))],
        (where, cols, coupling, pair_alpha_t, beta_ops, tie),
        [SMEM, SMEM, HBM, HBM, HBM, ANY],
        (pairs * pairs, 2 * MIB),
        [
            pltpu.VMEM((pairs, width), BF16),
            pltpu.VMEM(beta_ops.shape, BF16),
            pltpu.SemaphoreType.DMA((3,)),
        ],
    )


def excited_block(near, far, coupling, scale):
    pairs, width = near.shape

    def excited_block_kernel(near_ref, far_ref, coupling_ref, scale_ref, out_ref):
        total = near_ref[...].astype(F32) + far_ref[...].astype(F32)
        density = total.T.astype(BF16)
        out_ref[...] = (dot(density, coupling_ref[...]) * scale_ref[...]).astype(BF16)

    return call(
        excited_block_kernel,
        [shape((width, pairs))],
        (near, far, coupling, scale),
        [VMEM] * 4,
        (2 * pairs * pairs * width, 2 * MIB),
    )[0]


def mixed_blocks(own, mate, pair_own, beside, beyond):
    width = own.shape[0]

    def mixed_blocks_kernel(own_ref, mate_ref, pair_ref, beside_ref, beyond_ref, *outs):
        rights = (pair_ref[...], beside_ref[...], beyond_ref[1], beyond_ref[0])
        for half, rows in enumerate((own_ref, mate_ref)):
            for out, right in zip(outs, rights):
                out[half] = dot(rows[...], right).astype(out.dtype)

    return call(
        mixed_blocks_kernel,
        [shape((2, width, width), F32)] + [shape((2, width, width))] * 3,
        (own, mate, pair_own, beside, beyond),
        [VMEM] * 5,
        (16 * own.size * width, 1 * MIB),
    )


def finished(where, same, parts, denominators):
    rows, width = same.shape

    def finished_kernel(where_ref, same_ref, m0, m1, m2, m3, den_ref, out, held, sems):
        copies = []
        for k, part in enumerate((m0, m1, m2, m3)):
            for half in (0, 1):
                n = 2 * k + half
                at = block_rows(where_ref, k + 4 * half, width)
                held[n] = (same_ref[at, :] + part[half].astype(F32)) / den_ref[at, :]
                copies.append(pltpu.make_async_copy(held.at[n], out.at[at, :], sems.at[n]))
                copies[-1].start()
        for copy in copies:
            copy.wait()

    return call(
        finished_kernel,
        [shape((rows, width), F32)],
        (where, same, *parts, denominators),
        [SMEM] + [VMEM] * 6,
        (rows * width * 2, 2 * MIB),
        [pltpu.VMEM((8, width, width), F32), pltpu.SemaphoreType.DMA((8,))],
        out_specs=[HBM],
    )[0]


def same_spin_beta(blocks, placed):
    rows, width = blocks[0].shape

    def same_spin_beta_kernel(b0, b1, b2, b3, b4, w_ref, out_ref):
        left = jnp.concatenate([b[...] for b in (b0, b1, b2, b3, b4)], axis=1)
        out_ref[...] = dot(left, w_ref[...], ((1,), (1,)))

    return call(
        same_spin_beta_kernel,
        [shape((rows, width), F32)],
        (*blocks, placed),
        [VMEM] * 6,
        (2 * rows * width * width * 5, 2 * MIB),
        limit=24,
    )[0]


def alpha_rows(ops_ref, picked, start_ref, out_ref, ops_v, sems, part, select):
    step = ops_v.shape[1]
    half = start_ref.shape[0] // 2
    mine = range(part * half, (part + 1) * half, step)
    rest = slice((1 - part) * half, (2 - part) * half)
    copies = [
        pltpu.make_async_copy(ops_ref.at[r : r + step, :], ops_v.at[n], sems.at[n])
        for n, r in enumerate(mine)
    ]
    for copy in copies:
        copy.start()
    select()
    out_ref[rest, :] = start_ref[rest, :]
    for n, r in enumerate(mine):
        copies[n].wait()
        at = slice(r, r + step)
        out_ref[at, :] = start_ref[at, :] + dot(ops_v[n], picked[...])


def same_spin_alpha(where, cols, blocks, alpha_ops, start):
    rows, width = start.shape
    depth = blocks[0].shape[0]
    span = alpha_ops.shape[1]
    count = lax.axis_size(ALPHA)

    def same_spin_alpha_kernel(
        where_ref, cols_ref, own_ref, near_ref, far_ref, ops_ref, start_ref, out_ref, picked, ops_v, sems
    ):
        def select():
            for k in range(span // depth):
                offset = lax.rem(cols_ref[4 + k] - where_ref[10] + 1 + count, count)
                picked[k * depth : (k + 1) * depth, :] = jnp.where(
                    offset == 1,
                    own_ref[...],
                    jnp.where(offset == where_ref[11], near_ref[...], far_ref[...]),
                )

        alpha_rows(ops_ref, picked, start_ref, out_ref, ops_v, sems, 0, select)

    return call(
        same_spin_alpha_kernel,
        [shape((rows, width), F32), shape((span, width))],
        (where, cols, *blocks, alpha_ops, start),
        [SMEM, SMEM] + [VMEM] * 3 + [HBM, VMEM],
        (rows * width * depth * 4, 5 * MIB),
        [pltpu.VMEM((2, rows // 4, span), BF16), pltpu.SemaphoreType.DMA((2,))],
    )


def rest_of_alpha(picked, alpha_ops, start):
    rows, width = start.shape
    span = alpha_ops.shape[1]

    def rest_of_alpha_kernel(picked, ops_ref, start_ref, out_ref, ops_v, sems):
        alpha_rows(ops_ref, picked, start_ref, out_ref, ops_v, sems, 1, lambda: None)

    return call(
        rest_of_alpha_kernel,
        [shape((rows, width), F32)],
        (picked, alpha_ops, start),
        [VMEM, HBM, VMEM],
        (rows * width * span, 5 * MIB),
        [pltpu.VMEM((2, rows // 4, span), BF16), pltpu.SemaphoreType.DMA((2,))],
    )[0]


def local(
    coef,
    beta_ops,
    beta_cols,
    alpha_ops,
    alpha_cols,
    pair_alpha,
    pair_beta,
    pair_coupling,
    denominators,
):
    y, core = lax.axis_index("y"), lax.axis_index("c")
    low = lax.axis_index("zl")
    side = 1 + 2 * core
    row_blocks = [(y ^ m) * 2 for m in (0, side, 2, 4 - side)]
    where = [r + core for r in row_blocks] + [r + 1 - core for r in row_blocks]
    where += [core, lax.axis_index(BETA), lax.axis_index(ALPHA), 2 - 2 * low]
    where = jnp.stack(where).astype(jnp.int32)
    cols = jnp.concatenate([beta_cols[0], alpha_cols[0]])

    pair_t = pair_beta.T
    mate = swapped(coef, "c", 1)
    pair_mate = swapped(pair_t, "c", 1)
    coef_v, pair_v = loaded(coef, pair_t)

    below = rotated(coef_v, BETA, 2)
    above = rotated(coef_v, BETA, -2)
    xs, route = lax.axis_size("x"), []
    for i in range(xs):
        route += [(2 * i, 2 * ((i + 1) % xs)), (2 * i + 1, 2 * ((i - 1) % xs) + 1)]

    parts = density_parts(where, coef_v, mate, pair_v, pair_mate)
    coupling, scale, placed = staged(
        where, cols, pair_coupling, pair_alpha.T, beta_ops, parts[0]
    )
    turns = (None, crossing((1, 3)), crossing((2, 2)), crossing((3, 1)))
    got = [lax.ppermute(parts[k], ("y", "c"), turns[k]) for k in (1, 3, 2)]
    *got, below, above = lax.optimization_barrier((*got, below, above))
    near = swapped(coef_v, "zl", 1)
    total = parts[0].astype(F32)
    for part in got:
        total = total + part.astype(F32)
    total = total.astype(BF16)
    total, coupling, scale, placed = lax.optimization_barrier((total, coupling, scale, placed))

    far = lax.ppermute(near, ALPHA, route)
    first = lax.ppermute(total, ("zh", "c"), turns[1])
    sent, _ = lax.optimization_barrier((pair_v, total))
    beside = lax.ppermute(sent, ("y", "c"), turns[1])
    crossed = swapped(jnp.where(core == 0, above, below), "c", 1)
    first, beside = lax.optimization_barrier((first, beside))
    total = (total.astype(F32) + first.astype(F32)).astype(BF16)
    total, crossed = lax.optimization_barrier((total, crossed))
    beyond = lax.ppermute(jnp.stack([pair_v, beside]), ("y", "c"), turns[3])
    second = lax.ppermute(total, ("zh", "c"), turns[3])
    same = same_spin_beta([below, crossed, coef_v, mate, above], placed)
    around = [coef_v, near, far]
    same, picked = same_spin_alpha(where, cols, around, alpha_ops, same)
    second, same = lax.optimization_barrier((second, same))

    excited = excited_block(total, second, coupling, scale)
    mine, *out = mixed_blocks(excited, swapped(excited, "c", 1), pair_v, beside, beyond)
    back = [lax.ppermute(out[k - 1], ("y", "c"), turns[k]) for k in (1, 2, 3)]
    same = rest_of_alpha(picked, alpha_ops, same)
    *back, same = lax.optimization_barrier((*back, same))
    return finished(where, same, [mine, *back], denominators)


def solution(mesh):
    finer = Mesh(mesh.devices.reshape(4, 2, 4, 4, 2), (*ALPHA, *BETA))
    placed = (
        P(ALPHA, BETA),
        P(BETA, None),
        P(BETA, None),
        P(ALPHA, None),
        P(ALPHA, None),
        P(ALPHA, None),
        P(BETA, None),
        P(),
        P(ALPHA, BETA),
    )
    return jax.shard_map(
        local, mesh=finer, in_specs=placed, out_specs=P(ALPHA, BETA), check_vma=False
    )
```

```python
import jax
import jax.numpy as jnp
from jax import lax
from jax.experimental import pallas as pl
from jax.experimental.pallas import tpu as pltpu
from jax.sharding import Mesh
from jax.sharding import PartitionSpec as P

ALPHA = ("x", "zl")
BETA = ("y", "zh", "c")
F32 = jnp.float32
BF16 = jnp.bfloat16
SMEM = pl.BlockSpec(memory_space=pltpu.SMEM)
VMEM = pl.BlockSpec(memory_space=pltpu.VMEM)
HBM = pl.BlockSpec(memory_space=pltpu.HBM)
ANY = pl.BlockSpec(memory_space=pl.ANY)
MIB = 1 << 20


def dot(a, b, dims=((1,), (0,))):
    return lax.dot_general(a, b, (dims, ((), ())), preferred_element_type=F32)


def swapped(block, axis, mask):
    count = lax.axis_size(axis)
    return lax.ppermute(block, axis, [(i, i ^ mask) for i in range(count)])


def rotated(block, axis, distance):
    count = lax.axis_size(axis)
    return lax.ppermute(block, axis, [(i, (i + distance) % count) for i in range(count)])


def crossing(masks):
    return [(2 * i + h, 2 * (i ^ masks[h]) + h) for i in range(4) for h in (0, 1)]


def call(kernel, outs, args, specs, cost, scratch=(), aliases=None, out_specs=None, limit=16):
    args = [
        pltpu.with_memory_space_constraint(arg, pltpu.HBM) if spec is HBM else arg
        for arg, spec in zip(args, specs)
    ]
    return pl.pallas_call(
        kernel,
        out_shape=outs,
        in_specs=specs,
        out_specs=out_specs or [VMEM] * len(outs),
        scratch_shapes=list(scratch),
        input_output_aliases=aliases or {},
        compiler_params=pltpu.CompilerParams(vmem_limit_bytes=limit * MIB),
        cost_estimate=pl.CostEstimate(flops=cost[0], bytes_accessed=cost[1], transcendentals=0),
        name=kernel.__name__,
    )(*args)


def shape(dims, kind=BF16):
    return jax.ShapeDtypeStruct(dims, kind)


def block_rows(where_ref, k, width):
    return pl.ds(pl.multiple_of(where_ref[k] * width, width), width)


def loaded(coef, pair_t):
    def loaded_kernel(coef_ref, pair_ref, coef_out, pair_out, sems):
        copies = [
            pltpu.make_async_copy(coef_ref, coef_out, sems.at[0]),
            pltpu.make_async_copy(pair_ref, pair_out, sems.at[1]),
        ]
        for copy in copies:
            copy.start()
        for copy in copies:
            copy.wait()

    return call(
        loaded_kernel,
        [shape(coef.shape), shape(pair_t.shape)],
        (coef, pair_t),
        [HBM, HBM],
        (0, 1 * MIB),
        [pltpu.SemaphoreType.DMA((2,))],
    )


def density_parts(where, own, mate, pair_own, pair_mate):
    pairs, width = pair_mate.shape

    def density_parts_kernel(where_ref, own_ref, mate_ref, po_ref, pm_ref, *outs):
        left = jnp.concatenate([po_ref[...], pm_ref[...]], axis=1)
        for k, out in enumerate(outs):
            rows = block_rows(where_ref, k, width)
            right = jnp.concatenate([own_ref[rows, :], mate_ref[rows, :]], axis=1)
            part = dot(left, right, ((1,), (1,))).astype(BF16)
            if k == 1:
                out[0] = part
                out[1] = po_ref[...]
            else:
                out[...] = part

    one = shape((pairs, width))
    return call(
        density_parts_kernel,
        [one, shape((2, pairs, width)), one, one],
        (where, own, mate, pair_own, pair_mate),
        [SMEM] + [VMEM] * 4,
        (16 * pairs * width * width, 1 * MIB),
    )


def staged(where, cols, coupling, pair_alpha_t, beta_ops, tie):
    pairs, width = coupling.shape[0], beta_ops.shape[0]
    listed = beta_ops.shape[1] // width
    count = lax.axis_size(BETA)

    def staged_kernel(
        where_ref, cols_ref, c_ref, pa_ref, ops_ref, tie_ref, c_out, pa_out, w_out, pa_v, ops_v, sems
    ):
        rows = block_rows(where_ref, 0, width)
        copies = [
            pltpu.make_async_copy(ops_ref, ops_v, sems.at[0]),
            pltpu.make_async_copy(pa_ref.at[:, rows], pa_v, sems.at[1]),
            pltpu.make_async_copy(c_ref, c_out, sems.at[2]),
        ]
        for copy in copies:
            copy.start()
        copies[0].wait()
        core = where_ref[8]
        for n in range(5):
            offset = n if n in (0, 2, 4) else jnp.where(core == 0, n, 4 - n)
            tile = jnp.zeros((width, width), F32)
            for k in range(listed):
                here = lax.rem(cols_ref[k] - where_ref[9] + 2 + count, count)
                part = ops_v[:, k * width : (k + 1) * width].astype(F32)
                tile = jnp.where(here == offset, part, tile)
            w_out[:, n * width : (n + 1) * width] = tile.astype(BF16)
        copies[1].wait()
        pa_out[...] = pa_v[...].astype(F32).T
        copies[2].wait()

    return call(
        staged_kernel,
        [shape(coupling.shape), shape((width, pairs), F32), shape((width, 5 * width))],
        (where, cols, coupling, pair_alpha_t, beta_ops, tie),
        [SMEM, SMEM, HBM, HBM, HBM, ANY],
        (pairs * pairs, 2 * MIB),
        [
            pltpu.VMEM((pairs, width), BF16),
            pltpu.VMEM(beta_ops.shape, BF16),
            pltpu.SemaphoreType.DMA((3,)),
        ],
    )


def excited_block(near, far, coupling, scale):
    pairs, width = near.shape

    def excited_block_kernel(near_ref, far_ref, coupling_ref, scale_ref, out_ref):
        total = near_ref[...].astype(F32) + far_ref[...].astype(F32)
        density = total.T.astype(BF16)
        out_ref[...] = (dot(density, coupling_ref[...]) * scale_ref[...]).astype(BF16)

    return call(
        excited_block_kernel,
        [shape((width, pairs))],
        (near, far, coupling, scale),
        [VMEM] * 4,
        (2 * pairs * pairs * width, 2 * MIB),
    )[0]


def mixed_blocks(own, mate, pair_own, beside, beyond):
    width = own.shape[0]

    def mixed_blocks_kernel(own_ref, mate_ref, pair_ref, beside_ref, beyond_ref, *outs):
        rights = (pair_ref[...], beside_ref[...], beyond_ref[1], beyond_ref[0])
        for half, rows in enumerate((own_ref, mate_ref)):
            for out, right in zip(outs, rights):
                out[half] = dot(rows[...], right).astype(out.dtype)

    return call(
        mixed_blocks_kernel,
        [shape((2, width, width), F32)] + [shape((2, width, width))] * 3,
        (own, mate, pair_own, beside, beyond),
        [VMEM] * 5,
        (16 * own.size * width, 1 * MIB),
    )


def finished(where, same, parts, denominators):
    rows, width = same.shape

    def finished_kernel(where_ref, same_ref, m0, m1, m2, m3, den_ref, out, held, sems):
        copies = []
        for k, part in enumerate((m0, m1, m2, m3)):
            for half in (0, 1):
                n = 2 * k + half
                at = block_rows(where_ref, k + 4 * half, width)
                held[n] = (same_ref[at, :] + part[half].astype(F32)) / den_ref[at, :]
                copies.append(pltpu.make_async_copy(held.at[n], out.at[at, :], sems.at[n]))
                copies[-1].start()
        for copy in copies:
            copy.wait()

    return call(
        finished_kernel,
        [shape((rows, width), F32)],
        (where, same, *parts, denominators),
        [SMEM] + [VMEM] * 6,
        (rows * width * 2, 2 * MIB),
        [pltpu.VMEM((8, width, width), F32), pltpu.SemaphoreType.DMA((8,))],
        out_specs=[HBM],
    )[0]


def same_spin_beta(blocks, placed):
    rows, width = blocks[0].shape

    def same_spin_beta_kernel(b0, b1, b2, b3, b4, w_ref, out_ref):
        left = jnp.concatenate([b[...] for b in (b0, b1, b2, b3, b4)], axis=1)
        out_ref[...] = dot(left, w_ref[...], ((1,), (1,)))

    return call(
        same_spin_beta_kernel,
        [shape((rows, width), F32)],
        (*blocks, placed),
        [VMEM] * 6,
        (2 * rows * width * width * 5, 2 * MIB),
        limit=24,
    )[0]


def alpha_rows(ops_ref, picked, start_ref, out_ref, ops_v, sems, part, select):
    step = ops_v.shape[1]
    half = start_ref.shape[0] // 2
    mine = range(part * half, (part + 1) * half, step)
    rest = slice((1 - part) * half, (2 - part) * half)
    copies = [
        pltpu.make_async_copy(ops_ref.at[r : r + step, :], ops_v.at[n], sems.at[n])
        for n, r in enumerate(mine)
    ]
    for copy in copies:
        copy.start()
    select()
    out_ref[rest, :] = start_ref[rest, :]
    for n, r in enumerate(mine):
        copies[n].wait()
        at = slice(r, r + step)
        out_ref[at, :] = start_ref[at, :] + dot(ops_v[n], picked[...])


def same_spin_alpha(where, cols, blocks, alpha_ops, start):
    rows, width = start.shape
    depth = blocks[0].shape[0]
    span = alpha_ops.shape[1]
    count = lax.axis_size(ALPHA)

    def same_spin_alpha_kernel(
        where_ref, cols_ref, own_ref, near_ref, far_ref, ops_ref, start_ref, out_ref, picked, ops_v, sems
    ):
        def select():
            for k in range(span // depth):
                offset = lax.rem(cols_ref[4 + k] - where_ref[10] + 1 + count, count)
                picked[k * depth : (k + 1) * depth, :] = jnp.where(
                    offset == 1,
                    own_ref[...],
                    jnp.where(offset == where_ref[11], near_ref[...], far_ref[...]),
                )

        alpha_rows(ops_ref, picked, start_ref, out_ref, ops_v, sems, 0, select)

    return call(
        same_spin_alpha_kernel,
        [shape((rows, width), F32), shape((span, width))],
        (where, cols, *blocks, alpha_ops, start),
        [SMEM, SMEM] + [VMEM] * 3 + [HBM, VMEM],
        (rows * width * depth * 4, 5 * MIB),
        [pltpu.VMEM((2, rows // 4, span), BF16), pltpu.SemaphoreType.DMA((2,))],
    )


def rest_of_alpha(picked, alpha_ops, start):
    rows, width = start.shape
    span = alpha_ops.shape[1]

    def rest_of_alpha_kernel(picked, ops_ref, start_ref, out_ref, ops_v, sems):
        alpha_rows(ops_ref, picked, start_ref, out_ref, ops_v, sems, 1, lambda: None)

    return call(
        rest_of_alpha_kernel,
        [shape((rows, width), F32)],
        (picked, alpha_ops, start),
        [VMEM, HBM, VMEM],
        (rows * width * span, 5 * MIB),
        [pltpu.VMEM((2, rows // 4, span), BF16), pltpu.SemaphoreType.DMA((2,))],
    )[0]


def local(
    coef,
    beta_ops,
    beta_cols,
    alpha_ops,
    alpha_cols,
    pair_alpha,
    pair_beta,
    pair_coupling,
    denominators,
):
    y, core = lax.axis_index("y"), lax.axis_index("c")
    low = lax.axis_index("zl")
    side = 1 + 2 * core
    row_blocks = [(y ^ m) * 2 for m in (0, side, 2, 4 - side)]
    where = [r + core for r in row_blocks] + [r + 1 - core for r in row_blocks]
    where += [core, lax.axis_index(BETA), lax.axis_index(ALPHA), 2 - 2 * low]
    where = jnp.stack(where).astype(jnp.int32)
    cols = jnp.concatenate([beta_cols[0], alpha_cols[0]])

    pair_t = pair_beta.T
    mate = swapped(coef, "c", 1)
    pair_mate = swapped(pair_t, "c", 1)
    coef_v, pair_v = loaded(coef, pair_t)

    below = rotated(coef_v, BETA, 2)
    above = rotated(coef_v, BETA, -2)
    xs, route = lax.axis_size("x"), []
    for i in range(xs):
        route += [(2 * i, 2 * ((i + 1) % xs)), (2 * i + 1, 2 * ((i - 1) % xs) + 1)]

    parts = density_parts(where, coef_v, mate, pair_v, pair_mate)
    coupling, scale, placed = staged(
        where, cols, pair_coupling, pair_alpha.T, beta_ops, parts[0]
    )
    turns = (None, crossing((1, 3)), crossing((2, 2)), crossing((3, 1)))
    both = lax.ppermute(parts[1], ("y", "c"), turns[1])
    other = lax.ppermute(parts[3], ("y", "c"), turns[3])
    across, other = lax.optimization_barrier((parts[2], other))
    got = [both, other, lax.ppermute(across, ("y", "c"), turns[2])]
    near = swapped(coef_v, "zl", 1)
    *got, below, above, near = lax.optimization_barrier((*got, below, above, near))
    got[0], beside = got[0][0], got[0][1]
    total = parts[0].astype(F32)
    for part in got:
        total = total + part.astype(F32)
    total = total.astype(BF16)
    total, coupling, scale, placed = lax.optimization_barrier((total, coupling, scale, placed))

    far = lax.ppermute(near, ALPHA, route)
    first = lax.ppermute(total, ("zh", "c"), turns[1])
    crossed = swapped(jnp.where(core == 0, above, below), "c", 1)
    total = (total.astype(F32) + first.astype(F32)).astype(BF16)
    total, crossed = lax.optimization_barrier((total, crossed))
    beyond = lax.ppermute(jnp.stack([pair_v, beside]), ("y", "c"), turns[3])
    second = lax.ppermute(total, ("zh", "c"), turns[3])
    same = same_spin_beta([below, crossed, coef_v, mate, above], placed)
    around = [coef_v, near, far]
    same, picked = same_spin_alpha(where, cols, around, alpha_ops, same)
    second, same = lax.optimization_barrier((second, same))

    excited = excited_block(total, second, coupling, scale)
    mine, *out = mixed_blocks(excited, swapped(excited, "c", 1), pair_v, beside, beyond)
    back = [lax.ppermute(out[k - 1], ("y", "c"), turns[k]) for k in (1, 2, 3)]
    same = rest_of_alpha(picked, alpha_ops, same)
    *back, same = lax.optimization_barrier((*back, same))
    return finished(where, same, [mine, *back], denominators)


def solution(mesh):
    finer = Mesh(mesh.devices.reshape(4, 2, 4, 4, 2), (*ALPHA, *BETA))
    placed = (
        P(ALPHA, BETA),
        P(BETA, None),
        P(BETA, None),
        P(ALPHA, None),
        P(ALPHA, None),
        P(ALPHA, None),
        P(BETA, None),
        P(),
        P(ALPHA, BETA),
    )
    return jax.shard_map(
        local, mesh=finer, in_specs=placed, out_specs=P(ALPHA, BETA), check_vma=False
    )
```

```python
import jax
import jax.numpy as jnp
from jax import lax
from jax.experimental import pallas as pl
from jax.experimental.pallas import tpu as pltpu
from jax.sharding import Mesh
from jax.sharding import PartitionSpec as P

ALPHA = ("x", "zl")
BETA = ("y", "zh", "c")
F32 = jnp.float32
BF16 = jnp.bfloat16
SMEM = pl.BlockSpec(memory_space=pltpu.SMEM)
VMEM = pl.BlockSpec(memory_space=pltpu.VMEM)
HBM = pl.BlockSpec(memory_space=pltpu.HBM)
ANY = pl.BlockSpec(memory_space=pl.ANY)
MIB = 1 << 20


def dot(a, b, dims=((1,), (0,))):
    return lax.dot_general(a, b, (dims, ((), ())), preferred_element_type=F32)


def swapped(block, axis, mask):
    count = lax.axis_size(axis)
    return lax.ppermute(block, axis, [(i, i ^ mask) for i in range(count)])


def rotated(block, axis, distance):
    count = lax.axis_size(axis)
    return lax.ppermute(block, axis, [(i, (i + distance) % count) for i in range(count)])


def crossing(masks):
    return [(2 * i + h, 2 * (i ^ masks[h]) + h) for i in range(4) for h in (0, 1)]


def call(kernel, outs, args, specs, cost, scratch=(), aliases=None, out_specs=None, limit=16):
    args = [
        pltpu.with_memory_space_constraint(arg, pltpu.HBM) if spec is HBM else arg
        for arg, spec in zip(args, specs)
    ]
    return pl.pallas_call(
        kernel,
        out_shape=outs,
        in_specs=specs,
        out_specs=out_specs or [VMEM] * len(outs),
        scratch_shapes=list(scratch),
        input_output_aliases=aliases or {},
        compiler_params=pltpu.CompilerParams(vmem_limit_bytes=limit * MIB),
        cost_estimate=pl.CostEstimate(flops=cost[0], bytes_accessed=cost[1], transcendentals=0),
        name=kernel.__name__,
    )(*args)


def shape(dims, kind=BF16):
    return jax.ShapeDtypeStruct(dims, kind)


def block_rows(where_ref, k, width):
    return pl.ds(pl.multiple_of(where_ref[k] * width, width), width)


def loaded(coef, pair_t):
    def loaded_kernel(coef_ref, pair_ref, coef_out, pair_out, sems):
        copies = [
            pltpu.make_async_copy(coef_ref, coef_out, sems.at[0]),
            pltpu.make_async_copy(pair_ref, pair_out, sems.at[1]),
        ]
        for copy in copies:
            copy.start()
        for copy in copies:
            copy.wait()

    return call(
        loaded_kernel,
        [shape(coef.shape), shape(pair_t.shape)],
        (coef, pair_t),
        [HBM, HBM],
        (0, 1 * MIB),
        [pltpu.SemaphoreType.DMA((2,))],
    )


def density_parts(where, own, mate, pair_own, pair_mate):
    pairs, width = pair_mate.shape

    def density_parts_kernel(where_ref, own_ref, mate_ref, po_ref, pm_ref, *outs):
        left = jnp.concatenate([po_ref[...], pm_ref[...]], axis=1)
        for k, out in enumerate(outs):
            rows = block_rows(where_ref, k, width)
            right = jnp.concatenate([own_ref[rows, :], mate_ref[rows, :]], axis=1)
            out[...] = dot(left, right, ((1,), (1,))).astype(BF16)

    return call(
        density_parts_kernel,
        [shape((pairs, width))] * 4,
        (where, own, mate, pair_own, pair_mate),
        [SMEM] + [VMEM] * 4,
        (16 * pairs * width * width, 1 * MIB),
    )


def staged(where, cols, coupling, pair_alpha_t, beta_ops, tie):
    pairs, width = coupling.shape[0], beta_ops.shape[0]
    listed = beta_ops.shape[1] // width
    count = lax.axis_size(BETA)

    def staged_kernel(
        where_ref, cols_ref, c_ref, pa_ref, ops_ref, tie_ref, c_out, pa_out, w_out, pa_v, ops_v, sems
    ):
        rows = block_rows(where_ref, 0, width)
        copies = [
            pltpu.make_async_copy(ops_ref, ops_v, sems.at[0]),
            pltpu.make_async_copy(pa_ref.at[:, rows], pa_v, sems.at[1]),
            pltpu.make_async_copy(c_ref, c_out, sems.at[2]),
        ]
        for copy in copies:
            copy.start()
        copies[0].wait()
        core = where_ref[8]
        for n in range(5):
            offset = n if n in (0, 2, 4) else jnp.where(core == 0, n, 4 - n)
            tile = jnp.zeros((width, width), F32)
            for k in range(listed):
                here = lax.rem(cols_ref[k] - where_ref[9] + 2 + count, count)
                part = ops_v[:, k * width : (k + 1) * width].astype(F32)
                tile = jnp.where(here == offset, part, tile)
            w_out[:, n * width : (n + 1) * width] = tile.astype(BF16)
        copies[1].wait()
        pa_out[...] = pa_v[...].astype(F32).T
        copies[2].wait()

    return call(
        staged_kernel,
        [shape(coupling.shape), shape((width, pairs), F32), shape((width, 5 * width))],
        (where, cols, coupling, pair_alpha_t, beta_ops, tie),
        [SMEM, SMEM, HBM, HBM, HBM, ANY],
        (pairs * pairs, 2 * MIB),
        [
            pltpu.VMEM((pairs, width), BF16),
            pltpu.VMEM(beta_ops.shape, BF16),
            pltpu.SemaphoreType.DMA((3,)),
        ],
    )


def excited_block(near, far, coupling, scale):
    pairs, width = near.shape

    def excited_block_kernel(near_ref, far_ref, coupling_ref, scale_ref, out_ref):
        total = near_ref[...].astype(F32) + far_ref[...].astype(F32)
        density = total.T.astype(BF16)
        out_ref[...] = (dot(density, coupling_ref[...]) * scale_ref[...]).astype(BF16)

    return call(
        excited_block_kernel,
        [shape((width, pairs))],
        (near, far, coupling, scale),
        [VMEM] * 4,
        (2 * pairs * pairs * width, 2 * MIB),
    )[0]


def mixed_blocks(own, mate, pair_own, beside, beyond):
    width = own.shape[0]

    def mixed_blocks_kernel(own_ref, mate_ref, pair_ref, beside_ref, beyond_ref, *outs):
        rights = (pair_ref[...], beside_ref[...], beyond_ref[1], beyond_ref[0])
        for half, rows in enumerate((own_ref, mate_ref)):
            for out, right in zip(outs, rights):
                out[half] = dot(rows[...], right).astype(out.dtype)

    return call(
        mixed_blocks_kernel,
        [shape((2, width, width), F32)] + [shape((2, width, width))] * 3,
        (own, mate, pair_own, beside, beyond),
        [VMEM] * 5,
        (16 * own.size * width, 1 * MIB),
    )


def finished(where, same, parts, denominators):
    rows, width = same.shape

    def finished_kernel(where_ref, same_ref, m0, m1, m2, m3, den_ref, out, held, sems):
        copies = []
        for k, part in enumerate((m0, m1, m2, m3)):
            for half in (0, 1):
                n = 2 * k + half
                at = block_rows(where_ref, k + 4 * half, width)
                held[n] = (same_ref[at, :] + part[half].astype(F32)) / den_ref[at, :]
                copies.append(pltpu.make_async_copy(held.at[n], out.at[at, :], sems.at[n]))
                copies[-1].start()
        for copy in copies:
            copy.wait()

    return call(
        finished_kernel,
        [shape((rows, width), F32)],
        (where, same, *parts, denominators),
        [SMEM] + [VMEM] * 6,
        (rows * width * 2, 2 * MIB),
        [pltpu.VMEM((8, width, width), F32), pltpu.SemaphoreType.DMA((8,))],
        out_specs=[HBM],
    )[0]


def same_spin_beta(blocks, placed):
    rows, width = blocks[0].shape

    def same_spin_beta_kernel(b0, b1, b2, b3, b4, w_ref, out_ref):
        left = jnp.concatenate([b[...] for b in (b0, b1, b2, b3, b4)], axis=1)
        out_ref[...] = dot(left, w_ref[...], ((1,), (1,)))

    return call(
        same_spin_beta_kernel,
        [shape((rows, width), F32)],
        (*blocks, placed),
        [VMEM] * 6,
        (2 * rows * width * width * 5, 2 * MIB),
        limit=24,
    )[0]


def alpha_rows(ops_ref, picked, start_ref, out_ref, ops_v, sems, part, select):
    step = ops_v.shape[1]
    half = start_ref.shape[0] // 2
    mine = range(part * half, (part + 1) * half, step)
    rest = slice((1 - part) * half, (2 - part) * half)
    copies = [
        pltpu.make_async_copy(ops_ref.at[r : r + step, :], ops_v.at[n], sems.at[n])
        for n, r in enumerate(mine)
    ]
    for copy in copies:
        copy.start()
    select()
    out_ref[rest, :] = start_ref[rest, :]
    for n, r in enumerate(mine):
        copies[n].wait()
        at = slice(r, r + step)
        out_ref[at, :] = start_ref[at, :] + dot(ops_v[n], picked[...])


def same_spin_alpha(where, cols, blocks, alpha_ops, start):
    rows, width = start.shape
    depth = blocks[0].shape[0]
    span = alpha_ops.shape[1]
    count = lax.axis_size(ALPHA)

    def same_spin_alpha_kernel(
        where_ref, cols_ref, own_ref, near_ref, far_ref, ops_ref, start_ref, out_ref, picked, ops_v, sems
    ):
        def select():
            for k in range(span // depth):
                offset = lax.rem(cols_ref[4 + k] - where_ref[10] + 1 + count, count)
                picked[k * depth : (k + 1) * depth, :] = jnp.where(
                    offset == 1,
                    own_ref[...],
                    jnp.where(offset == where_ref[11], near_ref[...], far_ref[...]),
                )

        alpha_rows(ops_ref, picked, start_ref, out_ref, ops_v, sems, 0, select)

    return call(
        same_spin_alpha_kernel,
        [shape((rows, width), F32), shape((span, width))],
        (where, cols, *blocks, alpha_ops, start),
        [SMEM, SMEM] + [VMEM] * 3 + [HBM, VMEM],
        (rows * width * depth * 4, 5 * MIB),
        [pltpu.VMEM((4, rows // 8, span), BF16), pltpu.SemaphoreType.DMA((4,))],
    )


def rest_of_alpha(picked, alpha_ops, start):
    rows, width = start.shape
    span = alpha_ops.shape[1]

    def rest_of_alpha_kernel(picked, ops_ref, start_ref, out_ref, ops_v, sems):
        alpha_rows(ops_ref, picked, start_ref, out_ref, ops_v, sems, 1, lambda: None)

    return call(
        rest_of_alpha_kernel,
        [shape((rows, width), F32)],
        (picked, alpha_ops, start),
        [VMEM, HBM, VMEM],
        (rows * width * span, 5 * MIB),
        [pltpu.VMEM((4, rows // 8, span), BF16), pltpu.SemaphoreType.DMA((4,))],
    )[0]


def local(
    coef,
    beta_ops,
    beta_cols,
    alpha_ops,
    alpha_cols,
    pair_alpha,
    pair_beta,
    pair_coupling,
    denominators,
):
    y, core = lax.axis_index("y"), lax.axis_index("c")
    low = lax.axis_index("zl")
    side = 1 + 2 * core
    row_blocks = [(y ^ m) * 2 for m in (0, side, 2, 4 - side)]
    where = [r + core for r in row_blocks] + [r + 1 - core for r in row_blocks]
    where += [core, lax.axis_index(BETA), lax.axis_index(ALPHA), 2 - 2 * low]
    where = jnp.stack(where).astype(jnp.int32)
    cols = jnp.concatenate([beta_cols[0], alpha_cols[0]])

    pair_t = pair_beta.T
    mate = swapped(coef, "c", 1)
    pair_mate = swapped(pair_t, "c", 1)
    coef_v, pair_v = loaded(coef, pair_t)

    below = rotated(coef, BETA, 2)
    above = rotated(coef, BETA, -2)
    xs, route = lax.axis_size("x"), []
    for i in range(xs):
        route += [(2 * i, 2 * ((i + 1) % xs)), (2 * i + 1, 2 * ((i - 1) % xs) + 1)]

    parts = density_parts(where, coef_v, mate, pair_v, pair_mate)
    coupling, scale, placed = staged(
        where, cols, pair_coupling, pair_alpha.T, beta_ops, parts[0]
    )
    turns = (None, crossing((1, 3)), crossing((2, 2)), crossing((3, 1)))
    got = [lax.ppermute(parts[k], ("y", "c"), turns[k]) for k in (1, 3, 2)]
    *got, below, above = lax.optimization_barrier((*got, below, above))
    near = swapped(coef, "zl", 1)
    total = parts[0].astype(F32)
    for part in got:
        total = total + part.astype(F32)
    total = total.astype(BF16)
    total, coupling, scale, placed = lax.optimization_barrier((total, coupling, scale, placed))

    far = lax.ppermute(near, ALPHA, route)
    first = lax.ppermute(total, ("zh", "c"), turns[1])
    sent, _ = lax.optimization_barrier((pair_v, total))
    beside = lax.ppermute(sent, ("y", "c"), turns[1])
    crossed = swapped(jnp.where(core == 0, above, below), "c", 1)
    first, beside = lax.optimization_barrier((first, beside))
    total = (total.astype(F32) + first.astype(F32)).astype(BF16)
    total, crossed = lax.optimization_barrier((total, crossed))
    beyond = lax.ppermute(jnp.stack([pair_v, beside]), ("y", "c"), turns[3])
    second = lax.ppermute(total, ("zh", "c"), turns[3])
    same = same_spin_beta([below, crossed, coef_v, mate, above], placed)
    around = [coef_v, near, far]
    same, picked = same_spin_alpha(where, cols, around, alpha_ops, same)
    second, same = lax.optimization_barrier((second, same))

    excited = excited_block(total, second, coupling, scale)
    mine, *out = mixed_blocks(excited, swapped(excited, "c", 1), pair_v, beside, beyond)
    back = [lax.ppermute(out[k - 1], ("y", "c"), turns[k]) for k in (1, 2, 3)]
    same = rest_of_alpha(picked, alpha_ops, same)
    *back, same = lax.optimization_barrier((*back, same))
    return finished(where, same, [mine, *back], denominators)


def solution(mesh):
    finer = Mesh(mesh.devices.reshape(4, 2, 4, 4, 2), (*ALPHA, *BETA))
    placed = (
        P(ALPHA, BETA),
        P(BETA, None),
        P(BETA, None),
        P(ALPHA, None),
        P(ALPHA, None),
        P(ALPHA, None),
        P(BETA, None),
        P(),
        P(ALPHA, BETA),
    )
    return jax.shard_map(
        local, mesh=finer, in_specs=placed, out_specs=P(ALPHA, BETA), check_vma=False
    )
```

```python
import jax
import jax.numpy as jnp
from jax import lax
from jax.experimental import pallas as pl
from jax.experimental.pallas import tpu as pltpu
from jax.sharding import Mesh
from jax.sharding import PartitionSpec as P

ALPHA = ("x", "zl")
BETA = ("y", "zh", "c")
F32 = jnp.float32
BF16 = jnp.bfloat16
SMEM = pl.BlockSpec(memory_space=pltpu.SMEM)
VMEM = pl.BlockSpec(memory_space=pltpu.VMEM)
HBM = pl.BlockSpec(memory_space=pltpu.HBM)
ANY = pl.BlockSpec(memory_space=pl.ANY)
MIB = 1 << 20


def dot(a, b, dims=((1,), (0,))):
    return lax.dot_general(a, b, (dims, ((), ())), preferred_element_type=F32)


def swapped(block, axis, mask):
    count = lax.axis_size(axis)
    return lax.ppermute(block, axis, [(i, i ^ mask) for i in range(count)])


def rotated(block, axis, distance):
    count = lax.axis_size(axis)
    return lax.ppermute(block, axis, [(i, (i + distance) % count) for i in range(count)])


def crossing(masks):
    return [(2 * i + h, 2 * (i ^ masks[h]) + h) for i in range(4) for h in (0, 1)]


def call(kernel, outs, args, specs, cost, scratch=(), aliases=None, out_specs=None, limit=16):
    args = [
        pltpu.with_memory_space_constraint(arg, pltpu.HBM) if spec is HBM else arg
        for arg, spec in zip(args, specs)
    ]
    return pl.pallas_call(
        kernel,
        out_shape=outs,
        in_specs=specs,
        out_specs=out_specs or [VMEM] * len(outs),
        scratch_shapes=list(scratch),
        input_output_aliases=aliases or {},
        compiler_params=pltpu.CompilerParams(vmem_limit_bytes=limit * MIB),
        cost_estimate=pl.CostEstimate(flops=cost[0], bytes_accessed=cost[1], transcendentals=0),
        name=kernel.__name__,
    )(*args)


def shape(dims, kind=BF16):
    return jax.ShapeDtypeStruct(dims, kind)


def block_rows(where_ref, k, width):
    return pl.ds(pl.multiple_of(where_ref[k] * width, width), width)


def density_parts(where, coef, mate, pair_t, pair_mate):
    pairs, width = pair_mate.shape

    def density_parts_kernel(
        where_ref, coef_ref, mate_ref, pair_ref, pm_ref, o0, o1, o2, o3, coef_out, pair_out, acc, sems
    ):
        copies = [
            pltpu.make_async_copy(coef_ref, coef_out, sems.at[0]),
            pltpu.make_async_copy(pair_ref, pair_out, sems.at[1]),
        ]
        for copy in copies:
            copy.start()
        left = pm_ref[...]
        for k in range(4):
            rows = block_rows(where_ref, k, width)
            acc[k] = dot(left, mate_ref[rows, :], ((1,), (1,)))
        for copy in copies:
            copy.wait()
        left = pair_out[...]
        for k, out in enumerate((o0, o1, o2, o3)):
            rows = block_rows(where_ref, k, width)
            out[...] = (acc[k] + dot(left, coef_out[rows, :], ((1,), (1,)))).astype(BF16)

    return call(
        density_parts_kernel,
        [shape((pairs, width))] * 4 + [shape(coef.shape), shape(pair_t.shape)],
        (where, coef, mate, pair_t, pair_mate),
        [SMEM, HBM, VMEM, HBM, VMEM],
        (16 * pairs * width * width, 1 * MIB),
        [pltpu.VMEM((4, pairs, width), F32), pltpu.SemaphoreType.DMA((2,))],
    )


def staged(where, cols, coupling, pair_alpha_t, beta_ops, tie):
    pairs, width = coupling.shape[0], beta_ops.shape[0]
    listed = beta_ops.shape[1] // width
    count = lax.axis_size(BETA)

    def staged_kernel(
        where_ref, cols_ref, c_ref, pa_ref, ops_ref, tie_ref, c_out, pa_out, w_out, pa_v, ops_v, sems
    ):
        rows = block_rows(where_ref, 0, width)
        copies = [
            pltpu.make_async_copy(ops_ref, ops_v, sems.at[0]),
            pltpu.make_async_copy(pa_ref.at[:, rows], pa_v, sems.at[1]),
            pltpu.make_async_copy(c_ref, c_out, sems.at[2]),
        ]
        for copy in copies:
            copy.start()
        copies[0].wait()
        core = where_ref[8]
        for n in range(5):
            offset = n if n in (0, 2, 4) else jnp.where(core == 0, n, 4 - n)
            tile = jnp.zeros((width, width), F32)
            for k in range(listed):
                here = lax.rem(cols_ref[k] - where_ref[9] + 2 + count, count)
                part = ops_v[:, k * width : (k + 1) * width].astype(F32)
                tile = jnp.where(here == offset, part, tile)
            w_out[:, n * width : (n + 1) * width] = tile.astype(BF16)
        copies[1].wait()
        pa_out[...] = pa_v[...].astype(F32).T
        copies[2].wait()

    return call(
        staged_kernel,
        [shape(coupling.shape), shape((width, pairs), F32), shape((width, 5 * width))],
        (where, cols, coupling, pair_alpha_t, beta_ops, tie),
        [SMEM, SMEM, HBM, HBM, HBM, ANY],
        (pairs * pairs, 2 * MIB),
        [
            pltpu.VMEM((pairs, width), BF16),
            pltpu.VMEM(beta_ops.shape, BF16),
            pltpu.SemaphoreType.DMA((3,)),
        ],
    )


def excited_block(near, far, coupling, scale):
    pairs, width = near.shape

    def excited_block_kernel(near_ref, far_ref, coupling_ref, scale_ref, out_ref):
        total = near_ref[...].astype(F32) + far_ref[...].astype(F32)
        density = total.T.astype(BF16)
        out_ref[...] = (dot(density, coupling_ref[...]) * scale_ref[...]).astype(BF16)

    return call(
        excited_block_kernel,
        [shape((width, pairs))],
        (near, far, coupling, scale),
        [VMEM] * 4,
        (2 * pairs * pairs * width, 2 * MIB),
    )[0]


def mixed_blocks(own, mate, pair_own, beside, beyond):
    width = own.shape[0]

    def mixed_blocks_kernel(own_ref, mate_ref, pair_ref, beside_ref, beyond_ref, *outs):
        rights = (pair_ref[...], beside_ref[...], beyond_ref[1], beyond_ref[0])
        for half, rows in enumerate((own_ref, mate_ref)):
            for out, right in zip(outs, rights):
                out[half] = dot(rows[...], right).astype(out.dtype)

    return call(
        mixed_blocks_kernel,
        [shape((2, width, width), F32)] + [shape((2, width, width))] * 3,
        (own, mate, pair_own, beside, beyond),
        [VMEM] * 5,
        (16 * own.size * width, 1 * MIB),
    )


def finished(where, same, parts, denominators):
    rows, width = same.shape

    def finished_kernel(where_ref, same_ref, m0, m1, m2, m3, den_ref, out, held, sems):
        copies = []
        for k, part in enumerate((m0, m1, m2, m3)):
            for half in (0, 1):
                n = 2 * k + half
                at = block_rows(where_ref, k + 4 * half, width)
                held[n] = (same_ref[at, :] + part[half].astype(F32)) / den_ref[at, :]
                copies.append(pltpu.make_async_copy(held.at[n], out.at[at, :], sems.at[n]))
                copies[-1].start()
        for copy in copies:
            copy.wait()

    return call(
        finished_kernel,
        [shape((rows, width), F32)],
        (where, same, *parts, denominators),
        [SMEM] + [VMEM] * 6,
        (rows * width * 2, 2 * MIB),
        [pltpu.VMEM((8, width, width), F32), pltpu.SemaphoreType.DMA((8,))],
        out_specs=[HBM],
    )[0]


def same_spin_beta(blocks, placed):
    rows, width = blocks[0].shape

    def same_spin_beta_kernel(b0, b1, b2, b3, b4, w_ref, out_ref):
        left = jnp.concatenate([b[...] for b in (b0, b1, b2, b3, b4)], axis=1)
        out_ref[...] = dot(left, w_ref[...], ((1,), (1,)))

    return call(
        same_spin_beta_kernel,
        [shape((rows, width), F32)],
        (*blocks, placed),
        [VMEM] * 6,
        (2 * rows * width * width * 5, 2 * MIB),
        limit=24,
    )[0]


def alpha_rows(ops_ref, picked, start_ref, out_ref, ops_v, sems, part, select):
    step = ops_v.shape[1]
    half = start_ref.shape[0] // 2
    mine = range(part * half, (part + 1) * half, step)
    rest = slice((1 - part) * half, (2 - part) * half)
    copies = [
        pltpu.make_async_copy(ops_ref.at[r : r + step, :], ops_v.at[n], sems.at[n])
        for n, r in enumerate(mine)
    ]
    for copy in copies:
        copy.start()
    select()
    out_ref[rest, :] = start_ref[rest, :]
    for n, r in enumerate(mine):
        copies[n].wait()
        at = slice(r, r + step)
        out_ref[at, :] = start_ref[at, :] + dot(ops_v[n], picked[...])


def same_spin_alpha(where, cols, blocks, alpha_ops, start):
    rows, width = start.shape
    depth = blocks[0].shape[0]
    span = alpha_ops.shape[1]
    count = lax.axis_size(ALPHA)

    def same_spin_alpha_kernel(
        where_ref, cols_ref, own_ref, near_ref, far_ref, ops_ref, start_ref, out_ref, picked, ops_v, sems
    ):
        def select():
            for k in range(span // depth):
                offset = lax.rem(cols_ref[4 + k] - where_ref[10] + 1 + count, count)
                picked[k * depth : (k + 1) * depth, :] = jnp.where(
                    offset == 1,
                    own_ref[...],
                    jnp.where(offset == where_ref[11], near_ref[...], far_ref[...]),
                )

        alpha_rows(ops_ref, picked, start_ref, out_ref, ops_v, sems, 0, select)

    return call(
        same_spin_alpha_kernel,
        [shape((rows, width), F32), shape((span, width))],
        (where, cols, *blocks, alpha_ops, start),
        [SMEM, SMEM] + [VMEM] * 3 + [HBM, VMEM],
        (rows * width * depth * 4, 5 * MIB),
        [pltpu.VMEM((4, rows // 8, span), BF16), pltpu.SemaphoreType.DMA((4,))],
    )


def rest_of_alpha(picked, alpha_ops, start):
    rows, width = start.shape
    span = alpha_ops.shape[1]

    def rest_of_alpha_kernel(picked, ops_ref, start_ref, out_ref, ops_v, sems):
        alpha_rows(ops_ref, picked, start_ref, out_ref, ops_v, sems, 1, lambda: None)

    return call(
        rest_of_alpha_kernel,
        [shape((rows, width), F32)],
        (picked, alpha_ops, start),
        [VMEM, HBM, VMEM],
        (rows * width * span, 5 * MIB),
        [pltpu.VMEM((4, rows // 8, span), BF16), pltpu.SemaphoreType.DMA((4,))],
    )[0]


def local(
    coef,
    beta_ops,
    beta_cols,
    alpha_ops,
    alpha_cols,
    pair_alpha,
    pair_beta,
    pair_coupling,
    denominators,
):
    y, core = lax.axis_index("y"), lax.axis_index("c")
    low = lax.axis_index("zl")
    side = 1 + 2 * core
    row_blocks = [(y ^ m) * 2 for m in (0, side, 2, 4 - side)]
    where = [r + core for r in row_blocks] + [r + 1 - core for r in row_blocks]
    where += [core, lax.axis_index(BETA), lax.axis_index(ALPHA), 2 - 2 * low]
    where = jnp.stack(where).astype(jnp.int32)
    cols = jnp.concatenate([beta_cols[0], alpha_cols[0]])

    pair_t = pair_beta.T
    mate = swapped(coef, "c", 1)
    pair_mate = swapped(pair_t, "c", 1)

    below = rotated(coef, BETA, 2)
    above = rotated(coef, BETA, -2)
    xs, route = lax.axis_size("x"), []
    for i in range(xs):
        route += [(2 * i, 2 * ((i + 1) % xs)), (2 * i + 1, 2 * ((i - 1) % xs) + 1)]

    *parts, coef_v, pair_v = density_parts(where, coef, mate, pair_t, pair_mate)
    coupling, scale, placed = staged(
        where, cols, pair_coupling, pair_alpha.T, beta_ops, parts[0]
    )
    turns = (None, crossing((1, 3)), crossing((2, 2)), crossing((3, 1)))
    got = [lax.ppermute(parts[k], ("y", "c"), turns[k]) for k in (1, 3, 2)]
    *got, below, above = lax.optimization_barrier((*got, below, above))
    near = swapped(coef, "zl", 1)
    total = parts[0].astype(F32)
    for part in got:
        total = total + part.astype(F32)
    total = total.astype(BF16)
    total, coupling, scale, placed = lax.optimization_barrier((total, coupling, scale, placed))

    far = lax.ppermute(near, ALPHA, route)
    first = lax.ppermute(total, ("zh", "c"), turns[1])
    sent, _ = lax.optimization_barrier((pair_v, total))
    beside = lax.ppermute(sent, ("y", "c"), turns[1])
    crossed = swapped(jnp.where(core == 0, above, below), "c", 1)
    first, beside = lax.optimization_barrier((first, beside))
    total = (total.astype(F32) + first.astype(F32)).astype(BF16)
    total, crossed = lax.optimization_barrier((total, crossed))
    beyond = lax.ppermute(jnp.stack([pair_v, beside]), ("y", "c"), turns[3])
    second = lax.ppermute(total, ("zh", "c"), turns[3])
    same = same_spin_beta([below, crossed, coef_v, mate, above], placed)
    around = [coef_v, near, far]
    same, picked = same_spin_alpha(where, cols, around, alpha_ops, same)
    second, same = lax.optimization_barrier((second, same))

    excited = excited_block(total, second, coupling, scale)
    mine, *out = mixed_blocks(excited, swapped(excited, "c", 1), pair_v, beside, beyond)
    back = [lax.ppermute(out[k - 1], ("y", "c"), turns[k]) for k in (1, 2, 3)]
    same = rest_of_alpha(picked, alpha_ops, same)
    *back, same = lax.optimization_barrier((*back, same))
    return finished(where, same, [mine, *back], denominators)


def solution(mesh):
    finer = Mesh(mesh.devices.reshape(4, 2, 4, 4, 2), (*ALPHA, *BETA))
    placed = (
        P(ALPHA, BETA),
        P(BETA, None),
        P(BETA, None),
        P(ALPHA, None),
        P(ALPHA, None),
        P(ALPHA, None),
        P(BETA, None),
        P(),
        P(ALPHA, BETA),
    )
    return jax.shard_map(
        local, mesh=finer, in_specs=placed, out_specs=P(ALPHA, BETA), check_vma=False
    )
```

```python
import jax
import jax.numpy as jnp
from jax import lax
from jax.experimental import pallas as pl
from jax.experimental.pallas import tpu as pltpu
from jax.sharding import Mesh
from jax.sharding import PartitionSpec as P

ALPHA = ("x", "zl")
BETA = ("y", "zh", "c")
F32 = jnp.float32
BF16 = jnp.bfloat16
SMEM = pl.BlockSpec(memory_space=pltpu.SMEM)
VMEM = pl.BlockSpec(memory_space=pltpu.VMEM)
HBM = pl.BlockSpec(memory_space=pltpu.HBM)
ANY = pl.BlockSpec(memory_space=pl.ANY)
MIB = 1 << 20


def dot(a, b, dims=((1,), (0,))):
    return lax.dot_general(a, b, (dims, ((), ())), preferred_element_type=F32)


def swapped(block, axis, mask):
    count = lax.axis_size(axis)
    return lax.ppermute(block, axis, [(i, i ^ mask) for i in range(count)])


def rotated(block, axis, distance):
    count = lax.axis_size(axis)
    return lax.ppermute(block, axis, [(i, (i + distance) % count) for i in range(count)])


def crossing(masks):
    return [(2 * i + h, 2 * (i ^ masks[h]) + h) for i in range(4) for h in (0, 1)]


def call(kernel, outs, args, specs, cost, scratch=(), aliases=None, out_specs=None, limit=16):
    args = [
        pltpu.with_memory_space_constraint(arg, pltpu.HBM) if spec is HBM else arg
        for arg, spec in zip(args, specs)
    ]
    return pl.pallas_call(
        kernel,
        out_shape=outs,
        in_specs=specs,
        out_specs=out_specs or [VMEM] * len(outs),
        scratch_shapes=list(scratch),
        input_output_aliases=aliases or {},
        compiler_params=pltpu.CompilerParams(vmem_limit_bytes=limit * MIB),
        cost_estimate=pl.CostEstimate(flops=cost[0], bytes_accessed=cost[1], transcendentals=0),
        name=kernel.__name__,
    )(*args)


def shape(dims, kind=BF16):
    return jax.ShapeDtypeStruct(dims, kind)


def block_rows(where_ref, k, width):
    return pl.ds(pl.multiple_of(where_ref[k] * width, width), width)


def loaded(coef, pair_t):
    def loaded_kernel(coef_ref, pair_ref, coef_out, pair_out, sems):
        copies = [
            pltpu.make_async_copy(coef_ref, coef_out, sems.at[0]),
            pltpu.make_async_copy(pair_ref, pair_out, sems.at[1]),
        ]
        for copy in copies:
            copy.start()
        for copy in copies:
            copy.wait()

    return call(
        loaded_kernel,
        [shape(coef.shape), shape(pair_t.shape)],
        (coef, pair_t),
        [HBM, HBM],
        (0, 1 * MIB),
        [pltpu.SemaphoreType.DMA((2,))],
    )


def density_parts(where, own, mate, pair_own, pair_mate):
    pairs, width = pair_mate.shape

    def density_parts_kernel(where_ref, own_ref, mate_ref, po_ref, pm_ref, kept, beside, across):
        left = jnp.concatenate([po_ref[...], pm_ref[...]], axis=1)
        for k, out in ((1, beside.at[0]), (5, beside.at[1]), (2, across), (0, kept)):
            rows = block_rows(where_ref, k, width)
            right = jnp.concatenate([own_ref[rows, :], mate_ref[rows, :]], axis=1)
            out[...] = dot(left, right, ((1,), (1,))).astype(BF16)

    one = shape((pairs, width))
    return call(
        density_parts_kernel,
        [one, shape((2, pairs, width)), one],
        (where, own, mate, pair_own, pair_mate),
        [SMEM] + [VMEM] * 4,
        (16 * pairs * width * width, 1 * MIB),
    )


def staged(where, cols, coupling, pair_alpha_t, beta_ops, tie):
    pairs, width = coupling.shape[0], beta_ops.shape[0]
    listed = beta_ops.shape[1] // width
    count = lax.axis_size(BETA)

    def staged_kernel(
        where_ref, cols_ref, c_ref, pa_ref, ops_ref, tie_ref, c_out, pa_out, w_out, pa_v, ops_v, sems
    ):
        rows = block_rows(where_ref, 0, width)
        copies = [
            pltpu.make_async_copy(ops_ref, ops_v, sems.at[0]),
            pltpu.make_async_copy(pa_ref.at[:, rows], pa_v, sems.at[1]),
            pltpu.make_async_copy(c_ref, c_out, sems.at[2]),
        ]
        for copy in copies:
            copy.start()
        copies[0].wait()
        core = where_ref[8]
        for n in range(5):
            offset = n if n in (0, 2, 4) else jnp.where(core == 0, n, 4 - n)
            tile = jnp.zeros((width, width), F32)
            for k in range(listed):
                here = lax.rem(cols_ref[k] - where_ref[9] + 2 + count, count)
                part = ops_v[:, k * width : (k + 1) * width].astype(F32)
                tile = jnp.where(here == offset, part, tile)
            w_out[:, n * width : (n + 1) * width] = tile.astype(BF16)
        copies[1].wait()
        pa_out[...] = pa_v[...].astype(F32).T
        copies[2].wait()

    return call(
        staged_kernel,
        [shape(coupling.shape), shape((width, pairs), F32), shape((width, 5 * width))],
        (where, cols, coupling, pair_alpha_t, beta_ops, tie),
        [SMEM, SMEM, HBM, HBM, HBM, ANY],
        (pairs * pairs, 2 * MIB),
        [
            pltpu.VMEM((pairs, width), BF16),
            pltpu.VMEM(beta_ops.shape, BF16),
            pltpu.SemaphoreType.DMA((3,)),
        ],
    )


def excited_block(near, far, coupling, scale):
    pairs, width = near.shape

    def excited_block_kernel(near_ref, far_ref, coupling_ref, scale_ref, out_ref):
        total = near_ref[...].astype(F32) + far_ref[...].astype(F32)
        density = total.T.astype(BF16)
        out_ref[...] = (dot(density, coupling_ref[...]) * scale_ref[...]).astype(BF16)

    return call(
        excited_block_kernel,
        [shape((width, pairs))],
        (near, far, coupling, scale),
        [VMEM] * 4,
        (2 * pairs * pairs * width, 2 * MIB),
    )[0]


def mixed_blocks(own, mate, pair_own, beside, beyond):
    width = own.shape[0]

    def mixed_blocks_kernel(own_ref, mate_ref, pair_ref, beside_ref, beyond_ref, *outs):
        rights = (pair_ref[...], beside_ref[...], beyond_ref[1], beyond_ref[0])
        for half, rows in enumerate((own_ref, mate_ref)):
            for out, right in zip(outs, rights):
                out[half] = dot(rows[...], right).astype(out.dtype)

    return call(
        mixed_blocks_kernel,
        [shape((2, width, width), F32)] + [shape((2, width, width))] * 3,
        (own, mate, pair_own, beside, beyond),
        [VMEM] * 5,
        (16 * own.size * width, 1 * MIB),
    )


def finished(where, same, parts, denominators):
    rows, width = same.shape

    def finished_kernel(where_ref, same_ref, m0, m1, m2, m3, den_ref, out, held, sems):
        copies = []
        for k, part in enumerate((m0, m1, m2, m3)):
            for half in (0, 1):
                n = 2 * k + half
                at = block_rows(where_ref, k + 4 * half, width)
                held[n] = (same_ref[at, :] + part[half].astype(F32)) / den_ref[at, :]
                copies.append(pltpu.make_async_copy(held.at[n], out.at[at, :], sems.at[n]))
                copies[-1].start()
        for copy in copies:
            copy.wait()

    return call(
        finished_kernel,
        [shape((rows, width), F32)],
        (where, same, *parts, denominators),
        [SMEM] + [VMEM] * 6,
        (rows * width * 2, 2 * MIB),
        [pltpu.VMEM((8, width, width), F32), pltpu.SemaphoreType.DMA((8,))],
        out_specs=[HBM],
    )[0]


def same_spin_beta(blocks, placed):
    rows, width = blocks[0].shape

    def same_spin_beta_kernel(b0, b1, b2, b3, b4, w_ref, out_ref):
        left = jnp.concatenate([b[...] for b in (b0, b1, b2, b3, b4)], axis=1)
        out_ref[...] = dot(left, w_ref[...], ((1,), (1,)))

    return call(
        same_spin_beta_kernel,
        [shape((rows, width), F32)],
        (*blocks, placed),
        [VMEM] * 6,
        (2 * rows * width * width * 5, 2 * MIB),
        limit=24,
    )[0]


def alpha_rows(ops_ref, picked, start_ref, out_ref, ops_v, sems, part, select):
    step = ops_v.shape[1]
    half = start_ref.shape[0] // 2
    mine = range(part * half, (part + 1) * half, step)
    rest = slice((1 - part) * half, (2 - part) * half)
    copies = [
        pltpu.make_async_copy(ops_ref.at[r : r + step, :], ops_v.at[n], sems.at[n])
        for n, r in enumerate(mine)
    ]
    for copy in copies:
        copy.start()
    select()
    out_ref[rest, :] = start_ref[rest, :]
    for n, r in enumerate(mine):
        copies[n].wait()
        at = slice(r, r + step)
        out_ref[at, :] = start_ref[at, :] + dot(ops_v[n], picked[...])


def same_spin_alpha(where, cols, blocks, alpha_ops, start):
    rows, width = start.shape
    depth = blocks[0].shape[0]
    span = alpha_ops.shape[1]
    count = lax.axis_size(ALPHA)

    def same_spin_alpha_kernel(
        where_ref, cols_ref, own_ref, near_ref, far_ref, ops_ref, start_ref, out_ref, picked, ops_v, sems
    ):
        def select():
            for k in range(span // depth):
                offset = lax.rem(cols_ref[4 + k] - where_ref[10] + 1 + count, count)
                picked[k * depth : (k + 1) * depth, :] = jnp.where(
                    offset == 1,
                    own_ref[...],
                    jnp.where(offset == where_ref[11], near_ref[...], far_ref[...]),
                )

        alpha_rows(ops_ref, picked, start_ref, out_ref, ops_v, sems, 0, select)

    return call(
        same_spin_alpha_kernel,
        [shape((rows, width), F32), shape((span, width))],
        (where, cols, *blocks, alpha_ops, start),
        [SMEM, SMEM] + [VMEM] * 3 + [HBM, VMEM],
        (rows * width * depth * 4, 5 * MIB),
        [pltpu.VMEM((4, rows // 8, span), BF16), pltpu.SemaphoreType.DMA((4,))],
    )


def rest_of_alpha(picked, alpha_ops, start):
    rows, width = start.shape
    span = alpha_ops.shape[1]

    def rest_of_alpha_kernel(picked, ops_ref, start_ref, out_ref, ops_v, sems):
        alpha_rows(ops_ref, picked, start_ref, out_ref, ops_v, sems, 1, lambda: None)

    return call(
        rest_of_alpha_kernel,
        [shape((rows, width), F32)],
        (picked, alpha_ops, start),
        [VMEM, HBM, VMEM],
        (rows * width * span, 5 * MIB),
        [pltpu.VMEM((4, rows // 8, span), BF16), pltpu.SemaphoreType.DMA((4,))],
    )[0]


def local(
    coef,
    beta_ops,
    beta_cols,
    alpha_ops,
    alpha_cols,
    pair_alpha,
    pair_beta,
    pair_coupling,
    denominators,
):
    y, core = lax.axis_index("y"), lax.axis_index("c")
    low = lax.axis_index("zl")
    side = 1 + 2 * core
    row_blocks = [(y ^ m) * 2 for m in (0, side, 2, 4 - side)]
    where = [r + core for r in row_blocks] + [r + 1 - core for r in row_blocks]
    where += [core, lax.axis_index(BETA), lax.axis_index(ALPHA), 2 - 2 * low]
    where = jnp.stack(where).astype(jnp.int32)
    cols = jnp.concatenate([beta_cols[0], alpha_cols[0]])

    pair_t = pair_beta.T
    mate = swapped(coef, "c", 1)
    pair_mate = swapped(pair_t, "c", 1)
    coef_v, pair_v = loaded(coef, pair_t)

    below = rotated(coef, BETA, 2)
    above = rotated(coef, BETA, -2)
    xs, route = lax.axis_size("x"), []
    for i in range(xs):
        route += [(2 * i, 2 * ((i + 1) % xs)), (2 * i + 1, 2 * ((i - 1) % xs) + 1)]

    kept, sent, across = density_parts(where, coef_v, mate, pair_v, pair_mate)
    coupling, scale, placed = staged(
        where, cols, pair_coupling, pair_alpha.T, beta_ops, kept
    )
    turns = (None, crossing((1, 3)), crossing((2, 2)), crossing((3, 1)))
    sent = lax.ppermute(sent, ("y", "c"), turns[1])
    across = lax.ppermute(across, ("y", "c"), turns[2])
    got = [sent[0], swapped(sent[1], "c", 1), across]
    *got, below, above = lax.optimization_barrier((*got, below, above))
    near = swapped(coef, "zl", 1)
    total = kept.astype(F32)
    for part in got:
        total = total + part.astype(F32)
    total = total.astype(BF16)
    total, coupling, scale, placed = lax.optimization_barrier((total, coupling, scale, placed))

    far = lax.ppermute(near, ALPHA, route)
    first = lax.ppermute(total, ("zh", "c"), turns[1])
    sent, _ = lax.optimization_barrier((pair_v, total))
    beside = lax.ppermute(sent, ("y", "c"), turns[1])
    crossed = swapped(jnp.where(core == 0, above, below), "c", 1)
    first, beside = lax.optimization_barrier((first, beside))
    total = (total.astype(F32) + first.astype(F32)).astype(BF16)
    total, crossed = lax.optimization_barrier((total, crossed))
    beyond = lax.ppermute(jnp.stack([pair_v, beside]), ("y", "c"), turns[3])
    second = lax.ppermute(total, ("zh", "c"), turns[3])
    same = same_spin_beta([below, crossed, coef_v, mate, above], placed)
    around = [coef_v, near, far]
    same, picked = same_spin_alpha(where, cols, around, alpha_ops, same)
    second, same = lax.optimization_barrier((second, same))

    excited = excited_block(total, second, coupling, scale)
    mine, *out = mixed_blocks(excited, swapped(excited, "c", 1), pair_v, beside, beyond)
    back = [lax.ppermute(out[k - 1], ("y", "c"), turns[k]) for k in (1, 2, 3)]
    same = rest_of_alpha(picked, alpha_ops, same)
    *back, same = lax.optimization_barrier((*back, same))
    return finished(where, same, [mine, *back], denominators)


def solution(mesh):
    finer = Mesh(mesh.devices.reshape(4, 2, 4, 4, 2), (*ALPHA, *BETA))
    placed = (
        P(ALPHA, BETA),
        P(BETA, None),
        P(BETA, None),
        P(ALPHA, None),
        P(ALPHA, None),
        P(ALPHA, None),
        P(BETA, None),
        P(),
        P(ALPHA, BETA),
    )
    return jax.shard_map(
        local, mesh=finer, in_specs=placed, out_specs=P(ALPHA, BETA), check_vma=False
    )
```

```python
import jax
import jax.numpy as jnp
from jax import lax
from jax.experimental import pallas as pl
from jax.experimental.pallas import tpu as pltpu
from jax.sharding import Mesh
from jax.sharding import PartitionSpec as P

ALPHA = ("x", "zl")
BETA = ("y", "zh", "c")
F32 = jnp.float32
BF16 = jnp.bfloat16
SMEM = pl.BlockSpec(memory_space=pltpu.SMEM)
VMEM = pl.BlockSpec(memory_space=pltpu.VMEM)
HBM = pl.BlockSpec(memory_space=pltpu.HBM)
ANY = pl.BlockSpec(memory_space=pl.ANY)
MIB = 1 << 20


def dot(a, b, dims=((1,), (0,))):
    return lax.dot_general(a, b, (dims, ((), ())), preferred_element_type=F32)


def swapped(block, axis, mask):
    count = lax.axis_size(axis)
    return lax.ppermute(block, axis, [(i, i ^ mask) for i in range(count)])


def rotated(block, axis, distance):
    count = lax.axis_size(axis)
    return lax.ppermute(block, axis, [(i, (i + distance) % count) for i in range(count)])


def crossing(masks):
    return [(2 * i + h, 2 * (i ^ masks[h]) + h) for i in range(4) for h in (0, 1)]


def call(kernel, outs, args, specs, cost, scratch=(), aliases=None, out_specs=None, limit=16):
    args = [
        pltpu.with_memory_space_constraint(arg, pltpu.HBM) if spec is HBM else arg
        for arg, spec in zip(args, specs)
    ]
    return pl.pallas_call(
        kernel,
        out_shape=outs,
        in_specs=specs,
        out_specs=out_specs or [VMEM] * len(outs),
        scratch_shapes=list(scratch),
        input_output_aliases=aliases or {},
        compiler_params=pltpu.CompilerParams(vmem_limit_bytes=limit * MIB),
        cost_estimate=pl.CostEstimate(flops=cost[0], bytes_accessed=cost[1], transcendentals=0),
        name=kernel.__name__,
    )(*args)


def shape(dims, kind=BF16):
    return jax.ShapeDtypeStruct(dims, kind)


def block_rows(where_ref, k, width):
    return pl.ds(pl.multiple_of(where_ref[k] * width, width), width)


def loaded(coef, pair_t):
    def loaded_kernel(coef_ref, pair_ref, coef_out, pair_out, sems):
        copies = [
            pltpu.make_async_copy(coef_ref, coef_out, sems.at[0]),
            pltpu.make_async_copy(pair_ref, pair_out, sems.at[1]),
        ]
        for copy in copies:
            copy.start()
        for copy in copies:
            copy.wait()

    return call(
        loaded_kernel,
        [shape(coef.shape), shape(pair_t.shape)],
        (coef, pair_t),
        [HBM, HBM],
        (0, 1 * MIB),
        [pltpu.SemaphoreType.DMA((2,))],
    )


def density_parts(where, own, mate, pair_own, pair_mate):
    pairs, width = pair_mate.shape

    def density_parts_kernel(where_ref, own_ref, mate_ref, po_ref, pm_ref, *outs):
        left = jnp.concatenate([po_ref[...], pm_ref[...]], axis=1)
        for k, out in enumerate(outs):
            rows = block_rows(where_ref, k, width)
            right = jnp.concatenate([own_ref[rows, :], mate_ref[rows, :]], axis=1)
            out[...] = dot(left, right, ((1,), (1,))).astype(BF16)

    return call(
        density_parts_kernel,
        [shape((pairs, width))] * 4,
        (where, own, mate, pair_own, pair_mate),
        [SMEM] + [VMEM] * 4,
        (16 * pairs * width * width, 1 * MIB),
    )


def staged(where, cols, coupling, pair_alpha_t, beta_ops, tie):
    pairs, width = coupling.shape[0], beta_ops.shape[0]
    listed = beta_ops.shape[1] // width
    count = lax.axis_size(BETA)

    def staged_kernel(
        where_ref, cols_ref, c_ref, pa_ref, ops_ref, tie_ref, c_out, pa_out, w_out, pa_v, ops_v, sems
    ):
        rows = block_rows(where_ref, 0, width)
        copies = [
            pltpu.make_async_copy(ops_ref, ops_v, sems.at[0]),
            pltpu.make_async_copy(pa_ref.at[:, rows], pa_v, sems.at[1]),
            pltpu.make_async_copy(c_ref, c_out, sems.at[2]),
        ]
        for copy in copies:
            copy.start()
        copies[0].wait()
        core = where_ref[8]
        for n in range(5):
            offset = n if n in (0, 2, 4) else jnp.where(core == 0, n, 4 - n)
            tile = jnp.zeros((width, width), F32)
            for k in range(listed):
                here = lax.rem(cols_ref[k] - where_ref[9] + 2 + count, count)
                part = ops_v[:, k * width : (k + 1) * width].astype(F32)
                tile = jnp.where(here == offset, part, tile)
            w_out[:, n * width : (n + 1) * width] = tile.astype(BF16)
        copies[1].wait()
        pa_out[...] = pa_v[...].astype(F32).T
        copies[2].wait()

    return call(
        staged_kernel,
        [shape(coupling.shape), shape((width, pairs), F32), shape((width, 5 * width))],
        (where, cols, coupling, pair_alpha_t, beta_ops, tie),
        [SMEM, SMEM, HBM, HBM, HBM, ANY],
        (pairs * pairs, 2 * MIB),
        [
            pltpu.VMEM((pairs, width), BF16),
            pltpu.VMEM(beta_ops.shape, BF16),
            pltpu.SemaphoreType.DMA((3,)),
        ],
    )


def excited_block(near, far, coupling, scale):
    pairs, width = near.shape

    def excited_block_kernel(near_ref, far_ref, coupling_ref, scale_ref, out_ref):
        total = near_ref[...].astype(F32) + far_ref[...].astype(F32)
        density = total.T.astype(BF16)
        out_ref[...] = (dot(density, coupling_ref[...]) * scale_ref[...]).astype(BF16)

    return call(
        excited_block_kernel,
        [shape((width, pairs))],
        (near, far, coupling, scale),
        [VMEM] * 4,
        (2 * pairs * pairs * width, 2 * MIB),
    )[0]


def mixed_blocks(own, mate, pair_own, beside, beyond):
    width = own.shape[0]

    def mixed_blocks_kernel(own_ref, mate_ref, pair_ref, beside_ref, beyond_ref, *outs):
        rights = (pair_ref[...], beside_ref[...], beyond_ref[1], beyond_ref[0])
        for half, rows in enumerate((own_ref, mate_ref)):
            for out, right in zip(outs, rights):
                out[half] = dot(rows[...], right).astype(out.dtype)

    return call(
        mixed_blocks_kernel,
        [shape((2, width, width), F32)] + [shape((2, width, width))] * 3,
        (own, mate, pair_own, beside, beyond),
        [VMEM] * 5,
        (16 * own.size * width, 1 * MIB),
    )


def finished(where, same, parts, denominators):
    rows, width = same.shape

    def finished_kernel(where_ref, same_ref, m0, m1, m2, m3, den_ref, out, held, sems):
        copies = []
        for k, part in enumerate((m0, m1, m2, m3)):
            for half in (0, 1):
                n = 2 * k + half
                at = block_rows(where_ref, k + 4 * half, width)
                held[n] = (same_ref[at, :] + part[half].astype(F32)) / den_ref[at, :]
                copies.append(pltpu.make_async_copy(held.at[n], out.at[at, :], sems.at[n]))
                copies[-1].start()
        for copy in copies:
            copy.wait()

    return call(
        finished_kernel,
        [shape((rows, width), F32)],
        (where, same, *parts, denominators),
        [SMEM] + [VMEM] * 6,
        (rows * width * 2, 2 * MIB),
        [pltpu.VMEM((8, width, width), F32), pltpu.SemaphoreType.DMA((8,))],
        out_specs=[HBM],
    )[0]


def same_spin_beta(blocks, placed):
    rows, width = blocks[0].shape

    def same_spin_beta_kernel(b0, b1, b2, b3, b4, w_ref, out_ref):
        left = jnp.concatenate([b[...] for b in (b0, b1, b2, b3, b4)], axis=1)
        out_ref[...] = dot(left, w_ref[...], ((1,), (1,)))

    return call(
        same_spin_beta_kernel,
        [shape((rows, width), F32)],
        (*blocks, placed),
        [VMEM] * 6,
        (2 * rows * width * width * 5, 2 * MIB),
        limit=24,
    )[0]


def alpha_rows(ops_ref, picked, start_ref, out_ref, ops_v, sems, first, select):
    step = ops_v.shape[1]
    last = first + ops_v.shape[0] * step
    mine = range(first, last, step)
    rest = slice(last, None) if first == 0 else slice(0, first)
    copies = [
        pltpu.make_async_copy(ops_ref.at[r : r + step, :], ops_v.at[n], sems.at[n])
        for n, r in enumerate(mine)
    ]
    for copy in copies:
        copy.start()
    select()
    out_ref[rest, :] = start_ref[rest, :]
    for n, r in enumerate(mine):
        copies[n].wait()
        at = slice(r, r + step)
        out_ref[at, :] = start_ref[at, :] + dot(ops_v[n], picked[...])


def same_spin_alpha(where, cols, blocks, alpha_ops, start):
    rows, width = start.shape
    depth = blocks[0].shape[0]
    span = alpha_ops.shape[1]
    count = lax.axis_size(ALPHA)

    def same_spin_alpha_kernel(
        where_ref, cols_ref, own_ref, near_ref, far_ref, ops_ref, start_ref, out_ref, picked, ops_v, sems
    ):
        def select():
            for k in range(span // depth):
                offset = lax.rem(cols_ref[4 + k] - where_ref[10] + 1 + count, count)
                picked[k * depth : (k + 1) * depth, :] = jnp.where(
                    offset == 1,
                    own_ref[...],
                    jnp.where(offset == where_ref[11], near_ref[...], far_ref[...]),
                )

        alpha_rows(ops_ref, picked, start_ref, out_ref, ops_v, sems, 0, select)

    return call(
        same_spin_alpha_kernel,
        [shape((rows, width), F32), shape((span, width))],
        (where, cols, *blocks, alpha_ops, start),
        [SMEM, SMEM] + [VMEM] * 3 + [HBM, VMEM],
        (rows * width * depth * 4, 5 * MIB),
        [pltpu.VMEM((3, rows // 8, span), BF16), pltpu.SemaphoreType.DMA((3,))],
    )


def rest_of_alpha(picked, alpha_ops, start):
    rows, width = start.shape
    span = alpha_ops.shape[1]

    def rest_of_alpha_kernel(picked, ops_ref, start_ref, out_ref, ops_v, sems):
        alpha_rows(ops_ref, picked, start_ref, out_ref, ops_v, sems, rows - 5 * (rows // 8), lambda: None)

    return call(
        rest_of_alpha_kernel,
        [shape((rows, width), F32)],
        (picked, alpha_ops, start),
        [VMEM, HBM, VMEM],
        (rows * width * span, 5 * MIB),
        [pltpu.VMEM((5, rows // 8, span), BF16), pltpu.SemaphoreType.DMA((5,))],
    )[0]


def local(
    coef,
    beta_ops,
    beta_cols,
    alpha_ops,
    alpha_cols,
    pair_alpha,
    pair_beta,
    pair_coupling,
    denominators,
):
    y, core = lax.axis_index("y"), lax.axis_index("c")
    low = lax.axis_index("zl")
    side = 1 + 2 * core
    row_blocks = [(y ^ m) * 2 for m in (0, side, 2, 4 - side)]
    where = [r + core for r in row_blocks] + [r + 1 - core for r in row_blocks]
    where += [core, lax.axis_index(BETA), lax.axis_index(ALPHA), 2 - 2 * low]
    where = jnp.stack(where).astype(jnp.int32)
    cols = jnp.concatenate([beta_cols[0], alpha_cols[0]])

    pair_t = pair_beta.T
    mate = swapped(coef, "c", 1)
    pair_mate = swapped(pair_t, "c", 1)
    coef_v, pair_v = loaded(coef, pair_t)

    below = rotated(coef, BETA, 2)
    above = rotated(coef, BETA, -2)
    xs, route = lax.axis_size("x"), []
    for i in range(xs):
        route += [(2 * i, 2 * ((i + 1) % xs)), (2 * i + 1, 2 * ((i - 1) % xs) + 1)]

    parts = density_parts(where, coef_v, mate, pair_v, pair_mate)
    coupling, scale, placed = staged(
        where, cols, pair_coupling, pair_alpha.T, beta_ops, parts[0]
    )
    turns = (None, crossing((1, 3)), crossing((2, 2)), crossing((3, 1)))
    got = [lax.ppermute(parts[k], ("y", "c"), turns[k]) for k in (1, 3, 2)]
    *got, below, above = lax.optimization_barrier((*got, below, above))
    near = swapped(coef, "zl", 1)
    total = parts[0].astype(F32)
    for part in got:
        total = total + part.astype(F32)
    total = total.astype(BF16)
    total, coupling, scale, placed = lax.optimization_barrier((total, coupling, scale, placed))

    far = lax.ppermute(near, ALPHA, route)
    first = lax.ppermute(total, ("zh", "c"), turns[1])
    sent, _ = lax.optimization_barrier((pair_v, total))
    beside = lax.ppermute(sent, ("y", "c"), turns[1])
    crossed = swapped(jnp.where(core == 0, above, below), "c", 1)
    first, beside = lax.optimization_barrier((first, beside))
    total = (total.astype(F32) + first.astype(F32)).astype(BF16)
    total, crossed = lax.optimization_barrier((total, crossed))
    beyond = lax.ppermute(jnp.stack([pair_v, beside]), ("y", "c"), turns[3])
    second = lax.ppermute(total, ("zh", "c"), turns[3])
    same = same_spin_beta([below, crossed, coef_v, mate, above], placed)
    around = [coef_v, near, far]
    same, picked = same_spin_alpha(where, cols, around, alpha_ops, same)
    second, same = lax.optimization_barrier((second, same))

    excited = excited_block(total, second, coupling, scale)
    mine, *out = mixed_blocks(excited, swapped(excited, "c", 1), pair_v, beside, beyond)
    back = [lax.ppermute(out[k - 1], ("y", "c"), turns[k]) for k in (1, 2, 3)]
    same = rest_of_alpha(picked, alpha_ops, same)
    *back, same = lax.optimization_barrier((*back, same))
    return finished(where, same, [mine, *back], denominators)


def solution(mesh):
    finer = Mesh(mesh.devices.reshape(4, 2, 4, 4, 2), (*ALPHA, *BETA))
    placed = (
        P(ALPHA, BETA),
        P(BETA, None),
        P(BETA, None),
        P(ALPHA, None),
        P(ALPHA, None),
        P(ALPHA, None),
        P(BETA, None),
        P(),
        P(ALPHA, BETA),
    )
    return jax.shard_map(
        local, mesh=finer, in_specs=placed, out_specs=P(ALPHA, BETA), check_vma=False
    )
```

```python
import jax
import jax.numpy as jnp
from jax import lax
from jax.experimental import pallas as pl
from jax.experimental.pallas import tpu as pltpu
from jax.sharding import Mesh
from jax.sharding import PartitionSpec as P

ALPHA = ("x", "zl")
BETA = ("y", "zh", "c")
F32 = jnp.float32
BF16 = jnp.bfloat16
SMEM = pl.BlockSpec(memory_space=pltpu.SMEM)
VMEM = pl.BlockSpec(memory_space=pltpu.VMEM)
HBM = pl.BlockSpec(memory_space=pltpu.HBM)
ANY = pl.BlockSpec(memory_space=pl.ANY)
MIB = 1 << 20


def dot(a, b, dims=((1,), (0,))):
    return lax.dot_general(a, b, (dims, ((), ())), preferred_element_type=F32)


def swapped(block, axis, mask):
    count = lax.axis_size(axis)
    return lax.ppermute(block, axis, [(i, i ^ mask) for i in range(count)])


def rotated(block, axis, distance):
    count = lax.axis_size(axis)
    return lax.ppermute(block, axis, [(i, (i + distance) % count) for i in range(count)])


def crossing(masks):
    return [(2 * i + h, 2 * (i ^ masks[h]) + h) for i in range(4) for h in (0, 1)]


def call(kernel, outs, args, specs, cost, scratch=(), aliases=None, out_specs=None, limit=16):
    args = [
        pltpu.with_memory_space_constraint(arg, pltpu.HBM) if spec is HBM else arg
        for arg, spec in zip(args, specs)
    ]
    return pl.pallas_call(
        kernel,
        out_shape=outs,
        in_specs=specs,
        out_specs=out_specs or [VMEM] * len(outs),
        scratch_shapes=list(scratch),
        input_output_aliases=aliases or {},
        compiler_params=pltpu.CompilerParams(vmem_limit_bytes=limit * MIB),
        cost_estimate=pl.CostEstimate(flops=cost[0], bytes_accessed=cost[1], transcendentals=0),
        name=kernel.__name__,
    )(*args)


def shape(dims, kind=BF16):
    return jax.ShapeDtypeStruct(dims, kind)


def block_rows(where_ref, k, width):
    return pl.ds(pl.multiple_of(where_ref[k] * width, width), width)


def density_parts(where, coef, mate, pair_t, pair_mate):
    pairs, width = pair_mate.shape

    def density_parts_kernel(
        where_ref, coef_ref, mate_ref, pair_ref, pm_ref, o0, o1, o2, o3, coef_out, pair_out, acc, sems
    ):
        copies = [
            pltpu.make_async_copy(coef_ref, coef_out, sems.at[0]),
            pltpu.make_async_copy(pair_ref, pair_out, sems.at[1]),
        ]
        for copy in copies:
            copy.start()
        left = pm_ref[...]
        for k in range(4):
            rows = block_rows(where_ref, k, width)
            acc[k] = dot(left, mate_ref[rows, :], ((1,), (1,)))
        for copy in copies:
            copy.wait()
        left = pair_out[...]
        for k, out in enumerate((o0, o1, o2, o3)):
            rows = block_rows(where_ref, k, width)
            out[...] = (acc[k] + dot(left, coef_out[rows, :], ((1,), (1,)))).astype(BF16)

    return call(
        density_parts_kernel,
        [shape((pairs, width))] * 4 + [shape(coef.shape), shape(pair_t.shape)],
        (where, coef, mate, pair_t, pair_mate),
        [SMEM, HBM, VMEM, HBM, VMEM],
        (16 * pairs * width * width, 1 * MIB),
        [pltpu.VMEM((4, pairs, width), F32), pltpu.SemaphoreType.DMA((2,))],
    )


def staged(where, cols, coupling, pair_alpha_t, beta_ops, tie):
    pairs, width = coupling.shape[0], beta_ops.shape[0]
    listed = beta_ops.shape[1] // width
    count = lax.axis_size(BETA)

    def staged_kernel(
        where_ref, cols_ref, c_ref, pa_ref, ops_ref, tie_ref, c_out, pa_out, w_out, pa_v, ops_v, sems
    ):
        rows = block_rows(where_ref, 0, width)
        copies = [
            pltpu.make_async_copy(ops_ref, ops_v, sems.at[0]),
            pltpu.make_async_copy(pa_ref.at[:, rows], pa_v, sems.at[1]),
            pltpu.make_async_copy(c_ref, c_out, sems.at[2]),
        ]
        for copy in copies:
            copy.start()
        copies[0].wait()
        core = where_ref[8]
        for n in range(5):
            offset = n if n in (0, 2, 4) else jnp.where(core == 0, n, 4 - n)
            tile = jnp.zeros((width, width), F32)
            for k in range(listed):
                here = lax.rem(cols_ref[k] - where_ref[9] + 2 + count, count)
                part = ops_v[:, k * width : (k + 1) * width].astype(F32)
                tile = jnp.where(here == offset, part, tile)
            w_out[:, n * width : (n + 1) * width] = tile.astype(BF16)
        copies[1].wait()
        pa_out[...] = pa_v[...].astype(F32).T
        copies[2].wait()

    return call(
        staged_kernel,
        [shape(coupling.shape), shape((width, pairs), F32), shape((width, 5 * width))],
        (where, cols, coupling, pair_alpha_t, beta_ops, tie),
        [SMEM, SMEM, HBM, HBM, HBM, ANY],
        (pairs * pairs, 2 * MIB),
        [
            pltpu.VMEM((pairs, width), BF16),
            pltpu.VMEM(beta_ops.shape, BF16),
            pltpu.SemaphoreType.DMA((3,)),
        ],
    )


def excited_block(near, far, coupling, scale):
    pairs, width = near.shape

    def excited_block_kernel(near_ref, far_ref, coupling_ref, scale_ref, out_ref):
        total = near_ref[...].astype(F32) + far_ref[...].astype(F32)
        density = total.T.astype(BF16)
        out_ref[...] = (dot(density, coupling_ref[...]) * scale_ref[...]).astype(BF16)

    return call(
        excited_block_kernel,
        [shape((width, pairs))],
        (near, far, coupling, scale),
        [VMEM] * 4,
        (2 * pairs * pairs * width, 2 * MIB),
    )[0]


def mixed_blocks(own, mate, pair_own, beside, beyond):
    width = own.shape[0]

    def mixed_blocks_kernel(own_ref, mate_ref, pair_ref, beside_ref, beyond_ref, *outs):
        rights = (pair_ref[...], beside_ref[...], beyond_ref[1], beyond_ref[0])
        for half, rows in enumerate((own_ref, mate_ref)):
            for out, right in zip(outs, rights):
                out[half] = dot(rows[...], right).astype(out.dtype)

    return call(
        mixed_blocks_kernel,
        [shape((2, width, width), F32)] + [shape((2, width, width))] * 3,
        (own, mate, pair_own, beside, beyond),
        [VMEM] * 5,
        (16 * own.size * width, 1 * MIB),
    )


def finished(where, same, parts, denominators):
    rows, width = same.shape

    def finished_kernel(where_ref, same_ref, m0, m1, m2, m3, den_ref, out, held, sems):
        copies = []
        for k, part in enumerate((m0, m1, m2, m3)):
            for half in (0, 1):
                n = 2 * k + half
                at = block_rows(where_ref, k + 4 * half, width)
                held[n] = (same_ref[at, :] + part[half].astype(F32)) / den_ref[at, :]
                copies.append(pltpu.make_async_copy(held.at[n], out.at[at, :], sems.at[n]))
                copies[-1].start()
        for copy in copies:
            copy.wait()

    return call(
        finished_kernel,
        [shape((rows, width), F32)],
        (where, same, *parts, denominators),
        [SMEM] + [VMEM] * 6,
        (rows * width * 2, 2 * MIB),
        [pltpu.VMEM((8, width, width), F32), pltpu.SemaphoreType.DMA((8,))],
        out_specs=[HBM],
    )[0]


def same_spin_beta(blocks, placed):
    rows, width = blocks[0].shape

    def same_spin_beta_kernel(b0, b1, b2, b3, b4, w_ref, out_ref):
        left = jnp.concatenate([b[...] for b in (b0, b1, b2, b3, b4)], axis=1)
        out_ref[...] = dot(left, w_ref[...], ((1,), (1,)))

    return call(
        same_spin_beta_kernel,
        [shape((rows, width), F32)],
        (*blocks, placed),
        [VMEM] * 6,
        (2 * rows * width * width * 5, 2 * MIB),
        limit=24,
    )[0]


def alpha_rows(ops_ref, picked, start_ref, out_ref, ops_v, sems, first, select):
    step = ops_v.shape[1]
    last = first + ops_v.shape[0] * step
    mine = range(first, last, step)
    rest = slice(last, None) if first == 0 else slice(0, first)
    copies = [
        pltpu.make_async_copy(ops_ref.at[r : r + step, :], ops_v.at[n], sems.at[n])
        for n, r in enumerate(mine)
    ]
    for copy in copies:
        copy.start()
    select()
    out_ref[rest, :] = start_ref[rest, :]
    for n, r in enumerate(mine):
        copies[n].wait()
        at = slice(r, r + step)
        out_ref[at, :] = start_ref[at, :] + dot(ops_v[n], picked[...])


def same_spin_alpha(where, cols, blocks, alpha_ops, start):
    rows, width = start.shape
    depth = blocks[0].shape[0]
    span = alpha_ops.shape[1]
    count = lax.axis_size(ALPHA)

    def same_spin_alpha_kernel(
        where_ref, cols_ref, own_ref, near_ref, far_ref, ops_ref, start_ref, out_ref, picked, ops_v, sems
    ):
        def select():
            for k in range(span // depth):
                offset = lax.rem(cols_ref[4 + k] - where_ref[10] + 1 + count, count)
                picked[k * depth : (k + 1) * depth, :] = jnp.where(
                    offset == 1,
                    own_ref[...],
                    jnp.where(offset == where_ref[11], near_ref[...], far_ref[...]),
                )

        alpha_rows(ops_ref, picked, start_ref, out_ref, ops_v, sems, 0, select)

    return call(
        same_spin_alpha_kernel,
        [shape((rows, width), F32), shape((span, width))],
        (where, cols, *blocks, alpha_ops, start),
        [SMEM, SMEM] + [VMEM] * 3 + [HBM, VMEM],
        (rows * width * depth * 4, 5 * MIB),
        [pltpu.VMEM((3, rows // 8, span), BF16), pltpu.SemaphoreType.DMA((3,))],
    )


def rest_of_alpha(picked, alpha_ops, start):
    rows, width = start.shape
    span = alpha_ops.shape[1]

    def rest_of_alpha_kernel(picked, ops_ref, start_ref, out_ref, ops_v, sems):
        alpha_rows(ops_ref, picked, start_ref, out_ref, ops_v, sems, rows - 5 * (rows // 8), lambda: None)

    return call(
        rest_of_alpha_kernel,
        [shape((rows, width), F32)],
        (picked, alpha_ops, start),
        [VMEM, HBM, VMEM],
        (rows * width * span, 5 * MIB),
        [pltpu.VMEM((5, rows // 8, span), BF16), pltpu.SemaphoreType.DMA((5,))],
    )[0]


def local(
    coef,
    beta_ops,
    beta_cols,
    alpha_ops,
    alpha_cols,
    pair_alpha,
    pair_beta,
    pair_coupling,
    denominators,
):
    y, core = lax.axis_index("y"), lax.axis_index("c")
    low = lax.axis_index("zl")
    side = 1 + 2 * core
    row_blocks = [(y ^ m) * 2 for m in (0, side, 2, 4 - side)]
    where = [r + core for r in row_blocks] + [r + 1 - core for r in row_blocks]
    where += [core, lax.axis_index(BETA), lax.axis_index(ALPHA), 2 - 2 * low]
    where = jnp.stack(where).astype(jnp.int32)
    cols = jnp.concatenate([beta_cols[0], alpha_cols[0]])

    pair_t = pair_beta.T
    mate = swapped(coef, "c", 1)
    pair_mate = swapped(pair_t, "c", 1)

    below = rotated(coef, BETA, 2)
    above = rotated(coef, BETA, -2)
    xs, route = lax.axis_size("x"), []
    for i in range(xs):
        route += [(2 * i, 2 * ((i + 1) % xs)), (2 * i + 1, 2 * ((i - 1) % xs) + 1)]

    *parts, coef_v, pair_v = density_parts(where, coef, mate, pair_t, pair_mate)
    coupling, scale, placed = staged(
        where, cols, pair_coupling, pair_alpha.T, beta_ops, parts[0]
    )
    turns = (None, crossing((1, 3)), crossing((2, 2)), crossing((3, 1)))
    got = [lax.ppermute(parts[k], ("y", "c"), turns[k]) for k in (1, 3, 2)]
    *got, below, above = lax.optimization_barrier((*got, below, above))
    near = swapped(coef, "zl", 1)
    total = parts[0].astype(F32)
    for part in got:
        total = total + part.astype(F32)
    total = total.astype(BF16)
    total, coupling, scale, placed = lax.optimization_barrier((total, coupling, scale, placed))

    far = lax.ppermute(near, ALPHA, route)
    first = lax.ppermute(total, ("zh", "c"), turns[1])
    sent, _ = lax.optimization_barrier((pair_v, total))
    beside = lax.ppermute(sent, ("y", "c"), turns[1])
    crossed = swapped(jnp.where(core == 0, above, below), "c", 1)
    first, beside = lax.optimization_barrier((first, beside))
    total = (total.astype(F32) + first.astype(F32)).astype(BF16)
    total, crossed = lax.optimization_barrier((total, crossed))
    beyond = lax.ppermute(jnp.stack([pair_v, beside]), ("y", "c"), turns[3])
    second = lax.ppermute(total, ("zh", "c"), turns[3])
    same = same_spin_beta([below, crossed, coef_v, mate, above], placed)
    around = [coef_v, near, far]
    same, picked = same_spin_alpha(where, cols, around, alpha_ops, same)
    second, same = lax.optimization_barrier((second, same))

    excited = excited_block(total, second, coupling, scale)
    mine, *out = mixed_blocks(excited, swapped(excited, "c", 1), pair_v, beside, beyond)
    back = [lax.ppermute(out[k - 1], ("y", "c"), turns[k]) for k in (1, 2, 3)]
    same = rest_of_alpha(picked, alpha_ops, same)
    *back, same = lax.optimization_barrier((*back, same))
    return finished(where, same, [mine, *back], denominators)


def solution(mesh):
    finer = Mesh(mesh.devices.reshape(4, 2, 4, 4, 2), (*ALPHA, *BETA))
    placed = (
        P(ALPHA, BETA),
        P(BETA, None),
        P(BETA, None),
        P(ALPHA, None),
        P(ALPHA, None),
        P(ALPHA, None),
        P(BETA, None),
        P(),
        P(ALPHA, BETA),
    )
    return jax.shard_map(
        local, mesh=finer, in_specs=placed, out_specs=P(ALPHA, BETA), check_vma=False
    )
```
